32 devices in a mesh: grp: 2 (over y), pos: 16 (over z, x, core).
Axes of the slice: x: 2, y: 2, z: 4, core: 2. Of those that a mesh axis runs over, the one named last changes fastest.
Arguments:
- object_field: float32 [2, 2048, 2048], P(None, 'grp', 'pos'), may hold values from -5 to 5
- probe_field: float32 [2, 256, 256], replicated, may hold values from -5 to 5
- patterns: float32 [96, 256, 256], P(('grp', 'pos')), may hold values from 0.05 to 5
- corners: int32 [2, 96], P(None, ('grp', 'pos')), may hold values from 0 to 1792, as said below
- counts: int32 [32], replicated, may hold values from 1 to 3, as said below
Outputs:
- object_new: float32 [2, 2048, 2048], P(None, 'grp', 'pos')
- probe_new: float32 [2, 256, 256], replicated
The draws below stay inside these ranges and needn't reach their ends.
Inputs may be any that keep to these rules, and one draw needn't show every extreme that they name: `corners`: each slot's patch of 256 x 256 cells lies inside the object and inside its device's block of 1024 x 128 object cells extended by 128 cells on every side (the device at grp index a and pos index b holds rows a * 1024 to a * 1024 + 1023 and columns b * 128 to b * 128 + 127). The live slots of a device are its first counts[d] slots; some device has all 3 slots live.
All inputs are finite; a program needn't handle non-finite values.
Results may differ from the reference program's by a relative error of at most 0.00012.
Values sent between devices are 32-bit elements; how exact they have to be, the bound alone decides.
A program may use at most 64 MiB of HBM per device.

```python
import math
import jax
import jax.numpy as jnp
from jax import lax

M = 256
TR = 1024
TC = 128
HALO = 128
CAP = 3
NR = 2048
NC = 2048
SLOTS = 96
DEVICES = 32


def draw_corners(key, part):
    row_key, col_key = jax.random.split(key, 2)
    device = jnp.arange(SLOTS, dtype=jnp.int32) // CAP
    along = NC // TC
    grp_index = device // along
    pos_index = device % along
    row_low = jnp.maximum(0, grp_index * TR - HALO)
    row_high = jnp.minimum(NR - M, grp_index * TR + TR + HALO - M)
    col_low = jnp.maximum(0, pos_index * TC - HALO)
    col_high = jnp.minimum(NC - M, pos_index * TC + TC + HALO - M)
    rows = jax.random.randint(row_key, (SLOTS,), row_low, row_high + 1)
    cols = jax.random.randint(col_key, (SLOTS,), col_low, col_high + 1)
    last_first = SLOTS - CAP
    rows = rows.at[0].set(row_low[0]).at[last_first].set(row_high[last_first])
    cols = cols.at[0].set(col_low[0]).at[last_first].set(col_high[last_first])
    return jnp.stack((rows, cols)).astype(jnp.int32)


def draw_counts(key, part):
    base_key, hot_key, pick_key = jax.random.split(key, 3)
    base = jax.random.randint(base_key, (DEVICES,), 1, CAP // 2 + 1)
    hot = jax.random.randint(hot_key, (DEVICES,), 0, 8) == 0
    chosen = jnp.arange(DEVICES) == jax.random.randint(pick_key, (), 0, DEVICES)
    return jnp.where(hot | chosen, CAP, base).astype(jnp.int32)


def level_of(rng, dims, pieces, low, high):
    def one(dim, blocks):
        heights = jax.random.uniform(jax.random.fold_in(jax.random.fold_in(rng, 6), dim), (blocks,), jnp.float32, low / len(pieces), high / len(pieces))
        return jnp.repeat(jnp.exp(heights), dims[dim] // blocks).reshape((-1,) + (1,) * (len(dims) - dim - 1))

    loudness = one(*pieces[0])
    for cut in pieces[1:]:
        loudness = loudness * one(*cut)
    return loudness


def gaussian(stream_key, dims, deviation, bound, cuts=(), held_as=jnp.bfloat16):
    array = deviation * jax.random.normal(stream_key, dims, jnp.float32)
    if cuts:
        array = array * level_of(stream_key, dims, cuts, -0.22, 0.18)
    return jnp.clip(array, -bound, bound).astype(held_as)


def setup_inputs(seed: int = 0) -> dict:
    keys = jax.random.split(jax.random.key(seed), 6)
    return {
        "object_field": gaussian(keys[0], (2, NR, NC), 0.7, 5.0, ((1, 2), (2, 16)), jnp.float32),
        "probe_field": gaussian(keys[1], (2, M, M), 0.7, 5.0, (), jnp.float32),
        "patterns": jnp.clip(jnp.exp(math.log(5.0) - 4.6051702 * jax.random.uniform(keys[2], (SLOTS, M, M), jnp.float32) ** level_of(keys[2], (SLOTS, M, M), ((0, 32),), -0.2, 0.2)), 0.05, 5.0),
        "corners": draw_corners(jax.random.fold_in(keys[5], 71), 0),
        "counts": draw_counts(jax.random.fold_in(keys[5], 71), 0),
    }


def residual_wave(probe_field, patch_field, measured):
    wave = (probe_field[0] * patch_field[0] - probe_field[1] * patch_field[1]) + 1j * (probe_field[0] * patch_field[1] + probe_field[1] * patch_field[0])
    far = jnp.fft.fft2(wave, norm="ortho")
    excess = jnp.real(far) ** 2 + jnp.imag(far) ** 2 - measured
    back = jnp.fft.ifft2(excess * far, norm="ortho")
    return jnp.real(back), jnp.imag(back)


def reference(object_field, probe_field, patterns, corners, counts):
    slot_total = patterns.shape[0]
    per_device = slot_total // counts.shape[0]

    def visit_slot(index, totals):
        grad_object, grad_probe = totals
        owner = (index // per_device).astype(jnp.int32)
        is_live = (index % per_device) < counts[owner]
        weight = jnp.where(is_live, jnp.float32(1.0), jnp.float32(0.0))
        row_at = corners[0, index].astype(jnp.int32)
        col_at = corners[1, index].astype(jnp.int32)
        anchor = (jnp.int32(0), row_at, col_at)
        patch_field = lax.dynamic_slice(object_field, anchor, (2, M, M))
        chi_re, chi_im = residual_wave(probe_field, patch_field, patterns[index])
        chi_re = chi_re.astype(jnp.float32) * weight
        chi_im = chi_im.astype(jnp.float32) * weight
        obj_re = probe_field[0] * chi_re + probe_field[1] * chi_im
        obj_im = probe_field[0] * chi_im - probe_field[1] * chi_re
        prb_re = patch_field[0] * chi_re + patch_field[1] * chi_im
        prb_im = patch_field[0] * chi_im - patch_field[1] * chi_re
        current = lax.dynamic_slice(grad_object, anchor, (2, M, M))
        grad_object = lax.dynamic_update_slice(grad_object, current + jnp.stack((obj_re, obj_im)), anchor)
        return grad_object, grad_probe + jnp.stack((prb_re, prb_im))

    start_totals = (jnp.zeros(object_field.shape, jnp.float32), jnp.zeros(probe_field.shape, jnp.float32))
    grad_object, grad_probe = lax.fori_loop(0, slot_total, visit_slot, start_totals)
    live_total = jnp.sum(counts).astype(jnp.float32)
    object_new = object_field - 0.25 * grad_object
    probe_new = probe_field - 4.0 * grad_probe / live_total
    return object_new, probe_new
```

```python
import functools

import jax
import jax.numpy as jnp
import numpy as np
from jax import lax
from jax.experimental import pallas as pl
from jax.experimental.pallas import tpu as pltpu
from jax.sharding import PartitionSpec as P

HALO = 128
STEP_OBJECT = 0.25
STEP_PROBE = 4.0
MESH = pl.DeviceIdType.MESH


def dft_tables(order):
    indices = np.arange(order, dtype=np.int64)
    angles = (indices[:, None] * indices[None, :] % order) * (2.0 * np.pi / order)
    cos = np.cos(angles) / np.sqrt(order)
    sin = -np.sin(angles) / np.sqrt(order)
    left = np.block([[cos, -sin], [sin, cos]])
    right = np.block([[cos, sin], [-sin, cos]])
    both = np.stack([left, right]).astype(np.float32)
    high = both.astype(jnp.bfloat16)
    low = (both - high.astype(np.float32)).astype(jnp.bfloat16)
    return np.stack([high, low], axis=1)


def split(x):
    high = x.astype(jnp.bfloat16)
    low = (x - high.astype(jnp.float32)).astype(jnp.bfloat16)
    return high, low


def dot(a, b):
    return jnp.dot(a, b, preferred_element_type=jnp.float32)


def table_left(tab, which, data):
    high, low = split(data)
    th, tl = tab[which, 0], tab[which, 1]
    return dot(th, high) + (dot(th, low) + dot(tl, high))


def table_right(data, tab, which):
    high, low = split(data)
    th, tl = tab[which, 0], tab[which, 1]
    return dot(high, th) + (dot(low, th) + dot(high, tl))


def shares(rows, ring):
    owners = min(ring, rows // 8)
    return owners, rows // owners


def kernel(sizes, corners, counts, obj_hbm, prb_hbm, pat_hbm, tab_hbm, obj_out, prb_out,
           ext, prb, pat, tab, nb, stage, corv, cor_recv, cor_smem,
           gmid, gsend, grecv, gacc, yrecv, gp, p1r, p1, p3r, p2, p2x, pnew,
           loc, yh, corsem, cors, patsem, gsem, ysem, csem, asem, agsem, xsem, casem):
    G, PN, S, TR, M = sizes
    grp, pos = lax.axis_index("grp"), lax.axis_index("pos")
    core, chip, chips = lax.rem(pos, 2), pos // 2, PN // 2
    half = M // 2
    side, lines = lax.rem(chip, 2), chips // 2
    ring = G * lines
    owners, h3 = shares(half, ring)
    me = grp * lines + chip // 2
    late = side != core

    def at(g, p):
        return {"device_id": (g, p), "device_id_type": MESH}

    col_peer = [at(grp, lax.rem(pos + PN - 1, PN)), at(grp, lax.rem(pos + 1, PN))]
    row_peer = [at(lax.rem(grp + G - 1, G), pos), at(lax.rem(grp + 1, G), pos)]
    col_send, col_recv = [pos > 0, pos < PN - 1], [pos < PN - 1, pos > 0]
    row_send, row_recv = [grp > 0, grp < G - 1], [grp < G - 1, grp > 0]
    partner = at(grp, pos + 1 - 2 * core)

    across = at(grp, pos + 2 - 4 * side)

    def ring_at(k):
        return lax.rem(me + k, ring)

    def ring_peer(k):
        q = ring_at(k)
        return at(q // lines, (lax.rem(q, lines) * 2 + side) * 2 + core)

    locals_ = [
        pltpu.make_async_copy(obj_hbm, ext.at[:, pl.ds(HALO, TR), :], loc.at[0]),
        pltpu.make_async_copy(prb_hbm, prb, loc.at[1]),
        pltpu.make_async_copy(pat_hbm, pat, loc.at[2]),
        pltpu.make_async_copy(tab_hbm, tab, loc.at[3]),
    ]
    for c in locals_:
        c.start()

    barrier = pltpu.get_barrier_semaphore()
    for d in range(2):
        @pl.when(col_send[d])
        def _():
            pl.semaphore_signal(barrier, inc=1, **col_peer[d])
    for k in range(1, ring):
        pl.semaphore_signal(barrier, inc=1, **ring_peer(k))
    pl.semaphore_signal(barrier, inc=1, **across)
    expected = (pos > 0).astype(jnp.int32) + (pos < PN - 1).astype(jnp.int32) + ring

    lane = lax.broadcasted_iota(jnp.int32, (M, HALO), 1)
    row8 = lax.broadcasted_iota(jnp.int32, (8, 128), 0)
    packed = jnp.zeros((8, 128), jnp.int32)
    for s in range(S):
        packed = jnp.where(row8 == s, corners[0, s] - grp * TR + HALO, packed)
    corv[...] = packed
    zero = jnp.zeros((HALO, HALO), jnp.float32)
    for s in range(S):
        for c in range(2):
            for at_row in (0, HALO + M):
                gmid[s, c, pl.ds(at_row, HALO), :] = zero
                for d in range(2):
                    grecv[d, s, c, pl.ds(at_row, HALO), :] = zero
    gp[...] = jnp.zeros(gp.shape, jnp.float32)

    pl.semaphore_wait(barrier, expected)

    def cor_copy(d):
        return pltpu.make_async_remote_copy(corv, cor_recv.at[d], corsem.at[0, d], corsem.at[1, d], **col_peer[d])

    def cor_local(d):
        return pltpu.make_async_copy(cor_recv.at[d], cor_smem.at[d], cors.at[d])

    def halo_copy(d):
        src, dst = ((0, HALO + TR), (TR - HALO, 0))[d]
        return pltpu.make_async_remote_copy(
            obj_hbm.at[:, pl.ds(src, HALO), :], ext.at[:, pl.ds(dst, HALO), :], yh.at[0, d], yh.at[1, d], **row_peer[d])

    for d in range(2):
        @pl.when(col_send[d])
        def _():
            cor_copy(d).start()

        @pl.when(row_send[d])
        def _():
            halo_copy(d).start()
    for d in range(2):
        @pl.when(col_recv[d])
        def _():
            cor_copy(d).wait_recv()
            cor_local(d).start()
    for d in range(2):
        @pl.when(col_recv[d])
        def _():
            cor_local(d).wait()
    locals_[0].wait()
    for d in range(2):
        @pl.when(row_recv[d])
        def _():
            halo_copy(d).wait_recv()

    def patch_copy(d, s):
        return pltpu.make_async_remote_copy(
            stage.at[d, s], nb.at[d, s], patsem.at[0, d, s], patsem.at[1, d, s], **col_peer[d])

    def grad_copy(d, s, c):
        return pltpu.make_async_remote_copy(
            gsend.at[d, s, c], grecv.at[d, s, c, pl.ds(HALO, M), :],
            gsem.at[0, d, s, c], gsem.at[1, d, s, c], **col_peer[d])

    for s in range(S):
        for d in range(2):
            @pl.when(col_send[d])
            def _():
                r = jnp.clip(cor_smem[1 - d, s, 0], 0, TR + 2 * HALO - M)
                for c in range(2):
                    stage[d, s, c] = ext[c, pl.ds(r, M), :]
                patch_copy(d, s).start()

    for c in locals_[1:]:
        c.wait()
    own_count = counts[grp * PN + pos]

    def slot(s, carry):
        r = jnp.clip(corners[0, s] - grp * TR + HALO, 0, TR + 2 * HALO - M)
        shift = jnp.clip(corners[1, s] - pos * HALO + HALO, 0, HALO)
        for d in range(2):
            @pl.when(col_recv[d])
            def _():
                patch_copy(d, s).wait_recv()
        back = lax.rem(HALO - shift, HALO)
        forth = lax.rem(shift, HALO)
        first = lane < HALO - shift
        patch = []
        for c in range(2):
            mid = pltpu.roll(ext[c, pl.ds(r, M), :], back, 1)
            before = pltpu.roll(nb[1, s, c], back, 1)
            after = pltpu.roll(nb[0, s, c], back, 1)
            patch.append(jnp.concatenate([jnp.where(first, before, mid), jnp.where(first, mid, after)], axis=1))
        pr, pi = prb[0], prb[1]
        wave = jnp.concatenate([pr * patch[0] - pi * patch[1], pr * patch[1] + pi * patch[0]], axis=0)
        front = table_left(tab, 0, wave)
        far = table_right(jnp.concatenate([front[:M], front[M:]], axis=1), tab, 1)
        fr, fi = far[:, :M], far[:, M:]
        excess = fr * fr + fi * fi - pat[s]
        excess = jnp.where(jnp.full((M, M), s, jnp.int32) < own_count, excess, 0.0)
        back_ = table_left(tab, 1, jnp.concatenate([excess * fr, excess * fi], axis=0))
        chi = table_right(jnp.concatenate([back_[:M], back_[M:]], axis=1), tab, 0)
        cr, ci = chi[:, :M], chi[:, M:]
        parts = (pr * cr + pi * ci, pr * ci - pi * cr)
        gp[0] += patch[0] * cr + patch[1] * ci
        gp[1] += patch[0] * ci - patch[1] * cr
        tail = lane >= shift
        for c in range(2):
            g0 = pltpu.roll(parts[c][:, :HALO], forth, 1)
            g1 = pltpu.roll(parts[c][:, HALO:], forth, 1)
            gsend[0, s, c] = jnp.where(tail, g0, 0.0)
            gmid[s, c, pl.ds(HALO, M), :] = jnp.where(tail, g1, g0)
            gsend[1, s, c] = jnp.where(tail, 0.0, g1)
        for d in range(2):
            @pl.when(col_send[d] & ((core != d) | (late & (s < S - 1))))
            def _():
                for c in range(2):
                    grad_copy(d, s, c).start()
        return carry

    lax.fori_loop(0, S, slot, 0)

    core_copy = pltpu.make_async_remote_copy(
        gp.at[:, pl.ds((1 - core) * half, half), :], p1r, csem.at[0], csem.at[1], **partner)
    core_copy.start()

    def held(first, which):
        for d in range(2):
            @pl.when(col_send[d] & (core == d) & which)
            def _():
                for s in range(first, S):
                    for c in range(2):
                        grad_copy(d, s, c).start()

    for d in range(2):
        @pl.when(col_recv[d] & (core == d))
        def _():
            for s in range(S - 1):
                for c in range(2):
                    grad_copy(d, s, c).wait_recv()
    held(0, ~late)

    live = counts[0]
    for i in range(1, G * PN):
        live = live + counts[i]

    core_copy.wait_recv()
    p1[...] = gp[:, pl.ds(pl.multiple_of(core * half, half), half), :] + p1r[...]

    def share_rows(q):
        return pl.ds(pl.multiple_of(lax.rem(q, owners) * h3, 8), h3)

    def share_copy(k):
        return pltpu.make_async_remote_copy(
            p1.at[:, share_rows(ring_at(k)), :], p3r.at[k], asem.at[0, k], asem.at[1, k], **ring_peer(k))

    for k in range(1, ring):
        @pl.when(ring_at(k) < owners)
        def _():
            share_copy(k).start()

    def new_rows(owner):
        return pl.ds(pl.multiple_of(core * half + lax.rem(owner, owners) * h3, 8), h3)

    across_copy = pltpu.make_async_remote_copy(p2, p2x, xsem.at[0], xsem.at[1], **across)

    @pl.when(me < owners)
    def _():
        total = p1[:, share_rows(me), :]
        for k in range(1, ring):
            share_copy(k).wait_recv()
            total = total + p3r[k]
        p2[...] = total
        across_copy.start()

    held(S - 1, late)

    def spread_copy(k, owner):
        return pltpu.make_async_remote_copy(
            pnew.at[:, new_rows(owner), :], pnew.at[:, new_rows(owner), :], agsem.at[0, k], agsem.at[1, k],
            **ring_peer(k))

    @pl.when(me < owners)
    def _():
        across_copy.wait_recv()
        total = p2[...] + p2x[...]
        divisor = jnp.full(total.shape, live, jnp.int32).astype(jnp.float32)
        pnew[:, new_rows(me), :] = prb[:, new_rows(me), :] - STEP_PROBE * total / divisor
        for k in range(1, ring):
            spread_copy(k, me).start()

    for k in range(1, ring):
        source = lax.rem(me + ring - k, ring)

        @pl.when(source < owners)
        def _():
            spread_copy(k, source).wait_recv()

    def core_spread(c):
        rows = pl.ds(pl.multiple_of(c * half, half), half)
        return pltpu.make_async_remote_copy(pnew.at[:, rows, :], pnew.at[:, rows, :], casem.at[0], casem.at[1], **partner)

    core_spread(core).start()

    for d in range(2):
        @pl.when(col_recv[d])
        def _():
            for s in range(S):
                @pl.when((core != d) | (s == S - 1))
                def _():
                    for c in range(2):
                        grad_copy(d, s, c).wait_recv()

    def gather(base):
        totals = [jnp.zeros((HALO, HALO), jnp.float32)] * 2
        for s in range(S):
            off = jnp.clip(base - (corners[0, s] - grp * TR + HALO) + HALO, 0, HALO + M)
            totals = [totals[c] + gmid[s, c, pl.ds(off, HALO), :] for c in range(2)]
        for c in range(2):
            gacc[c, pl.ds(base, HALO), :] = totals[c]
        for d in range(2):
            @pl.when(col_recv[d])
            def _():
                for c in range(2):
                    total = gacc[c, pl.ds(base, HALO), :]
                    for s in range(S):
                        off = jnp.clip(base - cor_smem[d, s, 0] + HALO, 0, HALO + M)
                        total = total + grecv[d, s, c, pl.ds(off, HALO), :]
                    gacc[c, pl.ds(base, HALO), :] = total

    def gather_rim(chunk, carry):
        gather(pl.multiple_of(chunk * (TR + HALO), HALO))
        return carry

    def gather_core(chunk, carry):
        base = pl.multiple_of(chunk * HALO + HALO, HALO)
        gather(base)
        for c in range(2):
            obj_out[c, pl.ds(pl.multiple_of(chunk * HALO, HALO), HALO), :] = (
                ext[c, pl.ds(base, HALO), :] - STEP_OBJECT * gacc[c, pl.ds(base, HALO), :])
        return carry

    lax.fori_loop(0, 2, gather_rim, 0)

    def rim_copy(d):
        src = (0, HALO + TR)[d]
        return pltpu.make_async_remote_copy(
            gacc.at[:, pl.ds(src, HALO), :], yrecv.at[d], ysem.at[0, d], ysem.at[1, d], **row_peer[d])

    for d in range(2):
        @pl.when(row_send[d])
        def _():
            rim_copy(d).start()

    lax.fori_loop(0, TR // HALO, gather_core, 0)
    for d in range(2):
        @pl.when(row_recv[d])
        def _():
            rim_copy(d).wait_recv()
            rows = pl.ds((TR - HALO, 0)[d], HALO)
            obj_out[:, rows, :] = obj_out[:, rows, :] - STEP_OBJECT * yrecv[d]

    core_spread(1 - core).wait_recv()
    prb_out[...] = pnew[...]

    for d in range(2):
        @pl.when(col_send[d])
        def _():
            cor_copy(d).wait_send()
            for s in range(S):
                patch_copy(d, s).wait_send()
                for c in range(2):
                    grad_copy(d, s, c).wait_send()

        @pl.when(row_send[d])
        def _():
            halo_copy(d).wait_send()
            rim_copy(d).wait_send()
    core_copy.wait_send()

    @pl.when(me < owners)
    def _():
        across_copy.wait_send()
    for k in range(1, ring):
        @pl.when(ring_at(k) < owners)
        def _():
            share_copy(k).wait_send()

        @pl.when(me < owners)
        def _():
            spread_copy(k, me).wait_send()
    core_spread(core).wait_send()


def on_device(grp_size, pos_size, tables, object_field, probe_field, patterns, corners, counts):
    TR, S, M = object_field.shape[1], patterns.shape[0], probe_field.shape[1]
    chips, half = pos_size // 2, M // 2
    ring = grp_size * (chips // 2)
    owners, h3 = shares(half, ring)
    f32 = jnp.float32
    V, D = pltpu.VMEM, pltpu.SemaphoreType.DMA
    smem = pl.BlockSpec(memory_space=pltpu.SMEM)
    hbm = pl.BlockSpec(memory_space=pl.ANY)
    vmem = pl.BlockSpec(memory_space=pltpu.VMEM)
    return pl.pallas_call(
        functools.partial(kernel, (grp_size, pos_size, S, TR, M)),
        out_shape=(
            pltpu.VMEM(object_field.shape, f32),
            pltpu.VMEM(probe_field.shape, f32),
        ),
        in_specs=[smem, smem, hbm, hbm, hbm, hbm],
        out_specs=(vmem, vmem),
        scratch_shapes=[
            V((2, TR + 2 * HALO, HALO), f32),
            V((2, M, M), f32),
            V((S, M, M), f32),
            V(tables.shape, jnp.bfloat16),
            V((2, S, 2, M, HALO), f32),
            V((2, S, 2, M, HALO), f32),
            V((8, 128), jnp.int32),
            V((2, 8, 128), jnp.int32),
            pltpu.SMEM((2, 8, 128), jnp.int32),
            V((S, 2, M + 2 * HALO, HALO), f32),
            V((2, S, 2, M, HALO), f32),
            V((2, S, 2, M + 2 * HALO, HALO), f32),
            V((2, TR + 2 * HALO, HALO), f32),
            V((2, 2, HALO, HALO), f32),
            V((2, M, M), f32),
            V((2, half, M), f32),
            V((2, half, M), f32),
            V((ring, 2, h3, M), f32),
            V((2, h3, M), f32),
            V((2, h3, M), f32),
            V((2, M, M), f32),
            D((4,)), D((2, 2)), D((2, 2)), D((2,)), D((2, 2, S)), D((2, 2, S, 2)), D((2, 2)), D((2,)),
            D((2, ring)), D((2, ring)), D((2,)), D((2,)),
        ],
        compiler_params=pltpu.CompilerParams(
            collective_id=0, has_side_effects=True, vmem_limit_bytes=56 * 1024 * 1024
        ),
    )(corners, counts, object_field, probe_field, patterns, jnp.asarray(tables))


def solution(mesh):
    def body(object_field, probe_field, patterns, corners, counts):
        tables = dft_tables(probe_field.shape[1])
        return on_device(
            mesh.shape["grp"], mesh.shape["pos"], tables, object_field, probe_field, patterns, corners, counts
        )

    return jax.shard_map(
        body,
        mesh=mesh,
        in_specs=(
            P(None, "grp", "pos"),
            P(),
            P(("grp", "pos"), None, None),
            P(None, ("grp", "pos")),
            P(),
        ),
        out_specs=(P(None, "grp", "pos"), P()),
        check_vma=False,
    )
```

```python
import functools

import jax
import jax.numpy as jnp
import numpy as np
from jax import lax
from jax.experimental import pallas as pl
from jax.experimental.pallas import tpu as pltpu
from jax.sharding import PartitionSpec as P

HALO = 128
STEP_OBJECT = 0.25
STEP_PROBE = 4.0
MESH = pl.DeviceIdType.MESH


def dft_tables(order):
    half = order // 2
    columns = np.arange(half, dtype=np.int64)
    tables = []
    for odd in range(2):
        rows = 2 * np.arange(half, dtype=np.int64) + odd
        angles = (rows[:, None] * columns[None, :] % order) * (2.0 * np.pi / order)
        re, im = np.cos(angles) / np.sqrt(order), -np.sin(angles) / np.sqrt(order)
        block = np.block([[re, -im], [im, re]])
        tables.append(np.stack([block, block.T]))
    both = np.stack(tables).astype(np.float32)
    high = both.astype(jnp.bfloat16)
    low = (both - high.astype(np.float32)).astype(jnp.bfloat16)
    return np.stack([high, low], axis=2)


def split(x):
    high = x.astype(jnp.bfloat16)
    low = (x - high.astype(jnp.float32)).astype(jnp.bfloat16)
    return high, low


def dot(a, b):
    return jnp.dot(a, b, preferred_element_type=jnp.float32)


def table_left(tab, odd, turn, data):
    high, low = split(data)
    th, tl = tab[odd, turn, 0], tab[odd, turn, 1]
    return dot(th, high) + (dot(th, low) + dot(tl, high))


def table_right(data, tab, odd, turn):
    high, low = split(data)
    th, tl = tab[odd, turn, 0], tab[odd, turn, 1]
    return dot(high, th) + (dot(low, th) + dot(high, tl))


def rows_of(x, h):
    n = x.shape[0] // 2
    return x[h * n : (h + 1) * n]


def cols_of(x, h):
    n = x.shape[1] // 2
    return x[:, h * n : (h + 1) * n]


def stack(a, b):
    return jnp.concatenate([a, b], axis=0)


def side_by_side(a, b):
    return jnp.concatenate([a, b], axis=1)


def forward(tab, re, im):
    r0, r1, i0, i1 = rows_of(re, 0), rows_of(re, 1), rows_of(im, 0), rows_of(im, 1)
    even = table_left(tab, 0, 0, stack(r0 + r1, i0 + i1))
    odd = table_left(tab, 1, 0, stack(r0 - r1, i0 - i1))
    re, im = stack(rows_of(even, 0), rows_of(odd, 0)), stack(rows_of(even, 1), rows_of(odd, 1))
    r0, r1, i0, i1 = cols_of(re, 0), cols_of(re, 1), cols_of(im, 0), cols_of(im, 1)
    even = table_right(side_by_side(r0 + r1, i0 + i1), tab, 0, 1)
    odd = table_right(side_by_side(r0 - r1, i0 - i1), tab, 1, 1)
    return side_by_side(cols_of(even, 0), cols_of(odd, 0)), side_by_side(cols_of(even, 1), cols_of(odd, 1))


def backward(tab, re, im):
    even = table_left(tab, 0, 1, stack(rows_of(re, 0), rows_of(im, 0)))
    odd = table_left(tab, 1, 1, stack(rows_of(re, 1), rows_of(im, 1)))
    total, rest = even + odd, even - odd
    re, im = stack(rows_of(total, 0), rows_of(rest, 0)), stack(rows_of(total, 1), rows_of(rest, 1))
    even = table_right(side_by_side(cols_of(re, 0), cols_of(im, 0)), tab, 0, 0)
    odd = table_right(side_by_side(cols_of(re, 1), cols_of(im, 1)), tab, 1, 0)
    total, rest = even + odd, even - odd
    return side_by_side(cols_of(total, 0), cols_of(rest, 0)), side_by_side(cols_of(total, 1), cols_of(rest, 1))


def shares(rows, ring):
    owners = min(ring, rows // 8)
    return owners, rows // owners


def kernel(sizes, corners, counts, obj_hbm, prb_hbm, pat_hbm, tab_hbm, obj_out, prb_out,
           ext, prb, pat, patp, tab, nb, stage, corv, cor_recv, cor_smem,
           gmid, gsend, grecv, relay, turned, rim, yrecv, gp, p1r, p3r, p2, p2x, pnew,
           loc, yh, corsem, cors, patsem, gsem, rsem, fsem, ysem, csem, asem, agsem, xsem, casem):
    G, PN, S, TR, M = sizes
    grp, pos = lax.axis_index("grp"), lax.axis_index("pos")
    core, chip, chips = lax.rem(pos, 2), pos // 2, PN // 2
    side, lines = lax.rem(chip, 2), chips // 2
    ring = G * lines
    owners, h3 = shares(M, ring)
    me = grp * lines + chip // 2
    late = side != core
    blocks = TR // HALO + 2

    def at(g, p):
        return {"device_id": (g, lax.rem(p + PN, PN)), "device_id_type": MESH}

    col_peer = [at(grp, pos - 1), at(grp, pos + 1)]
    row_peer = [at(lax.rem(grp + G - 1, G), pos), at(lax.rem(grp + 1, G), pos)]
    col_send, col_recv = [pos > 0, pos < PN - 1], [pos < PN - 1, pos > 0]
    row_send, row_recv = [grp > 0, grp < G - 1], [grp < G - 1, grp > 0]
    partner = at(grp, pos + 1 - 2 * core)
    across = at(grp, pos + 2 * core - 1)
    has_outer = ((core == 0) & (pos > 0)) | ((core == 1) & (pos < PN - 1))
    has_relay = late & (((core == 1) & (pos + 3 < PN)) | ((core == 0) & (pos >= 3)))
    relay_peer, feeder = at(grp, pos + 6 * core - 3), at(grp, pos + 2 - 4 * core)
    forward_peer = at(grp, pos + 4 * core - 2)

    def ring_at(k):
        return lax.rem(me + k, ring)

    def ring_peer(k):
        q = ring_at(k)
        return at(q // lines, (lax.rem(q, lines) * 2 + side) * 2 + core)

    locals_ = [
        pltpu.make_async_copy(obj_hbm, ext.at[:, pl.ds(HALO, TR), :], loc.at[0]),
        pltpu.make_async_copy(prb_hbm, prb, loc.at[1]),
        pltpu.make_async_copy(tab_hbm, tab, loc.at[2]),
    ] + [
        pltpu.make_async_copy(pat_hbm.at[:, :, pl.ds(w * HALO, HALO)], pat.at[w], loc.at[3 + w])
        for w in range(2)
    ]
    for c in locals_:
        c.start()

    barrier = pltpu.get_barrier_semaphore()

    def greet(condition, peers):
        @pl.when(condition)
        def _():
            for peer in peers:
                pl.semaphore_signal(barrier, inc=1, **peer)
        return condition.astype(jnp.int32) * len(peers)

    expected = greet(col_send[0], [col_peer[0]]) + greet(col_send[1], [col_peer[1]])
    expected += greet(~late & row_send[0], [row_peer[0]]) + greet(~late & row_send[1], [row_peer[1]])
    expected += greet(late, [ring_peer(k) for k in range(1, ring)])
    expected += greet(~late & has_outer, [relay_peer, feeder]) + greet(has_relay, [relay_peer, forward_peer])

    lane = lax.broadcasted_iota(jnp.int32, (M, HALO), 1)
    row8 = lax.broadcasted_iota(jnp.int32, (8, 128), 0)
    packed = jnp.zeros((8, 128), jnp.int32)
    for s in range(S):
        packed = jnp.where(row8 == s, corners[0, s] - grp * TR + HALO, packed)
    corv[...] = packed
    gp[...] = jnp.zeros(gp.shape, jnp.float32)

    pl.semaphore_wait(barrier, expected)

    def cor_copy(d):
        return pltpu.make_async_remote_copy(corv, cor_recv.at[d], corsem.at[0, d], corsem.at[1, d], **col_peer[d])

    def cor_local(d):
        return pltpu.make_async_copy(cor_recv.at[d], cor_smem.at[d], cors.at[d])

    def halo_copy(d):
        src, dst = ((0, HALO + TR), (TR - HALO, 0))[d]
        return pltpu.make_async_remote_copy(
            obj_hbm.at[:, pl.ds(src, HALO), :], ext.at[:, pl.ds(dst, HALO), :], yh.at[0, d], yh.at[1, d], **row_peer[d])

    for d in range(2):
        @pl.when(col_send[d])
        def _():
            cor_copy(d).start()

        @pl.when(row_send[d])
        def _():
            halo_copy(d).start()
    for d in range(2):
        @pl.when(col_recv[d])
        def _():
            cor_copy(d).wait_recv()
            cor_local(d).start()
    for d in range(2):
        @pl.when(col_recv[d])
        def _():
            cor_local(d).wait()
    locals_[0].wait()
    for d in range(2):
        @pl.when(row_recv[d])
        def _():
            halo_copy(d).wait_recv()

    def patch_copy(d, s):
        return pltpu.make_async_remote_copy(
            stage.at[d, s], nb.at[d, s], patsem.at[0, d, s], patsem.at[1, d, s], **col_peer[d])

    for s in range(S):
        for d in range(2):
            @pl.when(col_send[d])
            def _():
                r = jnp.clip(cor_smem[1 - d, s, 0], 0, TR + 2 * HALO - M)
                for c in range(2):
                    stage[d, s, c] = ext[c, pl.ds(r, M), :]
                patch_copy(d, s).start()

    def grad_to(d, s, h, peer):
        return pltpu.make_async_remote_copy(
            gsend.at[d, s, h], grecv.at[d, s, h], gsem.at[0, d, s, h], gsem.at[1, d, s, h], **peer)

    def chip_grad(s, h):
        return grad_to(1 - core, s, h, partner)

    def outer_grad(s, h):
        return grad_to(core, s, h, across)

    def relay_grad(s, h):
        return pltpu.make_async_remote_copy(
            gsend.at[core, s, h], relay.at[s, h], gsem.at[0, core, s, h], rsem.at[s, h], **relay_peer)

    def forward_grad(s, h):
        return pltpu.make_async_remote_copy(
            relay.at[s, h], grecv.at[1 - core, s, h], fsem.at[s, h], gsem.at[1, 1 - core, s, h], **forward_peer)

    first_half = (grp < G - 1).astype(jnp.int32)
    halves = [first_half, 1 - first_half]

    for c in locals_[1:]:
        c.wait()
    own_count = counts[grp * PN + pos]

    column = lax.broadcasted_iota(jnp.int32, (M, M), 1)
    wanted = jnp.where(column < M // 2, 2 * column, 2 * column - (M - 1))
    pick = (lax.broadcasted_iota(jnp.int32, (M, M), 0) == wanted).astype(jnp.float32).astype(jnp.bfloat16)

    def reorder(s, carry):
        rows = side_by_side(*[
            stack(*[pat[w, s, pl.ds(odd, M // 2, stride=2), :] for odd in range(2)]) for w in range(2)
        ])
        high, low = split(rows)
        last = (rows - high.astype(jnp.float32) - low.astype(jnp.float32)).astype(jnp.bfloat16)
        patp[s] = dot(high, pick) + (dot(low, pick) + dot(last, pick))
        return carry

    lax.fori_loop(0, S, reorder, 0)

    def row_of(s):
        return jnp.clip(corners[0, s] - grp * TR + HALO, 0, TR + 2 * HALO - M)

    def slot(s, carry):
        r = row_of(s)
        shift = jnp.clip(corners[1, s] - pos * HALO + HALO, 0, HALO)
        for d in range(2):
            @pl.when(col_recv[d])
            def _():
                patch_copy(d, s).wait_recv()
        back = lax.rem(HALO - shift, HALO)
        forth = lax.rem(shift, HALO)
        first = lane < HALO - shift
        patch = []
        for c in range(2):
            mid = pltpu.roll(ext[c, pl.ds(r, M), :], back, 1)
            before = pltpu.roll(nb[1, s, c], back, 1)
            after = pltpu.roll(nb[0, s, c], back, 1)
            patch.append(side_by_side(jnp.where(first, before, mid), jnp.where(first, mid, after)))
        pr, pi = prb[0], prb[1]
        fr, fi = forward(tab, pr * patch[0] - pi * patch[1], pr * patch[1] + pi * patch[0])
        excess = fr * fr + fi * fi - patp[s]
        excess = jnp.where(jnp.full((M, M), s, jnp.int32) < own_count, excess, 0.0)
        cr, ci = backward(tab, excess * fr, excess * fi)
        parts = (pr * cr + pi * ci, pr * ci - pi * cr)
        gp[0] += patch[0] * cr + patch[1] * ci
        gp[1] += patch[0] * ci - patch[1] * cr
        tail = lane >= shift
        for c in range(2):
            for w in range(2):
                turned[c, w, :M] = cols_of(parts[c], w)
                turned[c, w, M:] = cols_of(parts[c], w)
        start = M - lax.rem(r, M)
        for c in range(2):
            g0, g1 = [pltpu.roll(turned[c, w, pl.ds(start, M), :], forth, 1) for w in range(2)]
            left, middle, right = jnp.where(tail, g0, 0.0), jnp.where(tail, g1, g0), jnp.where(tail, 0.0, g1)
            for h in range(2):
                gsend[0, s, h, c] = rows_of(left, h)
                gmid[s, h, c] = rows_of(middle, h)
                gsend[1, s, h, c] = rows_of(right, h)
        for h in range(2):
            chip_grad(s, h).start()

        @pl.when(has_outer & late)
        def _():
            outer_grad(s, halves[0]).start()

        @pl.when(has_outer & ~late)
        def _():
            for h in halves:
                relay_grad(s, h).start()
        return carry

    lax.fori_loop(0, S, slot, 0)

    core_copy = pltpu.make_async_remote_copy(gp, p1r, csem.at[0], csem.at[1], **partner)

    def share_rows(q):
        return pl.ds(pl.multiple_of(lax.rem(q, owners) * h3, 8), h3)

    def share_copy(k):
        return pltpu.make_async_remote_copy(
            gp.at[:, share_rows(ring_at(k)), :], p3r.at[k], asem.at[0, k], asem.at[1, k], **ring_peer(k))

    across_copy = pltpu.make_async_remote_copy(p2, p2x, xsem.at[0], xsem.at[1], **across)

    def spread_copy(k, owner):
        rows = share_rows(owner)
        return pltpu.make_async_remote_copy(
            pnew.at[:, rows, :], pnew.at[:, rows, :], agsem.at[0, k], agsem.at[1, k], **ring_peer(k))

    def hand_copy(owner):
        q = lax.rem(owner, owners)
        rows = share_rows(owner)
        return pltpu.make_async_remote_copy(
            pnew.at[:, rows, :], pnew.at[:, rows, :], casem.at[0, q], casem.at[1, q], **partner)

    def source(k):
        return lax.rem(me + ring - k, ring)

    def pass_on(h):
        @pl.when(has_relay)
        def _():
            for s in range(S):
                relay_grad(s, h).wait_recv()
                forward_grad(s, h).start()

    @pl.when(~late)
    def _():
        core_copy.start()

    @pl.when(late)
    def _():
        core_copy.wait_recv()
        gp[...] += p1r[...]
        for k in range(1, ring):
            @pl.when(ring_at(k) < owners)
            def _():
                share_copy(k).start()

        pass_on(halves[0])

        @pl.when(me < owners)
        def _():
            total = gp[:, share_rows(me), :]
            for k in range(1, ring):
                share_copy(k).wait_recv()
                total = total + p3r[k]
            p2[...] = total
            across_copy.start()

        @pl.when(has_outer)
        def _():
            for s in range(S):
                outer_grad(s, halves[1]).start()
        pass_on(halves[1])

    def covers(block, r):
        rows = lax.broadcasted_iota(jnp.int32, (HALO, HALO), 0) + (block * HALO - r)
        return (rows >= 0) & (rows < M)

    def own(totals, block, h):
        for s in range(S):
            inside = covers(block, row_of(s))
            totals = [t + jnp.where(inside, gmid[s, h, c], 0.0) for c, t in enumerate(totals)]
        return totals

    def others(totals, block, h, d):
        for s in range(S):
            inside = covers(block, cor_smem[d, s, 0])
            totals = [t + jnp.where(inside, grecv[d, s, h, c], 0.0) for c, t in enumerate(totals)]
        return totals

    zeros = [jnp.zeros((HALO, HALO), jnp.float32)] * 2

    for s in range(S):
        for h in range(2):
            grad_to(core, s, h, partner).wait_recv()

    def near(block, carry):
        h = lax.rem(block, 2)
        totals = others(own(zeros, block, h), block, h, core)
        rows = pl.ds(pl.multiple_of(block * HALO, HALO), HALO)
        for c in range(2):
            obj_out[c, pl.ds(pl.multiple_of(block * HALO - HALO, HALO), HALO), :] = (
                ext[c, rows, :] - STEP_OBJECT * totals[c])
        return carry

    lax.fori_loop(1, blocks - 1, near, 0)

    @pl.when(late & (me < owners))
    def _():
        live = counts[0]
        for i in range(1, G * PN):
            live = live + counts[i]
        across_copy.wait_recv()
        total = p2[...] + p2x[...]
        divisor = jnp.full(total.shape, live, jnp.int32).astype(jnp.float32)
        pnew[:, share_rows(me), :] = prb[:, share_rows(me), :] - STEP_PROBE * total / divisor
        for k in range(1, ring):
            spread_copy(k, me).start()
        hand_copy(me).start()

    def rim_copy(d):
        return pltpu.make_async_remote_copy(rim.at[d], yrecv.at[d], ysem.at[0, d], ysem.at[1, d], **row_peer[d])

    def finish(h):
        @pl.when(has_outer)
        def _():
            for s in range(S):
                grad_to(1 - core, s, h, partner).wait_recv()
        for d in range(2):
            block = d * (blocks - 1)

            @pl.when(row_send[d] & (h == d))
            def _():
                totals = others(own(zeros, block, d), block, d, core)
                for c in range(2):
                    rim[d, c] = totals[c]

                @pl.when(has_outer)
                def _():
                    more = others([rim[d, c] for c in range(2)], block, d, 1 - core)
                    for c in range(2):
                        rim[d, c] = more[c]
                rim_copy(d).start()

        @pl.when(has_outer)
        def _():
            def far(i, carry):
                block = 2 * i + 2 - h
                totals = others(zeros, block, h, 1 - core)
                rows = pl.ds(pl.multiple_of(block * HALO - HALO, HALO), HALO)
                for c in range(2):
                    obj_out[c, rows, :] = obj_out[c, rows, :] - STEP_OBJECT * totals[c]
                return carry

            lax.fori_loop(0, blocks // 2 - 1, far, 0)

    finish(halves[0])

    @pl.when(late)
    def _():
        for k in range(1, ring):
            @pl.when(source(k) < owners)
            def _():
                spread_copy(k, source(k)).wait_recv()
                hand_copy(source(k)).start()

    finish(halves[1])
    for d in range(2):
        @pl.when(row_recv[d])
        def _():
            rim_copy(d).wait_recv()
            rows = pl.ds((TR - HALO, 0)[d], HALO)
            obj_out[:, rows, :] = obj_out[:, rows, :] - STEP_OBJECT * yrecv[d]

    @pl.when(~late)
    def _():
        for q in range(owners):
            hand_copy(q).wait_recv()
    prb_out[...] = pnew[...]

    for d in range(2):
        @pl.when(col_send[d])
        def _():
            cor_copy(d).wait_send()
            for s in range(S):
                patch_copy(d, s).wait_send()

        @pl.when(row_send[d])
        def _():
            halo_copy(d).wait_send()
            rim_copy(d).wait_send()
    for s in range(S):
        for h in range(2):
            chip_grad(s, h).wait_send()

            @pl.when(has_outer)
            def _():
                outer_grad(s, h).wait_send()

            @pl.when(has_relay)
            def _():
                forward_grad(s, h).wait_send()

    @pl.when(~late)
    def _():
        core_copy.wait_send()

    @pl.when(late)
    def _():
        for k in range(1, ring):
            @pl.when(ring_at(k) < owners)
            def _():
                share_copy(k).wait_send()

        @pl.when(me < owners)
        def _():
            across_copy.wait_send()
            for k in range(1, ring):
                spread_copy(k, me).wait_send()
        for q in range(owners):
            hand_copy(q).wait_send()


def on_device(grp_size, pos_size, tables, object_field, probe_field, patterns, corners, counts):
    TR, S, M = object_field.shape[1], patterns.shape[0], probe_field.shape[1]
    ring = grp_size * (pos_size // 4)
    owners, h3 = shares(M, ring)
    f32 = jnp.float32
    V, D = pltpu.VMEM, pltpu.SemaphoreType.DMA
    smem = pl.BlockSpec(memory_space=pltpu.SMEM)
    hbm = pl.BlockSpec(memory_space=pl.ANY)
    vmem = pl.BlockSpec(memory_space=pltpu.VMEM)
    half = (2, HALO, HALO)
    return pl.pallas_call(
        functools.partial(kernel, (grp_size, pos_size, S, TR, M)),
        out_shape=(
            pltpu.VMEM(object_field.shape, f32),
            pltpu.VMEM(probe_field.shape, f32),
        ),
        in_specs=[smem, smem, hbm, hbm, hbm, hbm],
        out_specs=(vmem, vmem),
        scratch_shapes=[
            V((2, TR + 2 * HALO, HALO), f32),
            V((2, M, M), f32),
            V((2, S, M, HALO), f32),
            V((S, M, M), f32),
            V(tables.shape, jnp.bfloat16),
            V((2, S, 2, M, HALO), f32),
            V((2, S, 2, M, HALO), f32),
            V((8, 128), jnp.int32),
            V((2, 8, 128), jnp.int32),
            pltpu.SMEM((2, 8, 128), jnp.int32),
            V((S, 2, *half), f32),
            V((2, S, 2, *half), f32),
            V((2, S, 2, *half), f32),
            V((S, 2, *half), f32),
            V((2, 2, 2 * M, HALO), f32),
            V((2, *half), f32),
            V((2, *half), f32),
            V((2, M, M), f32),
            V((2, M, M), f32),
            V((ring, 2, h3, M), f32),
            V((2, h3, M), f32),
            V((2, h3, M), f32),
            V((2, M, M), f32),
            D((5,)), D((2, 2)), D((2, 2)), D((2,)), D((2, 2, S)), D((2, 2, S, 2)), D((S, 2)), D((S, 2)), D((2, 2)),
            D((2,)), D((2, ring)), D((2, ring)), D((2,)), D((2, owners)),
        ],
        compiler_params=pltpu.CompilerParams(
            collective_id=0, has_side_effects=True, vmem_limit_bytes=56 * 1024 * 1024
        ),
    )(corners, counts, object_field, probe_field, patterns, jnp.asarray(tables))

def solution(mesh):
    def body(object_field, probe_field, patterns, corners, counts):
        tables = dft_tables(probe_field.shape[1])
        return on_device(
            mesh.shape["grp"], mesh.shape["pos"], tables, object_field, probe_field, patterns, corners, counts
        )

    return jax.shard_map(
        body,
        mesh=mesh,
        in_specs=(
            P(None, "grp", "pos"),
            P(),
            P(("grp", "pos"), None, None),
            P(None, ("grp", "pos")),
            P(),
        ),
        out_specs=(P(None, "grp", "pos"), P()),
        check_vma=False,
    )
```

```python
import functools

import jax
import jax.numpy as jnp
import numpy as np
from jax import lax
from jax.experimental import pallas as pl
from jax.experimental.pallas import tpu as pltpu
from jax.sharding import PartitionSpec as P

HALO = 128
STEP_OBJECT = 0.25
STEP_PROBE = 4.0
MESH = pl.DeviceIdType.MESH


def dft_tables(order):
    half = order // 2
    columns = np.arange(half, dtype=np.int64)
    tables = []
    for odd in range(2):
        rows = 2 * np.arange(half, dtype=np.int64) + odd
        angles = (rows[:, None] * columns[None, :] % order) * (2.0 * np.pi / order)
        re, im = np.cos(angles) / np.sqrt(order), -np.sin(angles) / np.sqrt(order)
        block = np.block([[re, -im], [im, re]])
        tables.append(np.stack([block, block.T]))
    both = np.stack(tables).astype(np.float32)
    high = both.astype(jnp.bfloat16)
    low = (both - high.astype(np.float32)).astype(jnp.bfloat16)
    return np.stack([high, low], axis=2)


def split(x):
    high = x.astype(jnp.bfloat16)
    low = (x - high.astype(jnp.float32)).astype(jnp.bfloat16)
    return high, low


def dot(a, b):
    return jnp.dot(a, b, preferred_element_type=jnp.float32)


def table_left(tab, odd, turn, data):
    high, low = split(data)
    th, tl = tab[odd, turn, 0], tab[odd, turn, 1]
    return dot(th, high) + (dot(th, low) + dot(tl, high))


def table_right(data, tab, odd, turn):
    high, low = split(data)
    th, tl = tab[odd, turn, 0], tab[odd, turn, 1]
    return dot(high, th) + (dot(low, th) + dot(high, tl))


def rows_of(x, h):
    n = x.shape[0] // 2
    return x[h * n : (h + 1) * n]


def cols_of(x, h):
    n = x.shape[1] // 2
    return x[:, h * n : (h + 1) * n]


def stack(a, b):
    return jnp.concatenate([a, b], axis=0)


def side_by_side(a, b):
    return jnp.concatenate([a, b], axis=1)


def forward(tab, re, im):
    r0, r1, i0, i1 = rows_of(re, 0), rows_of(re, 1), rows_of(im, 0), rows_of(im, 1)
    even = table_left(tab, 0, 0, stack(r0 + r1, i0 + i1))
    odd = table_left(tab, 1, 0, stack(r0 - r1, i0 - i1))
    re, im = stack(rows_of(even, 0), rows_of(odd, 0)), stack(rows_of(even, 1), rows_of(odd, 1))
    r0, r1, i0, i1 = cols_of(re, 0), cols_of(re, 1), cols_of(im, 0), cols_of(im, 1)
    even = table_right(side_by_side(r0 + r1, i0 + i1), tab, 0, 1)
    odd = table_right(side_by_side(r0 - r1, i0 - i1), tab, 1, 1)
    return side_by_side(cols_of(even, 0), cols_of(odd, 0)), side_by_side(cols_of(even, 1), cols_of(odd, 1))


def backward(tab, re, im):
    even = table_left(tab, 0, 1, stack(rows_of(re, 0), rows_of(im, 0)))
    odd = table_left(tab, 1, 1, stack(rows_of(re, 1), rows_of(im, 1)))
    total, rest = even + odd, even - odd
    re, im = stack(rows_of(total, 0), rows_of(rest, 0)), stack(rows_of(total, 1), rows_of(rest, 1))
    even = table_right(side_by_side(cols_of(re, 0), cols_of(im, 0)), tab, 0, 0)
    odd = table_right(side_by_side(cols_of(re, 1), cols_of(im, 1)), tab, 1, 0)
    total, rest = even + odd, even - odd
    return side_by_side(cols_of(total, 0), cols_of(rest, 0)), side_by_side(cols_of(total, 1), cols_of(rest, 1))


def shares(rows, ring):
    owners = min(ring, rows // 8)
    return owners, rows // owners


def kernel(sizes, corners, counts, obj_hbm, prb_hbm, pat_hbm, tab_hbm, obj_out, prb_out,
           ext, prb, pat, patp, tab, nb, stage, cor_smem,
           gmid, gsend, grecv, relay, turned, rim, yrecv, gp, p1r, p3r, p2, p2x, pnew,
           loc, farsem, yh, corsem, patsem, gsem, rsem, fsem, ysem, csem, asem, agsem, xsem, casem):
    G, PN, S, TR, M = sizes
    grp, pos = lax.axis_index("grp"), lax.axis_index("pos")
    core, chip, chips = lax.rem(pos, 2), pos // 2, PN // 2
    side, lines = lax.rem(chip, 2), chips // 2
    ring = G * lines
    owners, h3 = shares(M, ring)
    me = grp * lines + chip // 2
    late = side != core
    blocks = TR // HALO + 2

    def at(g, p):
        return {"device_id": (g, lax.rem(p + PN, PN)), "device_id_type": MESH}

    col_peer = [at(grp, pos - 1), at(grp, pos + 1)]
    row_peer = [at(lax.rem(grp + G - 1, G), pos), at(lax.rem(grp + 1, G), pos)]
    col_send, col_recv = [pos > 0, pos < PN - 1], [pos < PN - 1, pos > 0]
    row_send, row_recv = [grp > 0, grp < G - 1], [grp < G - 1, grp > 0]
    partner = at(grp, pos + 1 - 2 * core)
    across = at(grp, pos + 2 * core - 1)
    has_outer = ((core == 0) & (pos > 0)) | ((core == 1) & (pos < PN - 1))
    has_relay = late & (((core == 1) & (pos + 3 < PN)) | ((core == 0) & (pos >= 3)))
    relay_peer, feeder = at(grp, pos + 6 * core - 3), at(grp, pos + 2 - 4 * core)
    forward_peer = at(grp, pos + 4 * core - 2)

    def ring_at(k):
        return lax.rem(me + k, ring)

    def ring_peer(k):
        q = ring_at(k)
        return at(q // lines, (lax.rem(q, lines) * 2 + side) * 2 + core)

    locals_ = [
        pltpu.make_async_copy(obj_hbm, ext.at[:, pl.ds(HALO, TR), :], loc.at[0]),
        pltpu.make_async_copy(prb_hbm, prb, loc.at[1]),
        pltpu.make_async_copy(tab_hbm, tab, loc.at[2]),
    ] + [
        pltpu.make_async_copy(pat_hbm.at[:, :, pl.ds(w * HALO, HALO)], pat.at[w], loc.at[3 + w])
        for w in range(2)
    ]
    for c in locals_:
        c.start()

    near_ring = [
        (late & row_send[0], row_peer[0]), (late & row_send[1], row_peer[1]),
        (late & (pos >= 4), at(grp, pos - 4)), (late & (pos + 4 < PN), at(grp, pos + 4)),
    ]
    barrier = pltpu.get_barrier_semaphore()

    def greet(condition, peers):
        @pl.when(condition)
        def _():
            for peer in peers:
                pl.semaphore_signal(barrier, inc=1, **peer)
        return condition.astype(jnp.int32) * len(peers)

    expected = greet(col_send[0], [col_peer[0]]) + greet(col_send[1], [col_peer[1]])
    expected += greet(row_send[0], [row_peer[0]]) + greet(row_send[1], [row_peer[1]])
    expected += greet(near_ring[2][0], [near_ring[2][1]]) + greet(near_ring[3][0], [near_ring[3][1]])
    expected += greet(~late & has_outer, [relay_peer, feeder]) + greet(has_relay, [relay_peer, forward_peer])

    lane = lax.broadcasted_iota(jnp.int32, (M, HALO), 1)
    gp[...] = jnp.zeros(gp.shape, jnp.float32)

    locals_[0].wait()
    pl.semaphore_wait(barrier, expected)

    def cor_copy(d):
        return pltpu.make_async_remote_copy(corners, cor_smem.at[d], corsem.at[0, d], corsem.at[1, d], **col_peer[d])

    def row_at(d, s):
        return jnp.clip(cor_smem[d, 0, s] - grp * TR + HALO, 0, TR + 2 * HALO - M)

    def halo_copy(d):
        src, dst = ((HALO, HALO + TR), (TR, 0))[d]
        return pltpu.make_async_remote_copy(
            ext.at[:, pl.ds(src, HALO), :], ext.at[:, pl.ds(dst, HALO), :], yh.at[0, d], yh.at[1, d], **row_peer[d])

    for d in range(2):
        @pl.when(col_send[d])
        def _():
            cor_copy(d).start()

        @pl.when(row_send[d])
        def _():
            halo_copy(d).start()
    for d in range(2):
        @pl.when(col_recv[d])
        def _():
            cor_copy(d).wait_recv()
    for d in range(2):
        @pl.when(row_recv[d])
        def _():
            halo_copy(d).wait_recv()

    def patch_copy(d, s):
        return pltpu.make_async_remote_copy(
            stage.at[d, s], nb.at[d, s], patsem.at[0, d, s], patsem.at[1, d, s], **col_peer[d])

    for s in range(S):
        for d in range(2):
            @pl.when(col_send[d])
            def _():
                r = row_at(1 - d, s)
                for c in range(2):
                    stage[d, s, c] = ext[c, pl.ds(r, M), :]
                patch_copy(d, s).start()

    for step in range(lines + G - 3):
        for there, peer in near_ring:
            @pl.when(there)
            def _():
                pl.semaphore_signal(farsem.at[step], inc=1, **peer)
        known = sum(there.astype(jnp.int32) for there, _ in near_ring)

        @pl.when(late)
        def _():
            pl.semaphore_wait(farsem.at[step], known)

    def grad_to(d, s, h, peer):
        return pltpu.make_async_remote_copy(
            gsend.at[d, s, h], grecv.at[d, s, h], gsem.at[0, d, s, h], gsem.at[1, d, s, h], **peer)

    def chip_grad(s, h):
        return grad_to(1 - core, s, h, partner)

    def outer_grad(s, h):
        return grad_to(core, s, h, across)

    def relay_grad(s, h):
        return pltpu.make_async_remote_copy(
            gsend.at[core, s, h], relay.at[s, h], gsem.at[0, core, s, h], rsem.at[s, h], **relay_peer)

    def forward_grad(s, h):
        return pltpu.make_async_remote_copy(
            relay.at[s, h], grecv.at[1 - core, s, h], fsem.at[s, h], gsem.at[1, 1 - core, s, h], **forward_peer)

    first_half = (grp < G - 1).astype(jnp.int32)
    halves = [first_half, 1 - first_half]

    for c in locals_[1:]:
        c.wait()
    own_count = counts[grp * PN + pos]

    column = lax.broadcasted_iota(jnp.int32, (M, M), 1)
    wanted = jnp.where(column < M // 2, 2 * column, 2 * column - (M - 1))
    pick = (lax.broadcasted_iota(jnp.int32, (M, M), 0) == wanted).astype(jnp.float32).astype(jnp.bfloat16)

    def reorder(s, carry):
        rows = side_by_side(*[
            stack(*[pat[w, s, pl.ds(odd, M // 2, stride=2), :] for odd in range(2)]) for w in range(2)
        ])
        high, low = split(rows)
        last = (rows - high.astype(jnp.float32) - low.astype(jnp.float32)).astype(jnp.bfloat16)
        patp[s] = dot(high, pick) + (dot(low, pick) + dot(last, pick))
        return carry

    lax.fori_loop(0, S, reorder, 0)

    def row_of(s):
        return jnp.clip(corners[0, s] - grp * TR + HALO, 0, TR + 2 * HALO - M)

    def slot(s, carry):
        r = row_of(s)
        shift = jnp.clip(corners[1, s] - pos * HALO + HALO, 0, HALO)
        for d in range(2):
            @pl.when(col_recv[d])
            def _():
                patch_copy(d, s).wait_recv()
        back = lax.rem(HALO - shift, HALO)
        forth = lax.rem(shift, HALO)
        first = lane < HALO - shift
        patch = []
        for c in range(2):
            mid = pltpu.roll(ext[c, pl.ds(r, M), :], back, 1)
            before = pltpu.roll(nb[1, s, c], back, 1)
            after = pltpu.roll(nb[0, s, c], back, 1)
            patch.append(side_by_side(jnp.where(first, before, mid), jnp.where(first, mid, after)))
        pr, pi = prb[0], prb[1]
        fr, fi = forward(tab, pr * patch[0] - pi * patch[1], pr * patch[1] + pi * patch[0])
        excess = fr * fr + fi * fi - patp[s]
        excess = jnp.where(jnp.full((M, M), s, jnp.int32) < own_count, excess, 0.0)
        cr, ci = backward(tab, excess * fr, excess * fi)
        parts = (pr * cr + pi * ci, pr * ci - pi * cr)
        gp[0] += patch[0] * cr + patch[1] * ci
        gp[1] += patch[0] * ci - patch[1] * cr
        tail = lane >= shift
        for c in range(2):
            for w in range(2):
                turned[c, w, :M] = cols_of(parts[c], w)
                turned[c, w, M:] = cols_of(parts[c], w)
        start = M - lax.rem(r, M)
        for c in range(2):
            g0, g1 = [pltpu.roll(turned[c, w, pl.ds(start, M), :], forth, 1) for w in range(2)]
            left, middle, right = jnp.where(tail, g0, 0.0), jnp.where(tail, g1, g0), jnp.where(tail, 0.0, g1)
            for h in range(2):
                gsend[0, s, h, c] = rows_of(left, h)
                gmid[s, h, c] = rows_of(middle, h)
                gsend[1, s, h, c] = rows_of(right, h)
        for h in range(2):
            chip_grad(s, h).start()

        @pl.when(has_outer & late)
        def _():
            outer_grad(s, halves[0]).start()

        @pl.when(has_outer & ~late)
        def _():
            relay_grad(s, halves[0]).start()
        return carry

    lax.fori_loop(0, S, slot, 0)

    core_copy = pltpu.make_async_remote_copy(gp, p1r, csem.at[0], csem.at[1], **partner)

    def share_rows(q):
        return pl.ds(pl.multiple_of(lax.rem(q, owners) * h3, 8), h3)

    def share_copy(c, k):
        return pltpu.make_async_remote_copy(
            gp.at[c, share_rows(ring_at(k)), :], p3r.at[c, k], asem.at[0, c, k], asem.at[1, c, k], **ring_peer(k))

    def across_copy(c):
        return pltpu.make_async_remote_copy(p2.at[c], p2x.at[c], xsem.at[0, c], xsem.at[1, c], **across)

    def spread_copy(c, k, owner):
        rows = share_rows(owner)
        return pltpu.make_async_remote_copy(
            pnew.at[c, rows, :], pnew.at[c, rows, :], agsem.at[0, c, k], agsem.at[1, c, k], **ring_peer(k))

    def hand_copy(c, owner):
        q = lax.rem(owner, owners)
        rows = share_rows(owner)
        return pltpu.make_async_remote_copy(
            pnew.at[c, rows, :], pnew.at[c, rows, :], casem.at[0, c, q], casem.at[1, c, q], **partner)

    def source(k):
        return lax.rem(me + ring - k, ring)

    def pass_on(h):
        @pl.when(has_relay)
        def _():
            for s in range(S):
                relay_grad(s, h).wait_recv()
                forward_grad(s, h).start()

    def covers(block, r):
        rows = lax.broadcasted_iota(jnp.int32, (HALO, HALO), 0) + (block * HALO - r)
        return (rows >= 0) & (rows < M)

    def own(totals, block, h):
        for s in range(S):
            inside = covers(block, row_of(s))
            totals = [t + jnp.where(inside, gmid[s, h, c], 0.0) for c, t in enumerate(totals)]
        return totals

    def others(totals, block, h, d):
        for s in range(S):
            inside = covers(block, row_at(d, s))
            totals = [t + jnp.where(inside, grecv[d, s, h, c], 0.0) for c, t in enumerate(totals)]
        return totals

    zeros = [jnp.zeros((HALO, HALO), jnp.float32)] * 2

    def near(block, carry):
        h = lax.rem(block, 2)
        totals = others(own(zeros, block, h), block, h, core)
        rows = pl.ds(pl.multiple_of(block * HALO, HALO), HALO)
        for c in range(2):
            obj_out[c, pl.ds(pl.multiple_of(block * HALO - HALO, HALO), HALO), :] = (
                ext[c, rows, :] - STEP_OBJECT * totals[c])
        return carry

    def near_all():
        for s in range(S):
            for h in range(2):
                grad_to(core, s, h, partner).wait_recv()
        lax.fori_loop(1, blocks - 1, near, 0)

    def second(first, last):
        @pl.when(has_outer)
        def _():
            for s in range(first, last):
                outer_grad(s, halves[1]).start()

    @pl.when(~late)
    def _():
        core_copy.start()

        @pl.when(has_outer)
        def _():
            for s in range(S):
                relay_grad(s, halves[1]).start()
        near_all()

    @pl.when(late)
    def _():
        core_copy.wait_recv()
        gp[...] += p1r[...]
        for c in range(2):
            for k in range(1, ring):
                @pl.when(ring_at(k) < owners)
                def _():
                    share_copy(c, k).start()

        pass_on(halves[0])
        near_all()
        for c in range(2):
            @pl.when(me < owners)
            def _():
                total = gp[c, share_rows(me), :]
                for k in range(1, ring):
                    share_copy(c, k).wait_recv()
                    total = total + p3r[c, k]
                p2[c] = total
                across_copy(c).start()

            second(*((0, 1), (1, S))[c])

        pass_on(halves[1])
        live = counts[0]
        for i in range(1, G * PN):
            live = live + counts[i]

        @pl.when(me < owners)
        def _():
            for c in range(2):
                across_copy(c).wait_recv()
                total = p2[c] + p2x[c]
                divisor = jnp.full(total.shape, live, jnp.int32).astype(jnp.float32)
                pnew[c, share_rows(me), :] = prb[c, share_rows(me), :] - STEP_PROBE * total / divisor
                for k in range(1, ring):
                    spread_copy(c, k, me).start()
                hand_copy(c, me).start()

    def rim_copy(d):
        return pltpu.make_async_remote_copy(rim.at[d], yrecv.at[d], ysem.at[0, d], ysem.at[1, d], **row_peer[d])

    def finish(h):
        @pl.when(has_outer)
        def _():
            for s in range(S):
                grad_to(1 - core, s, h, partner).wait_recv()
        for d in range(2):
            block = d * (blocks - 1)

            @pl.when(row_send[d] & (h == d))
            def _():
                totals = others(own(zeros, block, d), block, d, core)
                for c in range(2):
                    rim[d, c] = totals[c]

                @pl.when(has_outer)
                def _():
                    more = others([rim[d, c] for c in range(2)], block, d, 1 - core)
                    for c in range(2):
                        rim[d, c] = more[c]
                rim_copy(d).start()

        @pl.when(has_outer)
        def _():
            def far(i, carry):
                block = 2 * i + 2 - h
                totals = others(zeros, block, h, 1 - core)
                rows = pl.ds(pl.multiple_of(block * HALO - HALO, HALO), HALO)
                for c in range(2):
                    obj_out[c, rows, :] = obj_out[c, rows, :] - STEP_OBJECT * totals[c]
                return carry

            lax.fori_loop(0, blocks // 2 - 1, far, 0)

    finish(halves[0])

    @pl.when(late)
    def _():
        for c in range(2):
            for k in range(1, ring):
                @pl.when(source(k) < owners)
                def _():
                    spread_copy(c, k, source(k)).wait_recv()
                    hand_copy(c, source(k)).start()

    finish(halves[1])
    for d in range(2):
        @pl.when(row_recv[d])
        def _():
            rim_copy(d).wait_recv()
            rows = pl.ds((TR - HALO, 0)[d], HALO)
            obj_out[:, rows, :] = obj_out[:, rows, :] - STEP_OBJECT * yrecv[d]

    @pl.when(~late)
    def _():
        for c in range(2):
            for q in range(owners):
                hand_copy(c, q).wait_recv()
    prb_out[...] = pnew[...]

    for d in range(2):
        @pl.when(col_send[d])
        def _():
            cor_copy(d).wait_send()
            for s in range(S):
                patch_copy(d, s).wait_send()

        @pl.when(row_send[d])
        def _():
            halo_copy(d).wait_send()
            rim_copy(d).wait_send()
    for s in range(S):
        for h in range(2):
            chip_grad(s, h).wait_send()

            @pl.when(has_outer)
            def _():
                outer_grad(s, h).wait_send()

            @pl.when(has_relay)
            def _():
                forward_grad(s, h).wait_send()

    @pl.when(~late)
    def _():
        core_copy.wait_send()

    @pl.when(late)
    def _():
        for c in range(2):
            for k in range(1, ring):
                @pl.when(ring_at(k) < owners)
                def _():
                    share_copy(c, k).wait_send()

            @pl.when(me < owners)
            def _():
                across_copy(c).wait_send()
                for k in range(1, ring):
                    spread_copy(c, k, me).wait_send()
            for q in range(owners):
                hand_copy(c, q).wait_send()


def on_device(grp_size, pos_size, tables, object_field, probe_field, patterns, corners, counts):
    TR, S, M = object_field.shape[1], patterns.shape[0], probe_field.shape[1]
    ring = grp_size * (pos_size // 4)
    owners, h3 = shares(M, ring)
    f32 = jnp.float32
    V, D = pltpu.VMEM, pltpu.SemaphoreType.DMA
    smem = pl.BlockSpec(memory_space=pltpu.SMEM)
    hbm = pl.BlockSpec(memory_space=pl.ANY)
    vmem = pl.BlockSpec(memory_space=pltpu.VMEM)
    half = (2, HALO, HALO)
    return pl.pallas_call(
        functools.partial(kernel, (grp_size, pos_size, S, TR, M)),
        out_shape=(
            pltpu.VMEM(object_field.shape, f32),
            pltpu.VMEM(probe_field.shape, f32),
        ),
        in_specs=[smem, smem, hbm, hbm, hbm, hbm],
        out_specs=(vmem, vmem),
        scratch_shapes=[
            V((2, TR + 2 * HALO, HALO), f32),
            V((2, M, M), f32),
            V((2, S, M, HALO), f32),
            V((S, M, M), f32),
            V(tables.shape, jnp.bfloat16),
            V((2, S, 2, M, HALO), f32),
            V((2, S, 2, M, HALO), f32),
            pltpu.SMEM((2, *corners.shape), jnp.int32),
            V((S, 2, *half), f32),
            V((2, S, 2, *half), f32),
            V((2, S, 2, *half), f32),
            V((S, 2, *half), f32),
            V((2, 2, 2 * M, HALO), f32),
            V((2, *half), f32),
            V((2, *half), f32),
            V((2, M, M), f32),
            V((2, M, M), f32),
            V((2, ring, h3, M), f32),
            V((2, h3, M), f32),
            V((2, h3, M), f32),
            V((2, M, M), f32),
            D((5,)), pltpu.SemaphoreType.REGULAR((max(1, grp_size + pos_size // 4 - 3),)), D((2, 2)), D((2, 2)), D((2, 2, S)), D((2, 2, S, 2)), D((S, 2)), D((S, 2)), D((2, 2)),
            D((2,)), D((2, 2, ring)), D((2, 2, ring)), D((2, 2)), D((2, 2, owners)),
        ],
        compiler_params=pltpu.CompilerParams(
            collective_id=0, has_side_effects=True, vmem_limit_bytes=56 * 1024 * 1024
        ),
    )(corners, counts, object_field, probe_field, patterns, jnp.asarray(tables))

def solution(mesh):
    def body(object_field, probe_field, patterns, corners, counts):
        tables = dft_tables(probe_field.shape[1])
        return on_device(
            mesh.shape["grp"], mesh.shape["pos"], tables, object_field, probe_field, patterns, corners, counts
        )

    return jax.shard_map(
        body,
        mesh=mesh,
        in_specs=(
            P(None, "grp", "pos"),
            P(),
            P(("grp", "pos"), None, None),
            P(None, ("grp", "pos")),
            P(),
        ),
        out_specs=(P(None, "grp", "pos"), P()),
        check_vma=False,
    )
```

```python
import functools

import jax
import jax.numpy as jnp
import numpy as np
from jax import lax
from jax.experimental import pallas as pl
from jax.experimental.pallas import tpu as pltpu
from jax.sharding import PartitionSpec as P

HALO = 128
STEP_OBJECT = 0.25
STEP_PROBE = 4.0
MESH = pl.DeviceIdType.MESH


def dft_tables(order):
    half = order // 2
    columns = np.arange(half, dtype=np.int64)
    tables = []
    for odd in range(2):
        rows = 2 * np.arange(half, dtype=np.int64) + odd
        angles = (rows[:, None] * columns[None, :] % order) * (2.0 * np.pi / order)
        re, im = np.cos(angles) / np.sqrt(order), -np.sin(angles) / np.sqrt(order)
        block = np.block([[re, -im], [im, re]])
        tables.append(np.stack([block, block.T]))
    both = np.stack(tables).astype(np.float32)
    high = both.astype(jnp.bfloat16)
    low = (both - high.astype(np.float32)).astype(jnp.bfloat16)
    return np.stack([high, low], axis=2)


def split(x):
    high = x.astype(jnp.bfloat16)
    low = (x - high.astype(jnp.float32)).astype(jnp.bfloat16)
    return high, low


def dot(a, b):
    return jnp.dot(a, b, preferred_element_type=jnp.float32)


def table_left(tab, odd, turn, data):
    high, low = split(data)
    th, tl = tab[odd, turn, 0], tab[odd, turn, 1]
    return dot(th, high) + (dot(th, low) + dot(tl, high))


def table_right(data, tab, odd, turn):
    high, low = split(data)
    th, tl = tab[odd, turn, 0], tab[odd, turn, 1]
    return dot(high, th) + (dot(low, th) + dot(high, tl))


def rows_of(x, h):
    n = x.shape[0] // 2
    return x[h * n : (h + 1) * n]


def cols_of(x, h):
    n = x.shape[1] // 2
    return x[:, h * n : (h + 1) * n]


def stack(a, b):
    return jnp.concatenate([a, b], axis=0)


def side_by_side(a, b):
    return jnp.concatenate([a, b], axis=1)


def forward(tab, re, im):
    r0, r1, i0, i1 = rows_of(re, 0), rows_of(re, 1), rows_of(im, 0), rows_of(im, 1)
    even = table_left(tab, 0, 0, stack(r0 + r1, i0 + i1))
    odd = table_left(tab, 1, 0, stack(r0 - r1, i0 - i1))
    re, im = stack(rows_of(even, 0), rows_of(odd, 0)), stack(rows_of(even, 1), rows_of(odd, 1))
    r0, r1, i0, i1 = cols_of(re, 0), cols_of(re, 1), cols_of(im, 0), cols_of(im, 1)
    even = table_right(side_by_side(r0 + r1, i0 + i1), tab, 0, 1)
    odd = table_right(side_by_side(r0 - r1, i0 - i1), tab, 1, 1)
    return side_by_side(cols_of(even, 0), cols_of(odd, 0)), side_by_side(cols_of(even, 1), cols_of(odd, 1))


def backward(tab, re, im):
    even = table_left(tab, 0, 1, stack(rows_of(re, 0), rows_of(im, 0)))
    odd = table_left(tab, 1, 1, stack(rows_of(re, 1), rows_of(im, 1)))
    total, rest = even + odd, even - odd
    re, im = stack(rows_of(total, 0), rows_of(rest, 0)), stack(rows_of(total, 1), rows_of(rest, 1))
    even = table_right(side_by_side(cols_of(re, 0), cols_of(im, 0)), tab, 0, 0)
    odd = table_right(side_by_side(cols_of(re, 1), cols_of(im, 1)), tab, 1, 0)
    total, rest = even + odd, even - odd
    return side_by_side(cols_of(total, 0), cols_of(rest, 0)), side_by_side(cols_of(total, 1), cols_of(rest, 1))


def drain(ref, sem):
    pltpu.make_async_copy(ref, ref, sem).wait()


def shares(rows, ring):
    owners = min(ring, rows // 8)
    return owners, rows // owners


def kernel(sizes, corners, counts, obj_hbm, prb_hbm, pat_hbm, tab_hbm, obj_out, prb_out,
           ext, prb, pat, patp, tab, nb, stage, cor_smem,
           gmid, gsend, grecv, relay, turned, rim, yrecv, gp, p1r, p3r, p2, p2x, pnew,
           loc, farsem, yh, corsem, patsem, gsem, rsem, ysem, csem, asem, agsem, xsem, casem, outsem):
    G, PN, S, TR, M = sizes
    grp, pos = lax.axis_index("grp"), lax.axis_index("pos")
    core, chip, chips = lax.rem(pos, 2), pos // 2, PN // 2
    side, lines = lax.rem(chip, 2), chips // 2
    ring = G * lines
    owners, h3 = shares(M, ring)
    me = grp * lines + chip // 2
    late = side != core
    blocks = TR // HALO + 2

    def at(g, p):
        return {"device_id": (g, lax.rem(p + PN, PN)), "device_id_type": MESH}

    col_peer = [at(grp, pos - 1), at(grp, pos + 1)]
    row_peer = [at(lax.rem(grp + G - 1, G), pos), at(lax.rem(grp + 1, G), pos)]
    col_send, col_recv = [pos > 0, pos < PN - 1], [pos < PN - 1, pos > 0]
    row_send, row_recv = [grp > 0, grp < G - 1], [grp < G - 1, grp > 0]
    partner = at(grp, pos + 1 - 2 * core)
    across = at(grp, pos + 2 * core - 1)
    has_outer = ((core == 0) & (pos > 0)) | ((core == 1) & (pos < PN - 1))
    has_relay = late & (((core == 1) & (pos + 3 < PN)) | ((core == 0) & (pos >= 3)))
    relay_peer, feeder = at(grp, pos + 6 * core - 3), at(grp, pos + 2 - 4 * core)
    forward_peer = at(grp, pos + 4 * core - 2)

    def ring_at(k):
        return lax.rem(me + k, ring)

    def ring_peer(k):
        q = ring_at(k)
        return at(q // lines, (lax.rem(q, lines) * 2 + side) * 2 + core)

    locals_ = [
        pltpu.make_async_copy(obj_hbm, ext.at[:, pl.ds(HALO, TR), :], loc.at[0]),
        pltpu.make_async_copy(prb_hbm, prb, loc.at[1]),
        pltpu.make_async_copy(tab_hbm, tab, loc.at[2]),
    ] + [
        pltpu.make_async_copy(pat_hbm.at[:, :, pl.ds(w * HALO, HALO)], pat.at[w], loc.at[3])
        for w in range(2)
    ]
    for c in locals_:
        c.start()

    near_ring = [
        (late & row_send[0], row_peer[0]), (late & row_send[1], row_peer[1]),
        (late & (pos >= 4), at(grp, pos - 4)), (late & (pos + 4 < PN), at(grp, pos + 4)),
    ]
    barrier = pltpu.get_barrier_semaphore()

    def greet(condition, peers):
        @pl.when(condition)
        def _():
            for peer in peers:
                pl.semaphore_signal(barrier, inc=1, **peer)
        return condition.astype(jnp.int32) * len(peers)

    expected = greet(col_send[0], [col_peer[0]]) + greet(col_send[1], [col_peer[1]])
    expected += greet(row_send[0], [row_peer[0]]) + greet(row_send[1], [row_peer[1]])
    expected += greet(near_ring[2][0], [near_ring[2][1]]) + greet(near_ring[3][0], [near_ring[3][1]])
    expected += greet(~late & has_outer, [relay_peer, feeder]) + greet(has_relay, [relay_peer, forward_peer])

    lane = lax.broadcasted_iota(jnp.int32, (M, HALO), 1)
    gp[...] = jnp.zeros(gp.shape, jnp.float32)

    locals_[0].wait()
    pl.semaphore_wait(barrier, expected)

    def cor_copy(d):
        return pltpu.make_async_remote_copy(corners, cor_smem.at[d], corsem.at[0, d], corsem.at[1, d], **col_peer[d])

    def row_at(d, s):
        return jnp.clip(cor_smem[d, 0, s] - grp * TR + HALO, 0, TR + 2 * HALO - M)

    def halo_copy(d):
        src, dst = ((HALO, HALO + TR), (TR, 0))[d]
        return pltpu.make_async_remote_copy(
            ext.at[:, pl.ds(src, HALO), :], ext.at[:, pl.ds(dst, HALO), :], yh.at[0, d], yh.at[1, d], **row_peer[d])

    for d in range(2):
        @pl.when(col_send[d])
        def _():
            cor_copy(d).start()

        @pl.when(row_send[d])
        def _():
            halo_copy(d).start()
    for d in range(2):
        @pl.when(col_recv[d])
        def _():
            cor_copy(d).wait_recv()
    for d in range(2):
        @pl.when(row_recv[d])
        def _():
            halo_copy(d).wait_recv()

    def patch_copy(d, s):
        return pltpu.make_async_remote_copy(
            stage.at[d, s], nb.at[d, s], outsem.at[d], patsem.at[d, s], **col_peer[d])

    for s in range(S):
        for d in range(2):
            @pl.when(col_send[d])
            def _():
                r = row_at(1 - d, s)
                for c in range(2):
                    stage[d, s, c] = ext[c, pl.ds(r, M), :]
                patch_copy(d, s).start()

    for step in range(lines + G - 3):
        for there, peer in near_ring:
            @pl.when(there)
            def _():
                pl.semaphore_signal(farsem.at[step], inc=1, **peer)
        known = sum(there.astype(jnp.int32) for there, _ in near_ring)

        @pl.when(late)
        def _():
            pl.semaphore_wait(farsem.at[step], known)

    def chip_grad(s, h):
        d = 1 - core
        return pltpu.make_async_remote_copy(
            gsend.at[d, h, s], grecv.at[d, h, s], outsem.at[2 + d], gsem.at[d, 0], **partner)

    def outer_grad(s, h):
        return pltpu.make_async_remote_copy(
            gsend.at[core, h, s], grecv.at[core, h, s], outsem.at[2 + core], gsem.at[core, h], **across)

    def relay_grad(s, h):
        return pltpu.make_async_remote_copy(
            gsend.at[core, h, s], relay.at[h, s], outsem.at[2 + core], rsem.at[h], **relay_peer)

    def forward_grad(s, h):
        return pltpu.make_async_remote_copy(
            relay.at[h, s], grecv.at[1 - core, h, s], outsem.at[4], gsem.at[1 - core, h], **forward_peer)

    first_half = (grp < G - 1).astype(jnp.int32)
    halves = [first_half, 1 - first_half]

    for c in locals_[1:3]:
        c.wait()
    drain(pat, loc.at[3])
    own_count = counts[grp * PN + pos]

    column = lax.broadcasted_iota(jnp.int32, (M, M), 1)
    wanted = jnp.where(column < M // 2, 2 * column, 2 * column - (M - 1))
    pick = (lax.broadcasted_iota(jnp.int32, (M, M), 0) == wanted).astype(jnp.float32).astype(jnp.bfloat16)

    def reorder(s, carry):
        rows = side_by_side(*[
            stack(*[pat[w, s, pl.ds(odd, M // 2, stride=2), :] for odd in range(2)]) for w in range(2)
        ])
        high, low = split(rows)
        last = (rows - high.astype(jnp.float32) - low.astype(jnp.float32)).astype(jnp.bfloat16)
        patp[s] = dot(high, pick) + (dot(low, pick) + dot(last, pick))
        return carry

    lax.fori_loop(0, S, reorder, 0)

    def row_of(s):
        return jnp.clip(corners[0, s] - grp * TR + HALO, 0, TR + 2 * HALO - M)

    def slot(s, carry):
        r = row_of(s)
        shift = jnp.clip(corners[1, s] - pos * HALO + HALO, 0, HALO)
        for d in range(2):
            @pl.when(col_recv[d])
            def _():
                patch_copy(d, s).wait_recv()
        back = lax.rem(HALO - shift, HALO)
        forth = lax.rem(shift, HALO)
        first = lane < HALO - shift
        patch = []
        for c in range(2):
            mid = pltpu.roll(ext[c, pl.ds(r, M), :], back, 1)
            before = pltpu.roll(nb[1, s, c], back, 1)
            after = pltpu.roll(nb[0, s, c], back, 1)
            patch.append(side_by_side(jnp.where(first, before, mid), jnp.where(first, mid, after)))
        pr, pi = prb[0], prb[1]
        fr, fi = forward(tab, pr * patch[0] - pi * patch[1], pr * patch[1] + pi * patch[0])
        excess = fr * fr + fi * fi - patp[s]
        excess = jnp.where(jnp.full((M, M), s, jnp.int32) < own_count, excess, 0.0)
        cr, ci = backward(tab, excess * fr, excess * fi)
        parts = (pr * cr + pi * ci, pr * ci - pi * cr)
        gp[0] += patch[0] * cr + patch[1] * ci
        gp[1] += patch[0] * ci - patch[1] * cr
        tail = lane >= shift
        for c in range(2):
            for w in range(2):
                turned[c, w, :M] = cols_of(parts[c], w)
                turned[c, w, M:] = cols_of(parts[c], w)
        start = M - lax.rem(r, M)
        for c in range(2):
            g0, g1 = [pltpu.roll(turned[c, w, pl.ds(start, M), :], forth, 1) for w in range(2)]
            left, middle, right = jnp.where(tail, g0, 0.0), jnp.where(tail, g1, g0), jnp.where(tail, 0.0, g1)
            for h in range(2):
                gsend[0, h, s, c] = rows_of(left, h)
                gmid[s, h, c] = rows_of(middle, h)
                gsend[1, h, s, c] = rows_of(right, h)
        for h in range(2):
            chip_grad(s, h).start()

        @pl.when(has_outer & late)
        def _():
            outer_grad(s, halves[0]).start()

        @pl.when(has_outer & ~late)
        def _():
            relay_grad(s, halves[0]).start()
        return carry

    lax.fori_loop(0, S, slot, 0)

    core_copy = pltpu.make_async_remote_copy(gp, p1r, csem.at[0], csem.at[1], **partner)

    def share_rows(q):
        return pl.ds(pl.multiple_of(lax.rem(q, owners) * h3, 8), h3)

    def share_copy(c, k):
        return pltpu.make_async_remote_copy(
            gp.at[c, share_rows(ring_at(k)), :], p3r.at[c, k - 1], outsem.at[5], asem.at[c], **ring_peer(k))

    def across_copy(c):
        return pltpu.make_async_remote_copy(p2.at[c], p2x.at[c], xsem.at[0, c], xsem.at[1, c], **across)

    def spread_copy(c, k, owner):
        rows = share_rows(owner)
        return pltpu.make_async_remote_copy(
            pnew.at[c, rows, :], pnew.at[c, rows, :], outsem.at[6], agsem.at[c, k - 1], **ring_peer(k))

    def hand_copy(c, owner):
        rows = share_rows(owner)
        return pltpu.make_async_remote_copy(
            pnew.at[c, rows, :], pnew.at[c, rows, :], outsem.at[7], casem.at[0], **partner)

    def source(k):
        return lax.rem(me + ring - k, ring)

    def pass_on(h):
        @pl.when(has_relay)
        def _():
            drain(relay.at[h], rsem.at[h])
            for s in range(S):
                forward_grad(s, h).start()

    def covers(block, r):
        rows = lax.broadcasted_iota(jnp.int32, (HALO, HALO), 0) + (block * HALO - r)
        return (rows >= 0) & (rows < M)

    def own(totals, block, h):
        for s in range(S):
            inside = covers(block, row_of(s))
            totals = [t + jnp.where(inside, gmid[s, h, c], 0.0) for c, t in enumerate(totals)]
        return totals

    def others(totals, block, h, d):
        for s in range(S):
            inside = covers(block, row_at(d, s))
            totals = [t + jnp.where(inside, grecv[d, h, s, c], 0.0) for c, t in enumerate(totals)]
        return totals

    zeros = [jnp.zeros((HALO, HALO), jnp.float32)] * 2

    def near(block, carry):
        h = lax.rem(block, 2)
        totals = others(own(zeros, block, h), block, h, core)
        rows = pl.ds(pl.multiple_of(block * HALO, HALO), HALO)
        for c in range(2):
            obj_out[c, pl.ds(pl.multiple_of(block * HALO - HALO, HALO), HALO), :] = (
                ext[c, rows, :] - STEP_OBJECT * totals[c])
        return carry

    def near_all():
        drain(grecv.at[core], gsem.at[core, 0])
        lax.fori_loop(1, blocks - 1, near, 0)

    def second(first, last):
        @pl.when(has_outer)
        def _():
            for s in range(first, last):
                outer_grad(s, halves[1]).start()

    @pl.when(~late)
    def _():
        core_copy.start()

        @pl.when(has_outer)
        def _():
            for s in range(S):
                relay_grad(s, halves[1]).start()
        near_all()

    @pl.when(late)
    def _():
        core_copy.wait_recv()
        gp[...] += p1r[...]
        for c in range(2):
            for k in range(1, ring):
                @pl.when(ring_at(k) < owners)
                def _():
                    share_copy(c, k).start()

        pass_on(halves[0])
        near_all()
        for c in range(2):
            @pl.when(me < owners)
            def _():
                total = gp[c, share_rows(me), :]
                drain(p3r.at[c], asem.at[c])
                for k in range(ring - 1):
                    total = total + p3r[c, k]
                p2[c] = total
                across_copy(c).start()

            second(*((0, 1), (1, S))[c])

        pass_on(halves[1])
        live = counts[0]
        for i in range(1, G * PN):
            live = live + counts[i]

        @pl.when(me < owners)
        def _():
            for c in range(2):
                across_copy(c).wait_recv()
                total = p2[c] + p2x[c]
                divisor = jnp.full(total.shape, live, jnp.int32).astype(jnp.float32)
                pnew[c, share_rows(me), :] = prb[c, share_rows(me), :] - STEP_PROBE * total / divisor
                for k in range(1, ring):
                    spread_copy(c, k, me).start()
                hand_copy(c, me).start()

    def rim_copy(d):
        return pltpu.make_async_remote_copy(rim.at[d], yrecv.at[d], ysem.at[0, d], ysem.at[1, d], **row_peer[d])

    def finish(h):
        @pl.when(has_outer)
        def _():
            drain(grecv.at[1 - core, h], gsem.at[1 - core, h])
        for d in range(2):
            block = d * (blocks - 1)

            @pl.when(row_send[d] & (h == d))
            def _():
                totals = others(own(zeros, block, d), block, d, core)
                for c in range(2):
                    rim[d, c] = totals[c]

                @pl.when(has_outer)
                def _():
                    more = others([rim[d, c] for c in range(2)], block, d, 1 - core)
                    for c in range(2):
                        rim[d, c] = more[c]
                rim_copy(d).start()

        @pl.when(has_outer)
        def _():
            def far(i, carry):
                block = 2 * i + 2 - h
                totals = others(zeros, block, h, 1 - core)
                rows = pl.ds(pl.multiple_of(block * HALO - HALO, HALO), HALO)
                for c in range(2):
                    obj_out[c, rows, :] = obj_out[c, rows, :] - STEP_OBJECT * totals[c]
                return carry

            lax.fori_loop(0, blocks // 2 - 1, far, 0)

    finish(halves[0])

    @pl.when(late)
    def _():
        for c in range(2):
            for k in range(1, ring):
                @pl.when(source(k) < owners)
                def _():
                    spread_copy(c, k, source(k)).wait_recv()
                    hand_copy(c, source(k)).start()

    finish(halves[1])
    for d in range(2):
        @pl.when(row_recv[d])
        def _():
            rim_copy(d).wait_recv()
            rows = pl.ds((TR - HALO, 0)[d], HALO)
            obj_out[:, rows, :] = obj_out[:, rows, :] - STEP_OBJECT * yrecv[d]

    @pl.when(~late)
    def _():
        drain(pnew, casem.at[0])
    prb_out[...] = pnew[...]

    for d in range(2):
        @pl.when(col_send[d])
        def _():
            cor_copy(d).wait_send()
            drain(stage.at[d], outsem.at[d])

        @pl.when(row_send[d])
        def _():
            halo_copy(d).wait_send()
            rim_copy(d).wait_send()
    drain(gsend.at[1 - core], outsem.at[3 - core])

    @pl.when(has_outer)
    def _():
        drain(gsend.at[core], outsem.at[2 + core])

    @pl.when(has_relay)
    def _():
        drain(relay, outsem.at[4])

    @pl.when(~late)
    def _():
        core_copy.wait_send()

    @pl.when(late)
    def _():
        if ring == owners:
            drain(p3r, outsem.at[5])
            drain(p3r, outsem.at[6])
        else:
            for c in range(2):
                for k in range(1, ring):
                    @pl.when(ring_at(k) < owners)
                    def _():
                        share_copy(c, k).wait_send()

                @pl.when(me < owners)
                def _():
                    for k in range(1, ring):
                        spread_copy(c, k, me).wait_send()

        @pl.when(me < owners)
        def _():
            for c in range(2):
                across_copy(c).wait_send()
        drain(pnew, outsem.at[7])


def store(obj, prb, obj_out, prb_out, sems):
    copies = [pltpu.make_async_copy(obj.at[c], obj_out.at[c], sems.at[c]) for c in range(2)]
    copies.append(pltpu.make_async_copy(prb, prb_out, sems.at[2]))
    for c in copies:
        c.start()
    for c in copies:
        c.wait()


def on_device(grp_size, pos_size, tables, object_field, probe_field, patterns, corners, counts):
    TR, S, M = object_field.shape[1], patterns.shape[0], probe_field.shape[1]
    ring = grp_size * (pos_size // 4)
    owners, h3 = shares(M, ring)
    f32 = jnp.float32
    V, D = pltpu.VMEM, pltpu.SemaphoreType.DMA
    smem = pl.BlockSpec(memory_space=pltpu.SMEM)
    hbm = pl.BlockSpec(memory_space=pl.ANY)
    vmem = pl.BlockSpec(memory_space=pltpu.VMEM)
    half = (2, HALO, HALO)
    object_new, probe_new = pl.pallas_call(
        functools.partial(kernel, (grp_size, pos_size, S, TR, M)),
        out_shape=(
            pltpu.VMEM(object_field.shape, f32),
            pltpu.VMEM(probe_field.shape, f32),
        ),
        in_specs=[smem, smem, hbm, hbm, hbm, hbm],
        out_specs=(vmem, vmem),
        scratch_shapes=[
            V((2, TR + 2 * HALO, HALO), f32),
            V((2, M, M), f32),
            V((2, S, M, HALO), f32),
            V((S, M, M), f32),
            V(tables.shape, jnp.bfloat16),
            V((2, S, 2, M, HALO), f32),
            V((2, S, 2, M, HALO), f32),
            pltpu.SMEM((2, *corners.shape), jnp.int32),
            V((S, 2, *half), f32),
            V((2, 2, S, *half), f32),
            V((2, 2, S, *half), f32),
            V((2, S, *half), f32),
            V((2, 2, 2 * M, HALO), f32),
            V((2, *half), f32),
            V((2, *half), f32),
            V((2, M, M), f32),
            V((2, M, M), f32),
            V((2, ring - 1, h3, M), f32),
            V((2, h3, M), f32),
            V((2, h3, M), f32),
            V((2, M, M), f32),
            D((4,)), pltpu.SemaphoreType.REGULAR((max(1, grp_size + pos_size // 4 - 3),)), D((2, 2)), D((2, 2)), D((2, S)),
            D((2, 2)), D((2,)), D((2, 2)), D((2,)), D((2,)), D((2, ring - 1)), D((2, 2)), D((1,)), D((8,)),
        ],
        compiler_params=pltpu.CompilerParams(
            collective_id=0, has_side_effects=True, vmem_limit_bytes=56 * 1024 * 1024
        ),
    )(corners, counts, object_field, probe_field, patterns, jnp.asarray(tables))
    object_new = pltpu.with_memory_space_constraint(object_new, pltpu.VMEM)
    probe_new = pltpu.with_memory_space_constraint(probe_new, pltpu.VMEM)
    return pl.pallas_call(
        store,
        out_shape=(
            jax.ShapeDtypeStruct(object_field.shape, f32),
            jax.ShapeDtypeStruct(probe_field.shape, f32),
        ),
        in_specs=[hbm, hbm],
        out_specs=(hbm, hbm),
        scratch_shapes=[D((3,))],
        compiler_params=pltpu.CompilerParams(vmem_limit_bytes=1024 * 1024),
    )(object_new, probe_new)

def solution(mesh):
    def body(object_field, probe_field, patterns, corners, counts):
        tables = dft_tables(probe_field.shape[1])
        return on_device(
            mesh.shape["grp"], mesh.shape["pos"], tables, object_field, probe_field, patterns, corners, counts
        )

    return jax.shard_map(
        body,
        mesh=mesh,
        in_specs=(
            P(None, "grp", "pos"),
            P(),
            P(("grp", "pos"), None, None),
            P(None, ("grp", "pos")),
            P(),
        ),
        out_specs=(P(None, "grp", "pos"), P()),
        check_vma=False,
    )
```

```python
import functools

import jax
import jax.numpy as jnp
import numpy as np
from jax import lax
from jax.experimental import pallas as pl
from jax.experimental.pallas import tpu as pltpu
from jax.sharding import PartitionSpec as P

HALO = 128
STEP_OBJECT = 0.25
STEP_PROBE = 4.0
MESH = pl.DeviceIdType.MESH


def dft_tables(order):
    half = order // 2
    columns = np.arange(half, dtype=np.int64)
    tables = []
    for odd in range(2):
        rows = 2 * np.arange(half, dtype=np.int64) + odd
        angles = (rows[:, None] * columns[None, :] % order) * (2.0 * np.pi / order)
        re, im = np.cos(angles) / np.sqrt(order), -np.sin(angles) / np.sqrt(order)
        block = np.block([[re, -im], [im, re]])
        tables.append(np.stack([block, block.T]))
    both = np.stack(tables).astype(np.float32)
    high = both.astype(jnp.bfloat16)
    low = (both - high.astype(np.float32)).astype(jnp.bfloat16)
    return np.stack([high, low], axis=2)


def split(x):
    high = x.astype(jnp.bfloat16)
    low = (x - high.astype(jnp.float32)).astype(jnp.bfloat16)
    return high, low


def dot(a, b):
    return jnp.dot(a, b, preferred_element_type=jnp.float32)


def table_left(tab, odd, turn, data):
    high, low = split(data)
    th, tl = tab[odd, turn, 0], tab[odd, turn, 1]
    return dot(th, high) + (dot(th, low) + dot(tl, high))


def table_right(data, tab, odd, turn):
    high, low = split(data)
    th, tl = tab[odd, turn, 0], tab[odd, turn, 1]
    return dot(high, th) + (dot(low, th) + dot(high, tl))


def rows_of(x, h):
    n = x.shape[0] // 2
    return x[h * n : (h + 1) * n]


def cols_of(x, h):
    n = x.shape[1] // 2
    return x[:, h * n : (h + 1) * n]


def stack(a, b):
    return jnp.concatenate([a, b], axis=0)


def side_by_side(a, b):
    return jnp.concatenate([a, b], axis=1)


def forward(tab, re, im):
    r0, r1, i0, i1 = rows_of(re, 0), rows_of(re, 1), rows_of(im, 0), rows_of(im, 1)
    even = table_left(tab, 0, 0, stack(r0 + r1, i0 + i1))
    odd = table_left(tab, 1, 0, stack(r0 - r1, i0 - i1))
    re, im = stack(rows_of(even, 0), rows_of(odd, 0)), stack(rows_of(even, 1), rows_of(odd, 1))
    r0, r1, i0, i1 = cols_of(re, 0), cols_of(re, 1), cols_of(im, 0), cols_of(im, 1)
    even = table_right(side_by_side(r0 + r1, i0 + i1), tab, 0, 1)
    odd = table_right(side_by_side(r0 - r1, i0 - i1), tab, 1, 1)
    return side_by_side(cols_of(even, 0), cols_of(odd, 0)), side_by_side(cols_of(even, 1), cols_of(odd, 1))


def backward(tab, re, im):
    even = table_left(tab, 0, 1, stack(rows_of(re, 0), rows_of(im, 0)))
    odd = table_left(tab, 1, 1, stack(rows_of(re, 1), rows_of(im, 1)))
    total, rest = even + odd, even - odd
    re, im = stack(rows_of(total, 0), rows_of(rest, 0)), stack(rows_of(total, 1), rows_of(rest, 1))
    even = table_right(side_by_side(cols_of(re, 0), cols_of(im, 0)), tab, 0, 0)
    odd = table_right(side_by_side(cols_of(re, 1), cols_of(im, 1)), tab, 1, 0)
    total, rest = even + odd, even - odd
    return side_by_side(cols_of(total, 0), cols_of(rest, 0)), side_by_side(cols_of(total, 1), cols_of(rest, 1))


def drain(ref, sem):
    pltpu.make_async_copy(ref, ref, sem).wait()


def shares(rows, ring):
    owners = min(ring, rows // 8)
    return owners, rows // owners


def kernel(sizes, cor_hbm, cnt_hbm, obj_hbm, prb_hbm, pat_hbm, tab_hbm, obj_out, prb_out,
           corners, counts, ext, body, prb, prb2, pat, patp, tab, nb, stage, cor_smem,
           gmid, gsend, grecv, relay, turned, rim, yrecv, gp, p1r, p3r, p2, p2x, pnew,
           loc, farsem, yh, corsem, patsem, gsem, rsem, ysem, csem, asem, agsem, xsem, casem, outsem):
    G, PN, S, TR, M = sizes
    grp, pos = lax.axis_index("grp"), lax.axis_index("pos")
    core, chip, chips = lax.rem(pos, 2), pos // 2, PN // 2
    side, lines = lax.rem(chip, 2), chips // 2
    ring = G * lines
    owners, h3 = shares(M, ring)
    me = grp * lines + chip // 2
    late = side != core
    blocks = TR // HALO + 2

    def at(g, p):
        return {"device_id": (g, lax.rem(p + PN, PN)), "device_id_type": MESH}

    col_peer = [at(grp, pos - 1), at(grp, pos + 1)]
    row_peer = [at(lax.rem(grp + G - 1, G), pos), at(lax.rem(grp + 1, G), pos)]
    col_send, col_recv = [pos > 0, pos < PN - 1], [pos < PN - 1, pos > 0]
    row_send, row_recv = [grp > 0, grp < G - 1], [grp < G - 1, grp > 0]
    partner = at(grp, pos + 1 - 2 * core)
    across = at(grp, pos + 2 * core - 1)
    has_outer = ((core == 0) & (pos > 0)) | ((core == 1) & (pos < PN - 1))
    has_relay = late & (((core == 1) & (pos + 3 < PN)) | ((core == 0) & (pos >= 3)))
    relay_peer, feeder = at(grp, pos + 6 * core - 3), at(grp, pos + 2 - 4 * core)
    forward_peer = at(grp, pos + 4 * core - 2)

    def ring_at(k):
        return lax.rem(me + k, ring)

    def ring_peer(k):
        q = ring_at(k)
        return at(q // lines, (lax.rem(q, lines) * 2 + side) * 2 + core)

    locals_ = [
        pltpu.make_async_copy(cor_hbm, corners, loc.at[0]),
        pltpu.make_async_copy(obj_hbm, body, loc.at[1]),
        pltpu.make_async_copy(obj_hbm, ext.at[:, pl.ds(HALO, TR), :], loc.at[2]),
        pltpu.make_async_copy(cnt_hbm, counts, loc.at[3]),
        pltpu.make_async_copy(prb_hbm, prb, loc.at[4]),
        pltpu.make_async_copy(tab_hbm, tab, loc.at[5]),
    ]
    for w in range(2):
        columns = pl.ds(w * HALO, HALO)
        locals_.append(pltpu.make_async_copy(pat_hbm.at[:, :, columns], pat.at[w], loc.at[6]))
        for turn in range(2):
            locals_.append(pltpu.make_async_copy(
                prb_hbm.at[:, :, columns], prb2.at[:, w, pl.ds(turn * M, M), :], loc.at[7]))

    near_ring = [
        (late & row_send[0], row_peer[0]), (late & row_send[1], row_peer[1]),
        (late & (pos >= 4), at(grp, pos - 4)), (late & (pos + 4 < PN), at(grp, pos + 4)),
    ]
    barrier = pltpu.get_barrier_semaphore()

    def greet(condition, peers):
        @pl.when(condition)
        def _():
            for peer in peers:
                pl.semaphore_signal(barrier, inc=1, **peer)
        return condition.astype(jnp.int32) * len(peers)

    expected = greet(col_send[0], [col_peer[0]]) + greet(col_send[1], [col_peer[1]])
    expected += greet(row_send[0], [row_peer[0]]) + greet(row_send[1], [row_peer[1]])
    expected += greet(near_ring[2][0], [near_ring[2][1]]) + greet(near_ring[3][0], [near_ring[3][1]])
    expected += greet(~late & has_outer, [relay_peer, feeder]) + greet(has_relay, [relay_peer, forward_peer])

    for c in locals_:
        c.start()
    lane = lax.broadcasted_iota(jnp.int32, (M, HALO), 1)
    gp[...] = jnp.zeros(gp.shape, jnp.float32)

    for c in locals_[:3]:
        c.wait()
    pl.semaphore_wait(barrier, expected)

    def cor_copy(d):
        return pltpu.make_async_remote_copy(corners, cor_smem.at[d], corsem.at[0, d], corsem.at[1, d], **col_peer[d])

    def row_at(d, s):
        return jnp.clip(cor_smem[d, 0, s] - grp * TR + HALO, 0, TR + 2 * HALO - M)

    def halo_copy(d):
        src, dst = ((HALO, HALO + TR), (TR, 0))[d]
        return pltpu.make_async_remote_copy(
            ext.at[:, pl.ds(src, HALO), :], ext.at[:, pl.ds(dst, HALO), :], yh.at[0, d], yh.at[1, d], **row_peer[d])

    for d in range(2):
        @pl.when(col_send[d])
        def _():
            cor_copy(d).start()

        @pl.when(row_send[d])
        def _():
            halo_copy(d).start()
    for d in range(2):
        @pl.when(col_recv[d])
        def _():
            cor_copy(d).wait_recv()
    first_half = (grp < G - 1).astype(jnp.int32)
    halves = [first_half, 1 - first_half]

    def patch_copy(d, s, h):
        return pltpu.make_async_remote_copy(
            stage.at[d, s, h], nb.at[d, s, h], outsem.at[d], patsem.at[d, s], **col_peer[d])

    def wrapped(source, inset, c, r, h):
        after = r + HALO * (1 - h)
        base = after - lax.rem(after, 2 * HALO) + HALO * h
        last = source.shape[1] - HALO
        low, high = [
            source[c, pl.ds(jnp.clip(at_row - inset * HALO, 0, last), HALO), :]
            for at_row in (base, base + 2 * HALO)
        ]
        rows = lax.broadcasted_iota(jnp.int32, (HALO, HALO), 0) + base
        return jnp.where(rows >= r, low, high)

    def send_patch(s, which):
        h = halves[which]
        for d in range(2):
            @pl.when(col_send[d])
            def _():
                r = row_at(1 - d, s)
                for c in range(2):
                    stage[d, s, h, c] = wrapped((ext, body)[which], which, c, r, h)
                patch_copy(d, s, h).start()

    for s in range(min(2, S)):
        send_patch(s, 1)
    for d in range(2):
        @pl.when(row_recv[d])
        def _():
            halo_copy(d).wait_recv()
    for s in range(S):
        if s >= 2:
            send_patch(s, 1)
        send_patch(s, 0)

    for step in range(lines + G - 3):
        for there, peer in near_ring:
            @pl.when(there)
            def _():
                pl.semaphore_signal(farsem.at[step], inc=1, **peer)
        known = sum(there.astype(jnp.int32) for there, _ in near_ring)

        @pl.when(late)
        def _():
            pl.semaphore_wait(farsem.at[step], known)

    def chip_grad(s, h):
        d = 1 - core
        return pltpu.make_async_remote_copy(
            gsend.at[d, h, s], grecv.at[d, h, s], outsem.at[2 + d], gsem.at[d, 0], **partner)

    def outer_grad(s, h):
        return pltpu.make_async_remote_copy(
            gsend.at[core, h, s], grecv.at[core, h, s], outsem.at[2 + core], gsem.at[core, h], **across)

    def relay_grad(s, h):
        return pltpu.make_async_remote_copy(
            gsend.at[core, h, s], relay.at[h, s], outsem.at[2 + core], rsem.at[h], **relay_peer)

    def forward_grad(s, h):
        return pltpu.make_async_remote_copy(
            relay.at[h, s], grecv.at[1 - core, h, s], outsem.at[4], gsem.at[1 - core, h], **forward_peer)

    for c in locals_[3:6]:
        c.wait()
    drain(pat, loc.at[6])
    drain(prb2, loc.at[7])
    own_count = counts[grp * PN + pos]

    column = lax.broadcasted_iota(jnp.int32, (M, M), 1)
    wanted = jnp.where(column < M // 2, 2 * column, 2 * column - (M - 1))
    pick = (lax.broadcasted_iota(jnp.int32, (M, M), 0) == wanted).astype(jnp.float32).astype(jnp.bfloat16)

    def reorder(s, carry):
        rows = side_by_side(*[
            stack(*[pat[w, s, pl.ds(odd, M // 2, stride=2), :] for odd in range(2)]) for w in range(2)
        ])
        high, low = split(rows)
        last = (rows - high.astype(jnp.float32) - low.astype(jnp.float32)).astype(jnp.bfloat16)
        patp[s] = dot(high, pick) + (dot(low, pick) + dot(last, pick))
        return carry

    lax.fori_loop(0, S, reorder, 0)

    def row_of(s):
        return jnp.clip(corners[0, s] - grp * TR + HALO, 0, TR + 2 * HALO - M)

    def slot(s, carry):
        r = row_of(s)
        shift = jnp.clip(corners[1, s] - pos * HALO + HALO, 0, HALO)
        for d in range(2):
            @pl.when(col_recv[d])
            def _():
                drain(nb.at[d, s], patsem.at[d, s])
        back = lax.rem(HALO - shift, HALO)
        forth = lax.rem(shift, HALO)
        first = lane < HALO - shift
        patch = []
        for c in range(2):
            mid, before, after = [
                pltpu.roll(stack(*pair), back, 1)
                for pair in (
                    [wrapped(ext, 0, c, r, h) for h in range(2)],
                    [nb[1, s, h, c] for h in range(2)],
                    [nb[0, s, h, c] for h in range(2)],
                )
            ]
            patch.append(side_by_side(jnp.where(first, before, mid), jnp.where(first, mid, after)))
        turn = lax.rem(r, M)
        pr, pi = [side_by_side(*[prb2[c, w, pl.ds(M - turn, M), :] for w in range(2)]) for c in range(2)]
        fr, fi = forward(tab, pr * patch[0] - pi * patch[1], pr * patch[1] + pi * patch[0])
        excess = fr * fr + fi * fi - patp[s]
        excess = jnp.where(jnp.full((M, M), s, jnp.int32) < own_count, excess, 0.0)
        cr, ci = backward(tab, excess * fr, excess * fi)
        parts = (pr * cr + pi * ci, pr * ci - pi * cr)
        for c, part in enumerate((patch[0] * cr + patch[1] * ci, patch[0] * ci - patch[1] * cr)):
            for w in range(2):
                turned[c, w, :M] = cols_of(part, w)
                turned[c, w, M:] = cols_of(part, w)
                gp[c, :, w * HALO : (w + 1) * HALO] += turned[c, w, pl.ds(turn, M), :]
        tail = lane >= shift
        for c in range(2):
            g0, g1 = [pltpu.roll(cols_of(parts[c], w), forth, 1) for w in range(2)]
            left, middle, right = jnp.where(tail, g0, 0.0), jnp.where(tail, g1, g0), jnp.where(tail, 0.0, g1)
            for h in range(2):
                gsend[0, h, s, c] = rows_of(left, h)
                gmid[s, h, c] = rows_of(middle, h)
                gsend[1, h, s, c] = rows_of(right, h)
        for h in range(2):
            chip_grad(s, h).start()

        @pl.when(has_outer & late)
        def _():
            outer_grad(s, halves[0]).start()

        @pl.when(has_outer & ~late)
        def _():
            relay_grad(s, halves[0]).start()
        return carry

    lax.fori_loop(0, S, slot, 0)

    core_copy = pltpu.make_async_remote_copy(gp, p1r, csem.at[0], csem.at[1], **partner)

    def share_rows(q):
        return pl.ds(pl.multiple_of(lax.rem(q, owners) * h3, 8), h3)

    def share_copy(c, k):
        return pltpu.make_async_remote_copy(
            gp.at[c, share_rows(ring_at(k)), :], p3r.at[c, k - 1], outsem.at[5], asem.at[c], **ring_peer(k))

    def across_copy(c):
        return pltpu.make_async_remote_copy(p2.at[c], p2x.at[c], xsem.at[0, c], xsem.at[1, c], **across)

    def spread_copy(c, k, owner):
        rows = share_rows(owner)
        return pltpu.make_async_remote_copy(
            pnew.at[c, rows, :], pnew.at[c, rows, :], outsem.at[6], agsem.at[c, k - 1], **ring_peer(k))

    def hand_copy(c, owner):
        rows = share_rows(owner)
        return pltpu.make_async_remote_copy(
            pnew.at[c, rows, :], pnew.at[c, rows, :], outsem.at[7], casem.at[0], **partner)

    def source(k):
        return lax.rem(me + ring - k, ring)

    def pass_on(h):
        @pl.when(has_relay)
        def _():
            drain(relay.at[h], rsem.at[h])
            for s in range(S):
                forward_grad(s, h).start()

    def covers(block, r):
        rows = lax.broadcasted_iota(jnp.int32, (HALO, HALO), 0) + (block * HALO - r)
        return (rows >= 0) & (rows < M)

    def own(totals, block, h):
        for s in range(S):
            inside = covers(block, row_of(s))
            totals = [t + jnp.where(inside, gmid[s, h, c], 0.0) for c, t in enumerate(totals)]
        return totals

    def others(totals, block, h, d):
        for s in range(S):
            inside = covers(block, row_at(d, s))
            totals = [t + jnp.where(inside, grecv[d, h, s, c], 0.0) for c, t in enumerate(totals)]
        return totals

    zeros = [jnp.zeros((HALO, HALO), jnp.float32)] * 2

    def near(block, carry):
        h = lax.rem(block, 2)
        totals = others(own(zeros, block, h), block, h, core)
        rows = pl.ds(pl.multiple_of(block * HALO, HALO), HALO)
        for c in range(2):
            obj_out[c, pl.ds(pl.multiple_of(block * HALO - HALO, HALO), HALO), :] = (
                ext[c, rows, :] - STEP_OBJECT * totals[c])
        return carry

    def near_all():
        drain(grecv.at[core], gsem.at[core, 0])
        lax.fori_loop(1, blocks - 1, near, 0)

    def second(first, last):
        @pl.when(has_outer)
        def _():
            for s in range(first, last):
                outer_grad(s, halves[1]).start()

    @pl.when(~late)
    def _():
        core_copy.start()

        @pl.when(has_outer)
        def _():
            for s in range(S):
                relay_grad(s, halves[1]).start()
        near_all()

    @pl.when(late)
    def _():
        core_copy.wait_recv()
        gp[...] += p1r[...]
        for c in range(2):
            for k in range(1, ring):
                @pl.when(ring_at(k) < owners)
                def _():
                    share_copy(c, k).start()

        pass_on(halves[0])
        near_all()
        for c in range(2):
            @pl.when(me < owners)
            def _():
                total = gp[c, share_rows(me), :]
                drain(p3r.at[c], asem.at[c])
                for k in range(ring - 1):
                    total = total + p3r[c, k]
                p2[c] = total
                across_copy(c).start()

            second(*((0, 1), (1, S))[c])

        pass_on(halves[1])
        live = counts[0]
        for i in range(1, G * PN):
            live = live + counts[i]

        @pl.when(me < owners)
        def _():
            for c in range(2):
                across_copy(c).wait_recv()
                total = p2[c] + p2x[c]
                divisor = jnp.full(total.shape, live, jnp.int32).astype(jnp.float32)
                pnew[c, share_rows(me), :] = prb[c, share_rows(me), :] - STEP_PROBE * total / divisor
                for k in range(1, ring):
                    spread_copy(c, k, me).start()
                hand_copy(c, me).start()

    def rim_copy(d):
        return pltpu.make_async_remote_copy(rim.at[d], yrecv.at[d], ysem.at[0, d], ysem.at[1, d], **row_peer[d])

    def finish(h):
        @pl.when(has_outer)
        def _():
            drain(grecv.at[1 - core, h], gsem.at[1 - core, h])
        for d in range(2):
            block = d * (blocks - 1)

            @pl.when(row_send[d] & (h == d))
            def _():
                totals = others(own(zeros, block, d), block, d, core)
                for c in range(2):
                    rim[d, c] = totals[c]

                @pl.when(has_outer)
                def _():
                    more = others([rim[d, c] for c in range(2)], block, d, 1 - core)
                    for c in range(2):
                        rim[d, c] = more[c]
                rim_copy(d).start()

        @pl.when(has_outer)
        def _():
            def far(i, carry):
                block = 2 * i + 2 - h
                totals = others(zeros, block, h, 1 - core)
                rows = pl.ds(pl.multiple_of(block * HALO - HALO, HALO), HALO)
                for c in range(2):
                    obj_out[c, rows, :] = obj_out[c, rows, :] - STEP_OBJECT * totals[c]
                return carry

            lax.fori_loop(0, blocks // 2 - 1, far, 0)

    finish(halves[0])

    @pl.when(late)
    def _():
        for c in range(2):
            for k in range(1, ring):
                @pl.when(source(k) < owners)
                def _():
                    spread_copy(c, k, source(k)).wait_recv()
                    hand_copy(c, source(k)).start()

    finish(halves[1])
    for d in range(2):
        @pl.when(row_recv[d])
        def _():
            rim_copy(d).wait_recv()
            rows = pl.ds((TR - HALO, 0)[d], HALO)
            obj_out[:, rows, :] = obj_out[:, rows, :] - STEP_OBJECT * yrecv[d]

    @pl.when(~late)
    def _():
        drain(pnew, casem.at[0])
    prb_out[...] = pnew[...]

    for d in range(2):
        @pl.when(col_send[d])
        def _():
            cor_copy(d).wait_send()
            drain(stage.at[d], outsem.at[d])

        @pl.when(row_send[d])
        def _():
            halo_copy(d).wait_send()
            rim_copy(d).wait_send()
    drain(gsend.at[1 - core], outsem.at[3 - core])

    @pl.when(has_outer)
    def _():
        drain(gsend.at[core], outsem.at[2 + core])

    @pl.when(has_relay)
    def _():
        drain(relay, outsem.at[4])

    @pl.when(~late)
    def _():
        core_copy.wait_send()

    @pl.when(late)
    def _():
        if ring == owners:
            drain(p3r, outsem.at[5])
            drain(p3r, outsem.at[6])
        else:
            for c in range(2):
                for k in range(1, ring):
                    @pl.when(ring_at(k) < owners)
                    def _():
                        share_copy(c, k).wait_send()

                @pl.when(me < owners)
                def _():
                    for k in range(1, ring):
                        spread_copy(c, k, me).wait_send()

        @pl.when(me < owners)
        def _():
            for c in range(2):
                across_copy(c).wait_send()
        drain(pnew, outsem.at[7])


def store(obj, prb, obj_out, prb_out, sems):
    copies = [pltpu.make_async_copy(obj.at[c], obj_out.at[c], sems.at[c]) for c in range(2)]
    copies.append(pltpu.make_async_copy(prb, prb_out, sems.at[2]))
    for c in copies:
        c.start()
    for c in copies:
        c.wait()


def on_device(grp_size, pos_size, tables, object_field, probe_field, patterns, corners, counts):
    TR, S, M = object_field.shape[1], patterns.shape[0], probe_field.shape[1]
    ring = grp_size * (pos_size // 4)
    owners, h3 = shares(M, ring)
    f32 = jnp.float32
    V, D = pltpu.VMEM, pltpu.SemaphoreType.DMA
    hbm = pl.BlockSpec(memory_space=pl.ANY)
    vmem = pl.BlockSpec(memory_space=pltpu.VMEM)
    half = (2, HALO, HALO)
    object_new, probe_new = pl.pallas_call(
        functools.partial(kernel, (grp_size, pos_size, S, TR, M)),
        out_shape=(
            pltpu.VMEM(object_field.shape, f32),
            pltpu.VMEM(probe_field.shape, f32),
        ),
        in_specs=[hbm] * 6,
        out_specs=(vmem, vmem),
        scratch_shapes=[
            pltpu.SMEM(corners.shape, jnp.int32),
            pltpu.SMEM(counts.shape, jnp.int32),
            V((2, TR + 2 * HALO, HALO), f32),
            V((2, TR, HALO), f32),
            V((2, M, M), f32),
            V((2, 2, 2 * M, HALO), f32),
            V((2, S, M, HALO), f32),
            V((S, M, M), f32),
            V(tables.shape, jnp.bfloat16),
            V((2, S, 2, *half), f32),
            V((2, S, 2, *half), f32),
            pltpu.SMEM((2, *corners.shape), jnp.int32),
            V((S, 2, *half), f32),
            V((2, 2, S, *half), f32),
            V((2, 2, S, *half), f32),
            V((2, S, *half), f32),
            V((2, 2, 2 * M, HALO), f32),
            V((2, *half), f32),
            V((2, *half), f32),
            V((2, M, M), f32),
            V((2, M, M), f32),
            V((2, ring - 1, h3, M), f32),
            V((2, h3, M), f32),
            V((2, h3, M), f32),
            V((2, M, M), f32),
            D((8,)), pltpu.SemaphoreType.REGULAR((max(1, grp_size + pos_size // 4 - 3),)), D((2, 2)), D((2, 2)), D((2, S)),
            D((2, 2)), D((2,)), D((2, 2)), D((2,)), D((2,)), D((2, ring - 1)), D((2, 2)), D((1,)), D((8,)),
        ],
        compiler_params=pltpu.CompilerParams(
            collective_id=0, has_side_effects=True, vmem_limit_bytes=56 * 1024 * 1024
        ),
    )(corners, counts, object_field, probe_field, patterns, jnp.asarray(tables))
    object_new = pltpu.with_memory_space_constraint(object_new, pltpu.VMEM)
    probe_new = pltpu.with_memory_space_constraint(probe_new, pltpu.VMEM)
    return pl.pallas_call(
        store,
        out_shape=(
            jax.ShapeDtypeStruct(object_field.shape, f32),
            jax.ShapeDtypeStruct(probe_field.shape, f32),
        ),
        in_specs=[hbm, hbm],
        out_specs=(hbm, hbm),
        scratch_shapes=[D((3,))],
        compiler_params=pltpu.CompilerParams(vmem_limit_bytes=1024 * 1024),
    )(object_new, probe_new)

def solution(mesh):
    def body(object_field, probe_field, patterns, corners, counts):
        tables = dft_tables(probe_field.shape[1])
        return on_device(
            mesh.shape["grp"], mesh.shape["pos"], tables, object_field, probe_field, patterns, corners, counts
        )

    return jax.shard_map(
        body,
        mesh=mesh,
        in_specs=(
            P(None, "grp", "pos"),
            P(),
            P(("grp", "pos"), None, None),
            P(None, ("grp", "pos")),
            P(),
        ),
        out_specs=(P(None, "grp", "pos"), P()),
        check_vma=False,
    )
```

```python
import functools

import jax
import jax.numpy as jnp
import numpy as np
from jax import lax
from jax.experimental import pallas as pl
from jax.experimental.pallas import tpu as pltpu
from jax.sharding import PartitionSpec as P

HALO = 128
STEP_OBJECT = 0.25
STEP_PROBE = 4.0
PIECES = 1
MESH = pl.DeviceIdType.MESH


def dft_tables(order):
    half = order // 2
    columns = np.arange(half, dtype=np.int64)
    tables = []
    for odd in range(2):
        rows = 2 * np.arange(half, dtype=np.int64) + odd
        angles = (rows[:, None] * columns[None, :] % order) * (2.0 * np.pi / order)
        re, im = np.cos(angles) / np.sqrt(order), -np.sin(angles) / np.sqrt(order)
        block = np.block([[re, -im], [im, re]])
        tables.append(np.stack([block, block.T]))
    both = np.stack(tables).astype(np.float32)
    high = both.astype(jnp.bfloat16)
    low = (both - high.astype(np.float32)).astype(jnp.bfloat16)
    return np.stack([high, low], axis=2)


def split(x):
    high = x.astype(jnp.bfloat16)
    low = (x - high.astype(jnp.float32)).astype(jnp.bfloat16)
    return high, low


def dot(a, b):
    return jnp.dot(a, b, preferred_element_type=jnp.float32)


def table_left(tab, odd, turn, data):
    high, low = split(data)
    th, tl = tab[odd, turn, 0], tab[odd, turn, 1]
    return dot(th, high) + (dot(th, low) + dot(tl, high))


def table_right(data, tab, odd, turn):
    high, low = split(data)
    th, tl = tab[odd, turn, 0], tab[odd, turn, 1]
    return dot(high, th) + (dot(low, th) + dot(high, tl))


def rows_of(x, h):
    n = x.shape[0] // 2
    return x[h * n : (h + 1) * n]


def cols_of(x, h):
    n = x.shape[1] // 2
    return x[:, h * n : (h + 1) * n]


def stack(a, b):
    return jnp.concatenate([a, b], axis=0)


def side_by_side(a, b):
    return jnp.concatenate([a, b], axis=1)


def forward(tab, re, im):
    r0, r1, i0, i1 = rows_of(re, 0), rows_of(re, 1), rows_of(im, 0), rows_of(im, 1)
    even = table_left(tab, 0, 0, stack(r0 + r1, i0 + i1))
    odd = table_left(tab, 1, 0, stack(r0 - r1, i0 - i1))
    re, im = stack(rows_of(even, 0), rows_of(odd, 0)), stack(rows_of(even, 1), rows_of(odd, 1))
    r0, r1, i0, i1 = cols_of(re, 0), cols_of(re, 1), cols_of(im, 0), cols_of(im, 1)
    even = table_right(side_by_side(r0 + r1, i0 + i1), tab, 0, 1)
    odd = table_right(side_by_side(r0 - r1, i0 - i1), tab, 1, 1)
    return side_by_side(cols_of(even, 0), cols_of(odd, 0)), side_by_side(cols_of(even, 1), cols_of(odd, 1))


def backward(tab, re, im):
    even = table_left(tab, 0, 1, stack(rows_of(re, 0), rows_of(im, 0)))
    odd = table_left(tab, 1, 1, stack(rows_of(re, 1), rows_of(im, 1)))
    total, rest = even + odd, even - odd
    re, im = stack(rows_of(total, 0), rows_of(rest, 0)), stack(rows_of(total, 1), rows_of(rest, 1))
    even = table_right(side_by_side(cols_of(re, 0), cols_of(im, 0)), tab, 0, 0)
    odd = table_right(side_by_side(cols_of(re, 1), cols_of(im, 1)), tab, 1, 0)
    total, rest = even + odd, even - odd
    return side_by_side(cols_of(total, 0), cols_of(rest, 0)), side_by_side(cols_of(total, 1), cols_of(rest, 1))


def drain(ref, sem):
    pltpu.make_async_copy(ref, ref, sem).wait()


def shares(rows, ring):
    owners = min(ring, rows // 8)
    return owners, rows // owners


def kernel(sizes, cor_hbm, cnt_hbm, obj_hbm, prb_hbm, pat_hbm, tab_hbm, obj_out, prb_out,
           corners, counts, ext, body, prb, prb2, pat, patp, tab, nb, stage, cor_smem,
           gmid, gsend, grecv, relay, turned, rim, yrecv, gp, p1r, p3r, p2, p2x,
           loc, farsem, yh, corsem, patsem, gsem, rsem, ysem, csem, asem, agsem, xsem, casem, outsem):
    G, PN, S, TR, M = sizes
    grp, pos = lax.axis_index("grp"), lax.axis_index("pos")
    core, chip, chips = lax.rem(pos, 2), pos // 2, PN // 2
    side, lines = lax.rem(chip, 2), chips // 2
    ring = G * lines
    owners, h3 = shares(M, ring)
    me = grp * lines + chip // 2
    late = side != core
    blocks = TR // HALO + 2
    split_ring = ring == owners and G == 2

    def at(g, p):
        return {"device_id": (g, lax.rem(p + PN, PN)), "device_id_type": MESH}

    col_peer = [at(grp, pos - 1), at(grp, pos + 1)]
    row_peer = [at(lax.rem(grp + G - 1, G), pos), at(lax.rem(grp + 1, G), pos)]
    col_send, col_recv = [pos > 0, pos < PN - 1], [pos < PN - 1, pos > 0]
    row_send, row_recv = [grp > 0, grp < G - 1], [grp < G - 1, grp > 0]
    partner = at(grp, pos + 1 - 2 * core)
    across = at(grp, pos + 2 * core - 1)
    has_outer = ((core == 0) & (pos > 0)) | ((core == 1) & (pos < PN - 1))
    has_relay = late & (((core == 1) & (pos + 3 < PN)) | ((core == 0) & (pos >= 3)))
    relay_peer, feeder = at(grp, pos + 6 * core - 3), at(grp, pos + 2 - 4 * core)
    forward_peer = at(grp, pos + 4 * core - 2)

    def ring_at(k):
        return lax.rem(me + k, ring)

    def ring_peer(k):
        q = ring_at(k)
        return at(q // lines, (lax.rem(q, lines) * 2 + side) * 2 + core)

    locals_ = [
        pltpu.make_async_copy(cor_hbm, corners, loc.at[0]),
        pltpu.make_async_copy(obj_hbm, body, loc.at[1]),
        pltpu.make_async_copy(obj_hbm, ext.at[:, pl.ds(HALO, TR), :], loc.at[2]),
        pltpu.make_async_copy(cnt_hbm, counts, loc.at[3]),
        pltpu.make_async_copy(prb_hbm, prb, loc.at[4]),
        pltpu.make_async_copy(tab_hbm, tab, loc.at[5]),
    ]
    for w in range(2):
        columns = pl.ds(w * HALO, HALO)
        locals_.append(pltpu.make_async_copy(pat_hbm.at[:, :, columns], pat.at[w], loc.at[6]))
        for turn in range(2):
            locals_.append(pltpu.make_async_copy(
                prb_hbm.at[:, :, columns], prb2.at[:, w, pl.ds(turn * M, M), :], loc.at[7]))

    locals_[0].start()
    near_ring = [
        (late & row_send[0], row_peer[0]), (late & row_send[1], row_peer[1]),
        (late & (pos >= 4), at(grp, pos - 4)), (late & (pos + 4 < PN), at(grp, pos + 4)),
    ]
    barrier = pltpu.get_barrier_semaphore()

    def greet(condition, peers):
        @pl.when(condition)
        def _():
            for peer in peers:
                pl.semaphore_signal(barrier, inc=1, **peer)
        return condition.astype(jnp.int32) * len(peers)

    expected = greet(col_send[0], [col_peer[0]]) + greet(col_send[1], [col_peer[1]])
    expected += greet(row_send[0], [row_peer[0]]) + greet(row_send[1], [row_peer[1]])
    expected += greet(near_ring[2][0], [near_ring[2][1]]) + greet(near_ring[3][0], [near_ring[3][1]])
    expected += greet(~late & has_outer, [relay_peer, feeder]) + greet(has_relay, [relay_peer, forward_peer])

    for c in locals_[1:3]:
        c.start()
    lane = lax.broadcasted_iota(jnp.int32, (M, HALO), 1)
    gp[...] = jnp.zeros(gp.shape, jnp.float32)

    locals_[0].wait()
    pl.semaphore_wait(barrier, expected)

    def cor_copy(d):
        return pltpu.make_async_remote_copy(corners, cor_smem.at[d], corsem.at[0, d], corsem.at[1, d], **col_peer[d])

    def row_at(d, s):
        return jnp.clip(cor_smem[d, 0, s] - grp * TR + HALO, 0, TR + 2 * HALO - M)

    def halo_copy(d):
        src, dst = ((HALO, HALO + TR), (TR, 0))[d]
        return pltpu.make_async_remote_copy(
            ext.at[:, pl.ds(src, HALO), :], ext.at[:, pl.ds(dst, HALO), :], yh.at[0, d], yh.at[1, d], **row_peer[d])

    for d in range(2):
        @pl.when(col_send[d])
        def _():
            cor_copy(d).start()
    for c in locals_[1:3]:
        c.wait()
    for c in locals_[3:]:
        c.start()
    for d in range(2):
        @pl.when(row_send[d])
        def _():
            halo_copy(d).start()
    for d in range(2):
        @pl.when(col_recv[d])
        def _():
            cor_copy(d).wait_recv()
    first_half = (grp < G - 1).astype(jnp.int32)
    halves = [first_half, 1 - first_half]

    def patch_copy(d, s, h):
        return pltpu.make_async_remote_copy(
            stage.at[d, s, h], nb.at[d, s, h], outsem.at[d], patsem.at[d, s], **col_peer[d])

    def wrapped(source, inset, c, r, h):
        after = r + HALO * (1 - h)
        base = after - lax.rem(after, 2 * HALO) + HALO * h
        last = source.shape[1] - HALO
        low, high = [
            source[c, pl.ds(jnp.clip(at_row - inset * HALO, 0, last), HALO), :]
            for at_row in (base, base + 2 * HALO)
        ]
        rows = lax.broadcasted_iota(jnp.int32, (HALO, HALO), 0) + base
        return jnp.where(rows >= r, low, high)

    def send_patch(s, which):
        h = halves[which]
        for d in range(2):
            @pl.when(col_send[d])
            def _():
                r = row_at(1 - d, s)
                for c in range(2):
                    stage[d, s, h, c] = wrapped((ext, body)[which], which, c, r, h)
                patch_copy(d, s, h).start()

    for s in range(min(2, S)):
        send_patch(s, 1)
    for d in range(2):
        @pl.when(row_recv[d])
        def _():
            halo_copy(d).wait_recv()
    for s in range(S):
        if s >= 2:
            send_patch(s, 1)
        send_patch(s, 0)

    for step in range(lines + G - 3):
        for there, peer in near_ring:
            @pl.when(there)
            def _():
                pl.semaphore_signal(farsem.at[step], inc=1, **peer)
        known = sum(there.astype(jnp.int32) for there, _ in near_ring)

        @pl.when(late)
        def _():
            pl.semaphore_wait(farsem.at[step], known)

    def chip_grad(s, h):
        d = 1 - core
        return pltpu.make_async_remote_copy(
            gsend.at[d, h, s], grecv.at[d, h, s], outsem.at[2 + d], gsem.at[d, 0], **partner)

    def outer_grad(s, h):
        return pltpu.make_async_remote_copy(
            gsend.at[core, h, s], grecv.at[core, h, s], outsem.at[2 + core], gsem.at[core, h], **across)

    def relay_grad(s, h):
        return pltpu.make_async_remote_copy(
            gsend.at[core, h, s], relay.at[h, s], outsem.at[2 + core], rsem.at[h], **relay_peer)

    def forward_grad(s, h):
        return pltpu.make_async_remote_copy(
            relay.at[h, s], grecv.at[1 - core, h, s], outsem.at[4], gsem.at[1 - core, h], **forward_peer)

    for c in locals_[3:6]:
        c.wait()
    drain(pat, loc.at[6])
    drain(prb2, loc.at[7])
    own_count = counts[grp * PN + pos]

    column = lax.broadcasted_iota(jnp.int32, (M, M), 1)
    wanted = jnp.where(column < M // 2, 2 * column, 2 * column - (M - 1))
    pick = (lax.broadcasted_iota(jnp.int32, (M, M), 0) == wanted).astype(jnp.float32).astype(jnp.bfloat16)

    def reorder(s, carry):
        rows = side_by_side(*[
            stack(*[pat[w, s, pl.ds(odd, M // 2, stride=2), :] for odd in range(2)]) for w in range(2)
        ])
        high, low = split(rows)
        last = (rows - high.astype(jnp.float32) - low.astype(jnp.float32)).astype(jnp.bfloat16)
        patp[s] = dot(high, pick) + (dot(low, pick) + dot(last, pick))
        return carry

    lax.fori_loop(0, S, reorder, 0)

    def row_of(s):
        return jnp.clip(corners[0, s] - grp * TR + HALO, 0, TR + 2 * HALO - M)

    def slot(s, carry):
        r = row_of(s)
        shift = jnp.clip(corners[1, s] - pos * HALO + HALO, 0, HALO)
        for d in range(2):
            @pl.when(col_recv[d])
            def _():
                drain(nb.at[d, s], patsem.at[d, s])
        back = lax.rem(HALO - shift, HALO)
        forth = lax.rem(shift, HALO)
        first = lane < HALO - shift
        patch = []
        for c in range(2):
            mid, before, after = [
                pltpu.roll(stack(*pair), back, 1)
                for pair in (
                    [wrapped(ext, 0, c, r, h) for h in range(2)],
                    [nb[1, s, h, c] for h in range(2)],
                    [nb[0, s, h, c] for h in range(2)],
                )
            ]
            patch.append(side_by_side(jnp.where(first, before, mid), jnp.where(first, mid, after)))
        turn = lax.rem(r, M)
        pr, pi = [side_by_side(*[prb2[c, w, pl.ds(M - turn, M), :] for w in range(2)]) for c in range(2)]
        fr, fi = forward(tab, pr * patch[0] - pi * patch[1], pr * patch[1] + pi * patch[0])
        excess = fr * fr + fi * fi - patp[s]
        excess = jnp.where(jnp.full((M, M), s, jnp.int32) < own_count, excess, 0.0)
        cr, ci = backward(tab, excess * fr, excess * fi)
        parts = (pr * cr + pi * ci, pr * ci - pi * cr)
        for c, part in enumerate((patch[0] * cr + patch[1] * ci, patch[0] * ci - patch[1] * cr)):
            for w in range(2):
                turned[c, w, :M] = cols_of(part, w)
                turned[c, w, M:] = cols_of(part, w)
                gp[c, :, w * HALO : (w + 1) * HALO] += turned[c, w, pl.ds(turn, M), :]
        tail = lane >= shift
        for c in range(2):
            g0, g1 = [pltpu.roll(cols_of(parts[c], w), forth, 1) for w in range(2)]
            left, middle, right = jnp.where(tail, g0, 0.0), jnp.where(tail, g1, g0), jnp.where(tail, 0.0, g1)
            for h in range(2):
                gsend[0, h, s, c] = rows_of(left, h)
                gmid[s, h, c] = rows_of(middle, h)
                gsend[1, h, s, c] = rows_of(right, h)
        for h in range(2):
            chip_grad(s, h).start()

        @pl.when(has_outer & late)
        def _():
            outer_grad(s, halves[0]).start()

        @pl.when(has_outer & ~late)
        def _():
            relay_grad(s, halves[0]).start()
        return carry

    lax.fori_loop(0, S, slot, 0)

    core_copy = pltpu.make_async_remote_copy(gp, p1r, csem.at[0], csem.at[1], **partner)

    def share_rows(q):
        return pl.ds(pl.multiple_of(lax.rem(q, owners) * h3, 8), h3)

    def share_copy(c, k):
        return pltpu.make_async_remote_copy(
            gp.at[c, share_rows(ring_at(k)), :], p3r.at[c, k - 1], outsem.at[5], asem.at[c], **ring_peer(k))

    line = chip // 2

    def line_at(k):
        return lax.rem(line + k + lines, lines)

    def line_peer(k):
        return at(grp, (line_at(k) * 2 + side) * 2 + core)

    def group_at(j):
        return lax.rem(grp + j + G, G)

    def line_spread(c, k, owner):
        rows = share_rows(owner)
        return pltpu.make_async_remote_copy(
            prb_out.at[c, rows, :], prb_out.at[c, rows, :], outsem.at[6 + c], agsem.at[c, k - 1], **line_peer(k))

    def group_spread(c, j, k, owner):
        rows = share_rows(owner)
        return pltpu.make_async_remote_copy(
            prb_out.at[c, rows, :], prb_out.at[c, rows, :], outsem.at[8 + c], agsem.at[c, lines - 1 + (j - 1) * lines + k],
            **at(group_at(j), pos))

    def across_copy(c):
        return pltpu.make_async_remote_copy(p2.at[c], p2x.at[c], xsem.at[0, c], xsem.at[1, c], **across)

    def spread_copy(c, k, owner):
        rows = share_rows(owner)
        return pltpu.make_async_remote_copy(
            prb_out.at[c, rows, :], prb_out.at[c, rows, :], outsem.at[6], agsem.at[c, k - 1], **ring_peer(k))

    def hand_copy(c, owner):
        rows = share_rows(owner)
        return pltpu.make_async_remote_copy(
            prb_out.at[c, rows, :], prb_out.at[c, rows, :], outsem.at[10], casem.at[0], **partner)

    def source(k):
        return lax.rem(me + ring - k, ring)

    def pass_on(h):
        @pl.when(has_relay)
        def _():
            drain(relay.at[h], rsem.at[h])
            for s in range(S):
                forward_grad(s, h).start()

    def covers(block, r):
        rows = lax.broadcasted_iota(jnp.int32, (HALO, HALO), 0) + (block * HALO - r)
        return (rows >= 0) & (rows < M)

    def own(totals, block, h):
        for s in range(S):
            inside = covers(block, row_of(s))
            totals = [t + jnp.where(inside, gmid[s, h, c], 0.0) for c, t in enumerate(totals)]
        return totals

    def others(totals, block, h, d):
        for s in range(S):
            inside = covers(block, row_at(d, s))
            totals = [t + jnp.where(inside, grecv[d, h, s, c], 0.0) for c, t in enumerate(totals)]
        return totals

    zeros = [jnp.zeros((HALO, HALO), jnp.float32)] * 2

    def near(block, carry):
        h = lax.rem(block, 2)
        totals = others(own(zeros, block, h), block, h, core)
        rows = pl.ds(pl.multiple_of(block * HALO, HALO), HALO)
        for c in range(2):
            obj_out[c, pl.ds(pl.multiple_of(block * HALO - HALO, HALO), HALO), :] = (
                ext[c, rows, :] - STEP_OBJECT * totals[c])
        return carry

    def near_all():
        drain(grecv.at[core], gsem.at[core, 0])
        lax.fori_loop(1, blocks - 1, near, 0)

    def second(first, last):
        @pl.when(has_outer)
        def _():
            for s in range(first, last):
                outer_grad(s, halves[1]).start()

    @pl.when(~late)
    def _():
        core_copy.start()

        @pl.when(has_outer)
        def _():
            for s in range(S):
                relay_grad(s, halves[1]).start()
        near_all()

    @pl.when(late)
    def _():
        core_copy.wait_recv()
        gp[...] += p1r[...]
        for c in range(2):
            for k in range(1, ring):
                @pl.when(ring_at(k) < owners)
                def _():
                    share_copy(c, k).start()
        pass_on(halves[0])
        near_all()
        for c in range(2):
            @pl.when(me < owners)
            def _():
                total = gp[c, share_rows(me), :]
                drain(p3r.at[c], asem.at[c])
                for k in range(ring - 1):
                    total = total + p3r[c, k]
                p2[c] = total
                across_copy(c).start()

            second(*((0, 1), (1, S))[c])

        pass_on(halves[1])
        live = counts[0]
        for i in range(1, G * PN):
            live = live + counts[i]

        @pl.when(me < owners)
        def _():
            for c in range(2):
                across_copy(c).wait_recv()
                total = p2[c] + p2x[c]
                divisor = jnp.full(total.shape, live, jnp.int32).astype(jnp.float32)
                prb_out[c, share_rows(me), :] = prb[c, share_rows(me), :] - STEP_PROBE * total / divisor
                if split_ring:
                    for k in range(1, lines):
                        line_spread(c, k, me).start()
                    group_spread(c, 1, 0, me).start()
                else:
                    for k in range(1, ring):
                        spread_copy(c, k, me).start()
                hand_copy(c, me).start()

    def rim_copy(d):
        return pltpu.make_async_remote_copy(rim.at[d], yrecv.at[d], ysem.at[0, d], ysem.at[1, d], **row_peer[d])

    def finish(h):
        @pl.when(has_outer)
        def _():
            drain(grecv.at[1 - core, h], gsem.at[1 - core, h])
        for d in range(2):
            block = d * (blocks - 1)

            @pl.when(row_send[d] & (h == d))
            def _():
                totals = others(own(zeros, block, d), block, d, core)
                for c in range(2):
                    rim[d, c] = totals[c]

                @pl.when(has_outer)
                def _():
                    more = others([rim[d, c] for c in range(2)], block, d, 1 - core)
                    for c in range(2):
                        rim[d, c] = more[c]
                rim_copy(d).start()

        @pl.when(has_outer)
        def _():
            def far(i, carry):
                block = 2 * i + 2 - h
                totals = others(zeros, block, h, 1 - core)
                rows = pl.ds(pl.multiple_of(block * HALO - HALO, HALO), HALO)
                for c in range(2):
                    obj_out[c, rows, :] = obj_out[c, rows, :] - STEP_OBJECT * totals[c]
                return carry

            lax.fori_loop(0, blocks // 2 - 1, far, 0)

    finish(halves[0])
    finish(halves[1])

    @pl.when(late)
    def _():
        if split_ring:
            for c in range(2):
                for k in range(1, lines):
                    owner = grp * lines + line_at(-k)
                    line_spread(c, k, owner).wait_recv()
                    group_spread(c, 1, k, owner).start()
                    hand_copy(c, owner).start()
            for c in range(2):
                for k in range(lines):
                    owner = group_at(1) * lines + line_at(-k)
                    group_spread(c, 1, k, owner).wait_recv()
                    hand_copy(c, owner).start()
        else:
            for c in range(2):
                for k in range(1, ring):
                    @pl.when(source(k) < owners)
                    def _():
                        spread_copy(c, k, source(k)).wait_recv()
                        hand_copy(c, source(k)).start()

    for d in range(2):
        @pl.when(row_recv[d])
        def _():
            rim_copy(d).wait_recv()
            rows = pl.ds((TR - HALO, 0)[d], HALO)
            obj_out[:, rows, :] = obj_out[:, rows, :] - STEP_OBJECT * yrecv[d]

    @pl.when(~late)
    def _():
        drain(prb_out, casem.at[0])

    for d in range(2):
        @pl.when(col_send[d])
        def _():
            cor_copy(d).wait_send()
            drain(stage.at[d], outsem.at[d])

        @pl.when(row_send[d])
        def _():
            halo_copy(d).wait_send()
            rim_copy(d).wait_send()
    drain(gsend.at[1 - core], outsem.at[3 - core])

    @pl.when(has_outer)
    def _():
        drain(gsend.at[core], outsem.at[2 + core])

    @pl.when(has_relay)
    def _():
        drain(relay, outsem.at[4])

    @pl.when(~late)
    def _():
        core_copy.wait_send()

    @pl.when(late)
    def _():
        if split_ring:
            drain(p3r, outsem.at[5])
            for c in range(2):
                drain(prb_out.at[c, pl.ds(0, (lines - 1) * h3), :], outsem.at[6 + c])
                drain(prb_out.at[c, pl.ds(0, (G - 1) * lines * h3), :], outsem.at[8 + c])
        else:
            for c in range(2):
                for k in range(1, ring):
                    @pl.when(ring_at(k) < owners)
                    def _():
                        share_copy(c, k).wait_send()

                @pl.when(me < owners)
                def _():
                    for k in range(1, ring):
                        spread_copy(c, k, me).wait_send()

        @pl.when(me < owners)
        def _():
            for c in range(2):
                across_copy(c).wait_send()
        drain(prb_out, outsem.at[10])


def store(obj, prb, obj_out, prb_out, sems):
    pairs = []
    for whole, out in ((obj, obj_out), (prb, prb_out)):
        rows = whole.shape[1] // PIECES
        pairs += [(whole.at[:, pl.ds(i * rows, rows), :], out.at[:, pl.ds(i * rows, rows), :]) for i in range(PIECES)]
    copies = [pltpu.make_async_copy(*pair, sems.at[i]) for i, pair in enumerate(pairs)]
    for c in copies:
        c.start()
    for c in copies:
        c.wait()


def on_device(grp_size, pos_size, tables, object_field, probe_field, patterns, corners, counts):
    TR, S, M = object_field.shape[1], patterns.shape[0], probe_field.shape[1]
    ring = grp_size * (pos_size // 4)
    owners, h3 = shares(M, ring)
    f32 = jnp.float32
    V, D = pltpu.VMEM, pltpu.SemaphoreType.DMA
    hbm = pl.BlockSpec(memory_space=pl.ANY)
    vmem = pl.BlockSpec(memory_space=pltpu.VMEM)
    half = (2, HALO, HALO)
    object_new, probe_new = pl.pallas_call(
        functools.partial(kernel, (grp_size, pos_size, S, TR, M)),
        out_shape=(
            pltpu.VMEM(object_field.shape, f32),
            pltpu.VMEM(probe_field.shape, f32),
        ),
        in_specs=[hbm] * 6,
        out_specs=(vmem, vmem),
        scratch_shapes=[
            pltpu.SMEM(corners.shape, jnp.int32),
            pltpu.SMEM(counts.shape, jnp.int32),
            V((2, TR + 2 * HALO, HALO), f32),
            V((2, TR, HALO), f32),
            V((2, M, M), f32),
            V((2, 2, 2 * M, HALO), f32),
            V((2, S, M, HALO), f32),
            V((S, M, M), f32),
            V(tables.shape, jnp.bfloat16),
            V((2, S, 2, *half), f32),
            V((2, S, 2, *half), f32),
            pltpu.SMEM((2, *corners.shape), jnp.int32),
            V((S, 2, *half), f32),
            V((2, 2, S, *half), f32),
            V((2, 2, S, *half), f32),
            V((2, S, *half), f32),
            V((2, 2, 2 * M, HALO), f32),
            V((2, *half), f32),
            V((2, *half), f32),
            V((2, M, M), f32),
            V((2, M, M), f32),
            V((2, ring - 1, h3, M), f32),
            V((2, h3, M), f32),
            V((2, h3, M), f32),
            D((8,)), pltpu.SemaphoreType.REGULAR((max(1, grp_size + pos_size // 4 - 3),)), D((2, 2)), D((2, 2)), D((2, S)),
            D((2, 2)), D((2,)), D((2, 2)), D((2,)), D((2,)), D((2, ring - 1)), D((2, 2)), D((1,)), D((11,)),
        ],
        compiler_params=pltpu.CompilerParams(
            collective_id=0, has_side_effects=True, vmem_limit_bytes=56 * 1024 * 1024
        ),
    )(corners, counts, object_field, probe_field, patterns, jnp.asarray(tables))
    object_new = pltpu.with_memory_space_constraint(object_new, pltpu.VMEM)
    probe_new = pltpu.with_memory_space_constraint(probe_new, pltpu.VMEM)
    return pl.pallas_call(
        store,
        out_shape=(
            jax.ShapeDtypeStruct(object_field.shape, f32),
            jax.ShapeDtypeStruct(probe_field.shape, f32),
        ),
        in_specs=[hbm, hbm],
        out_specs=(hbm, hbm),
        scratch_shapes=[D((2 * PIECES,))],
        compiler_params=pltpu.CompilerParams(vmem_limit_bytes=1024 * 1024),
    )(object_new, probe_new)

def solution(mesh):
    def body(object_field, probe_field, patterns, corners, counts):
        tables = dft_tables(probe_field.shape[1])
        return on_device(
            mesh.shape["grp"], mesh.shape["pos"], tables, object_field, probe_field, patterns, corners, counts
        )

    return jax.shard_map(
        body,
        mesh=mesh,
        in_specs=(
            P(None, "grp", "pos"),
            P(),
            P(("grp", "pos"), None, None),
            P(None, ("grp", "pos")),
            P(),
        ),
        out_specs=(P(None, "grp", "pos"), P()),
        check_vma=False,
    )
```

```python
import functools

import jax
import jax.numpy as jnp
import numpy as np
from jax import lax
from jax.experimental import pallas as pl
from jax.experimental.pallas import tpu as pltpu
from jax.sharding import PartitionSpec as P

HALO = 128
STEP_OBJECT = 0.25
STEP_PROBE = 4.0
PIECES = 1
MESH = pl.DeviceIdType.MESH


def dft_tables(order):
    half = order // 2
    columns = np.arange(half, dtype=np.int64)
    tables = []
    for odd in range(2):
        rows = 2 * np.arange(half, dtype=np.int64) + odd
        angles = (rows[:, None] * columns[None, :] % order) * (2.0 * np.pi / order)
        re, im = np.cos(angles) / np.sqrt(order), -np.sin(angles) / np.sqrt(order)
        block = np.block([[re, -im], [im, re]])
        tables.append(np.stack([block, block.T]))
    both = np.stack(tables).astype(np.float32)
    high = both.astype(jnp.bfloat16)
    low = (both - high.astype(np.float32)).astype(jnp.bfloat16)
    return np.stack([high, low], axis=2)


def split(x):
    high = x.astype(jnp.bfloat16)
    low = (x - high.astype(jnp.float32)).astype(jnp.bfloat16)
    return high, low


def dot(a, b):
    return jnp.dot(a, b, preferred_element_type=jnp.float32)


def table_left(tab, odd, turn, data):
    high, low = split(data)
    th, tl = tab[odd, turn, 0], tab[odd, turn, 1]
    return dot(th, high) + (dot(th, low) + dot(tl, high))


def table_right(data, tab, odd, turn):
    high, low = split(data)
    th, tl = tab[odd, turn, 0], tab[odd, turn, 1]
    return dot(high, th) + (dot(low, th) + dot(high, tl))


def rows_of(x, h):
    n = x.shape[0] // 2
    return x[h * n : (h + 1) * n]


def cols_of(x, h):
    n = x.shape[1] // 2
    return x[:, h * n : (h + 1) * n]


def stack(a, b):
    return jnp.concatenate([a, b], axis=0)


def side_by_side(a, b):
    return jnp.concatenate([a, b], axis=1)


def forward(tab, re, im):
    r0, r1, i0, i1 = rows_of(re, 0), rows_of(re, 1), rows_of(im, 0), rows_of(im, 1)
    even = table_left(tab, 0, 0, stack(r0 + r1, i0 + i1))
    odd = table_left(tab, 1, 0, stack(r0 - r1, i0 - i1))
    re, im = stack(rows_of(even, 0), rows_of(odd, 0)), stack(rows_of(even, 1), rows_of(odd, 1))
    r0, r1, i0, i1 = cols_of(re, 0), cols_of(re, 1), cols_of(im, 0), cols_of(im, 1)
    even = table_right(side_by_side(r0 + r1, i0 + i1), tab, 0, 1)
    odd = table_right(side_by_side(r0 - r1, i0 - i1), tab, 1, 1)
    return side_by_side(cols_of(even, 0), cols_of(odd, 0)), side_by_side(cols_of(even, 1), cols_of(odd, 1))


def backward(tab, re, im):
    even = table_left(tab, 0, 1, stack(rows_of(re, 0), rows_of(im, 0)))
    odd = table_left(tab, 1, 1, stack(rows_of(re, 1), rows_of(im, 1)))
    total, rest = even + odd, even - odd
    re, im = stack(rows_of(total, 0), rows_of(rest, 0)), stack(rows_of(total, 1), rows_of(rest, 1))
    even = table_right(side_by_side(cols_of(re, 0), cols_of(im, 0)), tab, 0, 0)
    odd = table_right(side_by_side(cols_of(re, 1), cols_of(im, 1)), tab, 1, 0)
    total, rest = even + odd, even - odd
    return side_by_side(cols_of(total, 0), cols_of(rest, 0)), side_by_side(cols_of(total, 1), cols_of(rest, 1))


def drain(ref, sem):
    pltpu.make_async_copy(ref, ref, sem).wait()


def shares(rows, ring):
    owners = min(ring, rows // 8)
    return owners, rows // owners


def kernel(sizes, cor_hbm, cnt_hbm, obj_hbm, prb_hbm, pat_hbm, tab_hbm, obj_out, prb_out,
           corners, counts, ext, body, prb, prb2, pat, patp, tab, nb, stage, cor_smem,
           gmid, gsend, grecv, relay, turned, rim, yrecv, gp, p1r, p3r, p2, p2x,
           loc, farsem, yh, corsem, patsem, gsem, rsem, ysem, csem, asem, agsem, xsem, casem, outsem):
    G, PN, S, TR, M = sizes
    grp, pos = lax.axis_index("grp"), lax.axis_index("pos")
    core, chip, chips = lax.rem(pos, 2), pos // 2, PN // 2
    side, lines = lax.rem(chip, 2), chips // 2
    ring = G * lines
    owners, h3 = shares(M, ring)
    me = grp * lines + chip // 2
    late = side != core
    blocks = TR // HALO + 2
    split_ring = ring == owners and G == 2

    def at(g, p):
        return {"device_id": (g, lax.rem(p + PN, PN)), "device_id_type": MESH}

    col_peer = [at(grp, pos - 1), at(grp, pos + 1)]
    row_peer = [at(lax.rem(grp + G - 1, G), pos), at(lax.rem(grp + 1, G), pos)]
    col_send, col_recv = [pos > 0, pos < PN - 1], [pos < PN - 1, pos > 0]
    row_send, row_recv = [grp > 0, grp < G - 1], [grp < G - 1, grp > 0]
    partner = at(grp, pos + 1 - 2 * core)
    across = at(grp, pos + 2 * core - 1)
    has_outer = ((core == 0) & (pos > 0)) | ((core == 1) & (pos < PN - 1))
    has_relay = late & (((core == 1) & (pos + 3 < PN)) | ((core == 0) & (pos >= 3)))
    relay_peer, feeder = at(grp, pos + 6 * core - 3), at(grp, pos + 2 - 4 * core)
    forward_peer = at(grp, pos + 4 * core - 2)

    def ring_at(k):
        return lax.rem(me + k, ring)

    def ring_peer(k):
        q = ring_at(k)
        return at(q // lines, (lax.rem(q, lines) * 2 + side) * 2 + core)

    locals_ = [
        pltpu.make_async_copy(cor_hbm, corners, loc.at[0]),
        pltpu.make_async_copy(obj_hbm, body, loc.at[1]),
        pltpu.make_async_copy(obj_hbm, ext.at[:, pl.ds(HALO, TR), :], loc.at[2]),
        pltpu.make_async_copy(cnt_hbm, counts, loc.at[3]),
        pltpu.make_async_copy(prb_hbm, prb, loc.at[4]),
        pltpu.make_async_copy(tab_hbm, tab, loc.at[5]),
    ]
    for w in range(2):
        columns = pl.ds(w * HALO, HALO)
        locals_.append(pltpu.make_async_copy(pat_hbm.at[:, :, columns], pat.at[w], loc.at[6]))
        for turn in range(2):
            locals_.append(pltpu.make_async_copy(
                prb_hbm.at[:, :, columns], prb2.at[:, w, pl.ds(turn * M, M), :], loc.at[7]))

    locals_[0].start()
    near_ring = [
        (late & row_send[0], row_peer[0]), (late & row_send[1], row_peer[1]),
        (late & (pos >= 4), at(grp, pos - 4)), (late & (pos + 4 < PN), at(grp, pos + 4)),
    ]
    barrier = pltpu.get_barrier_semaphore()

    def greet(condition, peers):
        @pl.when(condition)
        def _():
            for peer in peers:
                pl.semaphore_signal(barrier, inc=1, **peer)
        return condition.astype(jnp.int32) * len(peers)

    expected = greet(col_send[0], [col_peer[0]]) + greet(col_send[1], [col_peer[1]])
    expected += greet(row_send[0], [row_peer[0]]) + greet(row_send[1], [row_peer[1]])
    expected += greet(near_ring[2][0], [near_ring[2][1]]) + greet(near_ring[3][0], [near_ring[3][1]])
    expected += greet(~late & has_outer, [relay_peer, feeder]) + greet(has_relay, [relay_peer, forward_peer])

    for c in locals_[1:3]:
        c.start()
    lane = lax.broadcasted_iota(jnp.int32, (M, HALO), 1)
    gp[...] = jnp.zeros(gp.shape, jnp.float32)

    locals_[0].wait()
    pl.semaphore_wait(barrier, expected)

    def cor_copy(d):
        return pltpu.make_async_remote_copy(corners, cor_smem.at[d], corsem.at[0, d], corsem.at[1, d], **col_peer[d])

    def row_at(d, s):
        return jnp.clip(cor_smem[d, 0, s] - grp * TR + HALO, 0, TR + 2 * HALO - M)

    def halo_copy(d):
        src, dst = ((HALO, HALO + TR), (TR, 0))[d]
        return pltpu.make_async_remote_copy(
            ext.at[:, pl.ds(src, HALO), :], ext.at[:, pl.ds(dst, HALO), :], yh.at[0, d], yh.at[1, d], **row_peer[d])

    for d in range(2):
        @pl.when(col_send[d])
        def _():
            cor_copy(d).start()
    for c in locals_[1:3]:
        c.wait()
    for c in locals_[3:]:
        c.start()
    for d in range(2):
        @pl.when(row_send[d])
        def _():
            halo_copy(d).start()
    for d in range(2):
        @pl.when(col_recv[d])
        def _():
            cor_copy(d).wait_recv()
    first_half = (grp < G - 1).astype(jnp.int32)
    halves = [first_half, 1 - first_half]

    def patch_copy(d, s, h):
        return pltpu.make_async_remote_copy(
            stage.at[d, s, h], nb.at[d, s, h], outsem.at[d], patsem.at[d, s], **col_peer[d])

    def wrapped(source, inset, c, r, h):
        after = r + HALO * (1 - h)
        base = after - lax.rem(after, 2 * HALO) + HALO * h
        last = source.shape[1] - HALO
        low, high = [
            source[c, pl.ds(jnp.clip(at_row - inset * HALO, 0, last), HALO), :]
            for at_row in (base, base + 2 * HALO)
        ]
        rows = lax.broadcasted_iota(jnp.int32, (HALO, HALO), 0) + base
        return jnp.where(rows >= r, low, high)

    def send_patch(s, which):
        h = halves[which]
        for d in range(2):
            @pl.when(col_send[d])
            def _():
                r = row_at(1 - d, s)
                for c in range(2):
                    stage[d, s, h, c] = wrapped((ext, body)[which], which, c, r, h)
                patch_copy(d, s, h).start()

    for s in range(min(2, S)):
        send_patch(s, 1)
    for d in range(2):
        @pl.when(row_recv[d])
        def _():
            halo_copy(d).wait_recv()
    for s in range(S):
        if s >= 2:
            send_patch(s, 1)
        send_patch(s, 0)

    for step in range(lines + G - 3):
        for there, peer in near_ring:
            @pl.when(there)
            def _():
                pl.semaphore_signal(farsem.at[step], inc=1, **peer)
        known = sum(there.astype(jnp.int32) for there, _ in near_ring)

        @pl.when(late)
        def _():
            pl.semaphore_wait(farsem.at[step], known)

    def chip_grad(s, h):
        d = 1 - core
        return pltpu.make_async_remote_copy(
            gsend.at[d, h, s], grecv.at[d, h, s], outsem.at[2 + d], gsem.at[d, 0], **partner)

    def outer_grad(s, h):
        return pltpu.make_async_remote_copy(
            gsend.at[core, h, s], grecv.at[core, h, s], outsem.at[2 + core], gsem.at[core, h], **across)

    def relay_grad(s, h):
        return pltpu.make_async_remote_copy(
            gsend.at[core, h, s], relay.at[h, s], outsem.at[2 + core], rsem.at[h], **relay_peer)

    def forward_grad(s, h):
        return pltpu.make_async_remote_copy(
            relay.at[h, s], grecv.at[1 - core, h, s], outsem.at[4], gsem.at[1 - core, h], **forward_peer)

    for c in locals_[3:6]:
        c.wait()
    drain(pat, loc.at[6])
    drain(prb2, loc.at[7])
    own_count = counts[grp * PN + pos]

    column = lax.broadcasted_iota(jnp.int32, (M, M), 1)
    wanted = jnp.where(column < M // 2, 2 * column, 2 * column - (M - 1))
    pick = (lax.broadcasted_iota(jnp.int32, (M, M), 0) == wanted).astype(jnp.float32).astype(jnp.bfloat16)

    def reorder(s, carry):
        rows = side_by_side(*[
            stack(*[pat[w, s, pl.ds(odd, M // 2, stride=2), :] for odd in range(2)]) for w in range(2)
        ])
        high, low = split(rows)
        last = (rows - high.astype(jnp.float32) - low.astype(jnp.float32)).astype(jnp.bfloat16)
        patp[s] = dot(high, pick) + (dot(low, pick) + dot(last, pick))
        return carry

    lax.fori_loop(0, S, reorder, 0)

    def row_of(s):
        return jnp.clip(corners[0, s] - grp * TR + HALO, 0, TR + 2 * HALO - M)

    def slot(s, carry):
        r = row_of(s)
        shift = jnp.clip(corners[1, s] - pos * HALO + HALO, 0, HALO)
        for d in range(2):
            @pl.when(col_recv[d])
            def _():
                drain(nb.at[d, s], patsem.at[d, s])
        back = lax.rem(HALO - shift, HALO)
        forth = lax.rem(shift, HALO)
        first = lane < HALO - shift
        patch = []
        for c in range(2):
            mid, before, after = [
                pltpu.roll(stack(*pair), back, 1)
                for pair in (
                    [wrapped(ext, 0, c, r, h) for h in range(2)],
                    [nb[1, s, h, c] for h in range(2)],
                    [nb[0, s, h, c] for h in range(2)],
                )
            ]
            patch.append(side_by_side(jnp.where(first, before, mid), jnp.where(first, mid, after)))
        turn = lax.rem(r, M)
        pr, pi = [side_by_side(*[prb2[c, w, pl.ds(M - turn, M), :] for w in range(2)]) for c in range(2)]
        fr, fi = forward(tab, pr * patch[0] - pi * patch[1], pr * patch[1] + pi * patch[0])
        excess = fr * fr + fi * fi - patp[s]
        excess = jnp.where(jnp.full((M, M), s, jnp.int32) < own_count, excess, 0.0)
        cr, ci = backward(tab, excess * fr, excess * fi)
        parts = (pr * cr + pi * ci, pr * ci - pi * cr)
        for c, part in enumerate((patch[0] * cr + patch[1] * ci, patch[0] * ci - patch[1] * cr)):
            for w in range(2):
                turned[c, w, :M] = cols_of(part, w)
                turned[c, w, M:] = cols_of(part, w)
                gp[c, :, w * HALO : (w + 1) * HALO] += turned[c, w, pl.ds(turn, M), :]
        tail = lane >= shift
        for c in range(2):
            g0, g1 = [pltpu.roll(cols_of(parts[c], w), forth, 1) for w in range(2)]
            left, middle, right = jnp.where(tail, g0, 0.0), jnp.where(tail, g1, g0), jnp.where(tail, 0.0, g1)
            for h in range(2):
                gsend[0, h, s, c] = rows_of(left, h)
                gmid[s, h, c] = rows_of(middle, h)
                gsend[1, h, s, c] = rows_of(right, h)
        for h in range(2):
            chip_grad(s, h).start()

        @pl.when(has_outer & late)
        def _():
            outer_grad(s, halves[0]).start()

        @pl.when(has_outer & ~late)
        def _():
            relay_grad(s, halves[0]).start()
        return carry

    lax.fori_loop(0, S, slot, 0)

    core_copy = pltpu.make_async_remote_copy(gp, p1r, csem.at[0], csem.at[1], **partner)

    def share_rows(q):
        return pl.ds(pl.multiple_of(lax.rem(q, owners) * h3, 8), h3)

    pieces = M // HALO

    def chunk(q, owner):
        return q // pieces, share_rows(owner), pl.ds(q % pieces * HALO, HALO)

    def share_copy(q, k):
        return pltpu.make_async_remote_copy(
            gp.at[chunk(q, ring_at(k))], p3r.at[q, k - 1], outsem.at[5], asem.at[q], **ring_peer(k))

    def pass_share(q, owner, send_sem, recv_sem, peer):
        where = chunk(q, owner)
        return pltpu.make_async_remote_copy(prb_out.at[where], prb_out.at[where], send_sem, recv_sem, **peer)

    line = chip // 2

    def line_at(k):
        return lax.rem(line + k + lines, lines)

    def line_peer(k):
        return at(grp, (line_at(k) * 2 + side) * 2 + core)

    def group_at(j):
        return lax.rem(grp + j + G, G)

    def line_spread(q, k):
        return pass_share(q, me, outsem.at[6], agsem.at[q, 0], line_peer(k))

    def group_spread(q, owner):
        return pass_share(q, owner, outsem.at[7], agsem.at[q, 1], at(group_at(1), pos))

    def spread_copy(q, k, owner):
        return pass_share(q, owner, outsem.at[6], agsem.at[q, 0], ring_peer(k))

    def hand_copy(q, owner):
        return pass_share(q, owner, outsem.at[8], casem.at[0], partner)

    def across_copy(q):
        return pltpu.make_async_remote_copy(p2.at[q], p2x.at[q], xsem.at[0, q], xsem.at[1, q], **across)

    chunks = range(2 * pieces)

    def source(k):
        return lax.rem(me + ring - k, ring)

    def pass_on(h):
        @pl.when(has_relay)
        def _():
            drain(relay.at[h], rsem.at[h])
            for s in range(S):
                forward_grad(s, h).start()

    def covers(block, r):
        rows = lax.broadcasted_iota(jnp.int32, (HALO, HALO), 0) + (block * HALO - r)
        return (rows >= 0) & (rows < M)

    def own(totals, block, h):
        for s in range(S):
            inside = covers(block, row_of(s))
            totals = [t + jnp.where(inside, gmid[s, h, c], 0.0) for c, t in enumerate(totals)]
        return totals

    def others(totals, block, h, d):
        for s in range(S):
            inside = covers(block, row_at(d, s))
            totals = [t + jnp.where(inside, grecv[d, h, s, c], 0.0) for c, t in enumerate(totals)]
        return totals

    zeros = [jnp.zeros((HALO, HALO), jnp.float32)] * 2

    def near(block, carry):
        h = lax.rem(block, 2)
        totals = others(own(zeros, block, h), block, h, core)
        rows = pl.ds(pl.multiple_of(block * HALO, HALO), HALO)
        for c in range(2):
            obj_out[c, pl.ds(pl.multiple_of(block * HALO - HALO, HALO), HALO), :] = (
                ext[c, rows, :] - STEP_OBJECT * totals[c])
        return carry

    def near_all():
        drain(grecv.at[core], gsem.at[core, 0])
        lax.fori_loop(1, blocks - 1, near, 0)

    def second(first, last):
        @pl.when(has_outer)
        def _():
            for s in range(first, last):
                outer_grad(s, halves[1]).start()

    @pl.when(~late)
    def _():
        core_copy.start()

        @pl.when(has_outer)
        def _():
            for s in range(S):
                relay_grad(s, halves[1]).start()
        near_all()

    @pl.when(late)
    def _():
        core_copy.wait_recv()
        gp[...] += p1r[...]
        for q in chunks:
            for k in range(1, ring):
                @pl.when(ring_at(k) < owners)
                def _():
                    share_copy(q, k).start()
        pass_on(halves[0])
        near_all()
        for q in chunks:
            @pl.when(me < owners)
            def _():
                total = gp[chunk(q, me)]
                drain(p3r.at[q], asem.at[q])
                for k in range(ring - 1):
                    total = total + p3r[q, k]
                p2[q] = total
                across_copy(q).start()

            if q == pieces - 1:
                second(0, 1)
        second(1, S)

        pass_on(halves[1])
        live = counts[0]
        for i in range(1, G * PN):
            live = live + counts[i]

        @pl.when(me < owners)
        def _():
            for q in chunks:
                across_copy(q).wait_recv()
                total = p2[q] + p2x[q]
                divisor = jnp.full(total.shape, live, jnp.int32).astype(jnp.float32)
                prb_out[chunk(q, me)] = prb[chunk(q, me)] - STEP_PROBE * total / divisor
                if split_ring:
                    for k in range(1, lines):
                        line_spread(q, k).start()
                    group_spread(q, me).start()
                else:
                    for k in range(1, ring):
                        spread_copy(q, k, me).start()
                hand_copy(q, me).start()

    def rim_copy(d):
        return pltpu.make_async_remote_copy(rim.at[d], yrecv.at[d], ysem.at[0, d], ysem.at[1, d], **row_peer[d])

    def finish(h):
        @pl.when(has_outer)
        def _():
            drain(grecv.at[1 - core, h], gsem.at[1 - core, h])
        for d in range(2):
            block = d * (blocks - 1)

            @pl.when(row_send[d] & (h == d))
            def _():
                totals = others(own(zeros, block, d), block, d, core)
                for c in range(2):
                    rim[d, c] = totals[c]

                @pl.when(has_outer)
                def _():
                    more = others([rim[d, c] for c in range(2)], block, d, 1 - core)
                    for c in range(2):
                        rim[d, c] = more[c]
                rim_copy(d).start()

        @pl.when(has_outer)
        def _():
            def far(i, carry):
                block = 2 * i + 2 - h
                totals = others(zeros, block, h, 1 - core)
                rows = pl.ds(pl.multiple_of(block * HALO - HALO, HALO), HALO)
                for c in range(2):
                    obj_out[c, rows, :] = obj_out[c, rows, :] - STEP_OBJECT * totals[c]
                return carry

            lax.fori_loop(0, blocks // 2 - 1, far, 0)

    finish(halves[0])
    finish(halves[1])

    @pl.when(late)
    def _():
        if split_ring:
            for q in chunks:
                drain(prb_out.at[0, pl.ds(0, (lines - 1) * h3), pl.ds(0, HALO)], agsem.at[q, 0])
                for k in range(1, lines):
                    owner = grp * lines + line_at(-k)
                    group_spread(q, owner).start()
                    hand_copy(q, owner).start()
            for q in chunks:
                drain(prb_out.at[0, pl.ds(0, lines * h3), pl.ds(0, HALO)], agsem.at[q, 1])
                for k in range(lines):
                    hand_copy(q, group_at(1) * lines + line_at(-k)).start()
        else:
            for q in chunks:
                for k in range(1, ring):
                    @pl.when(source(k) < owners)
                    def _():
                        spread_copy(q, k, source(k)).wait_recv()
                        hand_copy(q, source(k)).start()

    for d in range(2):
        @pl.when(row_recv[d])
        def _():
            rim_copy(d).wait_recv()
            rows = pl.ds((TR - HALO, 0)[d], HALO)
            obj_out[:, rows, :] = obj_out[:, rows, :] - STEP_OBJECT * yrecv[d]

    @pl.when(~late)
    def _():
        drain(prb_out, casem.at[0])

    for d in range(2):
        @pl.when(col_send[d])
        def _():
            cor_copy(d).wait_send()
            drain(stage.at[d], outsem.at[d])

        @pl.when(row_send[d])
        def _():
            halo_copy(d).wait_send()
            rim_copy(d).wait_send()
    drain(gsend.at[1 - core], outsem.at[3 - core])

    @pl.when(has_outer)
    def _():
        drain(gsend.at[core], outsem.at[2 + core])

    @pl.when(has_relay)
    def _():
        drain(relay, outsem.at[4])

    @pl.when(~late)
    def _():
        core_copy.wait_send()

    @pl.when(late)
    def _():
        if split_ring:
            drain(p3r, outsem.at[5])
            drain(prb_out.at[:, pl.ds(0, (lines - 1) * h3), :], outsem.at[6])
            drain(prb_out.at[:, pl.ds(0, lines * h3), :], outsem.at[7])
        else:
            for q in chunks:
                for k in range(1, ring):
                    @pl.when(ring_at(k) < owners)
                    def _():
                        share_copy(q, k).wait_send()

                @pl.when(me < owners)
                def _():
                    for k in range(1, ring):
                        spread_copy(q, k, me).wait_send()

        @pl.when(me < owners)
        def _():
            for q in chunks:
                across_copy(q).wait_send()
        drain(prb_out, outsem.at[8])


def store(obj, prb, obj_out, prb_out, sems):
    pairs = []
    for whole, out in ((obj, obj_out), (prb, prb_out)):
        rows = whole.shape[1] // PIECES
        pairs += [(whole.at[:, pl.ds(i * rows, rows), :], out.at[:, pl.ds(i * rows, rows), :]) for i in range(PIECES)]
    copies = [pltpu.make_async_copy(*pair, sems.at[i]) for i, pair in enumerate(pairs)]
    for c in copies:
        c.start()
    for c in copies:
        c.wait()


def on_device(grp_size, pos_size, tables, object_field, probe_field, patterns, corners, counts):
    TR, S, M = object_field.shape[1], patterns.shape[0], probe_field.shape[1]
    ring = grp_size * (pos_size // 4)
    owners, h3 = shares(M, ring)
    f32 = jnp.float32
    V, D = pltpu.VMEM, pltpu.SemaphoreType.DMA
    hbm = pl.BlockSpec(memory_space=pl.ANY)
    vmem = pl.BlockSpec(memory_space=pltpu.VMEM)
    half, chunks = (2, HALO, HALO), 2 * (M // HALO)
    object_new, probe_new = pl.pallas_call(
        functools.partial(kernel, (grp_size, pos_size, S, TR, M)),
        out_shape=(
            pltpu.VMEM(object_field.shape, f32),
            pltpu.VMEM(probe_field.shape, f32),
        ),
        in_specs=[hbm] * 6,
        out_specs=(vmem, vmem),
        scratch_shapes=[
            pltpu.SMEM(corners.shape, jnp.int32),
            pltpu.SMEM(counts.shape, jnp.int32),
            V((2, TR + 2 * HALO, HALO), f32),
            V((2, TR, HALO), f32),
            V((2, M, M), f32),
            V((2, 2, 2 * M, HALO), f32),
            V((2, S, M, HALO), f32),
            V((S, M, M), f32),
            V(tables.shape, jnp.bfloat16),
            V((2, S, 2, *half), f32),
            V((2, S, 2, *half), f32),
            pltpu.SMEM((2, *corners.shape), jnp.int32),
            V((S, 2, *half), f32),
            V((2, 2, S, *half), f32),
            V((2, 2, S, *half), f32),
            V((2, S, *half), f32),
            V((2, 2, 2 * M, HALO), f32),
            V((2, *half), f32),
            V((2, *half), f32),
            V((2, M, M), f32),
            V((2, M, M), f32),
            V((chunks, ring - 1, h3, HALO), f32),
            V((chunks, h3, HALO), f32),
            V((chunks, h3, HALO), f32),
            D((8,)), pltpu.SemaphoreType.REGULAR((max(1, grp_size + pos_size // 4 - 3),)), D((2, 2)), D((2, 2)), D((2, S)),
            D((2, 2)), D((2,)), D((2, 2)), D((2,)), D((chunks,)), D((chunks, 2)), D((2, chunks)), D((1,)), D((9,)),
        ],
        compiler_params=pltpu.CompilerParams(
            collective_id=0, has_side_effects=True, vmem_limit_bytes=56 * 1024 * 1024
        ),
    )(corners, counts, object_field, probe_field, patterns, jnp.asarray(tables))
    object_new = pltpu.with_memory_space_constraint(object_new, pltpu.VMEM)
    probe_new = pltpu.with_memory_space_constraint(probe_new, pltpu.VMEM)
    return pl.pallas_call(
        store,
        out_shape=(
            jax.ShapeDtypeStruct(object_field.shape, f32),
            jax.ShapeDtypeStruct(probe_field.shape, f32),
        ),
        in_specs=[hbm, hbm],
        out_specs=(hbm, hbm),
        scratch_shapes=[D((2 * PIECES,))],
        compiler_params=pltpu.CompilerParams(vmem_limit_bytes=1024 * 1024),
    )(object_new, probe_new)

def solution(mesh):
    def body(object_field, probe_field, patterns, corners, counts):
        tables = dft_tables(probe_field.shape[1])
        return on_device(
            mesh.shape["grp"], mesh.shape["pos"], tables, object_field, probe_field, patterns, corners, counts
        )

    return jax.shard_map(
        body,
        mesh=mesh,
        in_specs=(
            P(None, "grp", "pos"),
            P(),
            P(("grp", "pos"), None, None),
            P(None, ("grp", "pos")),
            P(),
        ),
        out_specs=(P(None, "grp", "pos"), P()),
        check_vma=False,
    )
```

```python
import functools

import jax
import jax.numpy as jnp
import numpy as np
from jax import lax
from jax.experimental import pallas as pl
from jax.experimental.pallas import tpu as pltpu
from jax.sharding import PartitionSpec as P

HALO = 128
STEP_OBJECT = 0.25
STEP_PROBE = 4.0
PIECES = 1
MESH = pl.DeviceIdType.MESH


def dft_tables(order):
    half = order // 2
    columns = np.arange(half, dtype=np.int64)
    tables = []
    for odd in range(2):
        rows = 2 * np.arange(half, dtype=np.int64) + odd
        angles = (rows[:, None] * columns[None, :] % order) * (2.0 * np.pi / order)
        re, im = np.cos(angles) / np.sqrt(order), -np.sin(angles) / np.sqrt(order)
        block = np.block([[re, -im], [im, re]])
        tables.append(np.stack([block, block.T]))
    both = np.stack(tables).astype(np.float32)
    high = both.astype(jnp.bfloat16)
    low = (both - high.astype(np.float32)).astype(jnp.bfloat16)
    return np.stack([high, low], axis=2)


def split(x):
    high = x.astype(jnp.bfloat16)
    low = (x - high.astype(jnp.float32)).astype(jnp.bfloat16)
    return high, low


def dot(a, b):
    return jnp.dot(a, b, preferred_element_type=jnp.float32)


def table_left(tab, odd, turn, data):
    high, low = split(data)
    th, tl = tab[odd, turn, 0], tab[odd, turn, 1]
    return dot(th, high) + (dot(th, low) + dot(tl, high))


def table_right(data, tab, odd, turn):
    high, low = split(data)
    th, tl = tab[odd, turn, 0], tab[odd, turn, 1]
    return dot(high, th) + (dot(low, th) + dot(high, tl))


def rows_of(x, h):
    n = x.shape[0] // 2
    return x[h * n : (h + 1) * n]


def cols_of(x, h):
    n = x.shape[1] // 2
    return x[:, h * n : (h + 1) * n]


def stack(a, b):
    return jnp.concatenate([a, b], axis=0)


def side_by_side(a, b):
    return jnp.concatenate([a, b], axis=1)


def forward(tab, re, im):
    r0, r1, i0, i1 = rows_of(re, 0), rows_of(re, 1), rows_of(im, 0), rows_of(im, 1)
    even = table_left(tab, 0, 0, stack(r0 + r1, i0 + i1))
    odd = table_left(tab, 1, 0, stack(r0 - r1, i0 - i1))
    re, im = stack(rows_of(even, 0), rows_of(odd, 0)), stack(rows_of(even, 1), rows_of(odd, 1))
    r0, r1, i0, i1 = cols_of(re, 0), cols_of(re, 1), cols_of(im, 0), cols_of(im, 1)
    even = table_right(side_by_side(r0 + r1, i0 + i1), tab, 0, 1)
    odd = table_right(side_by_side(r0 - r1, i0 - i1), tab, 1, 1)
    return side_by_side(cols_of(even, 0), cols_of(odd, 0)), side_by_side(cols_of(even, 1), cols_of(odd, 1))


def backward(tab, re, im):
    even = table_left(tab, 0, 1, stack(rows_of(re, 0), rows_of(im, 0)))
    odd = table_left(tab, 1, 1, stack(rows_of(re, 1), rows_of(im, 1)))
    total, rest = even + odd, even - odd
    re, im = stack(rows_of(total, 0), rows_of(rest, 0)), stack(rows_of(total, 1), rows_of(rest, 1))
    even = table_right(side_by_side(cols_of(re, 0), cols_of(im, 0)), tab, 0, 0)
    odd = table_right(side_by_side(cols_of(re, 1), cols_of(im, 1)), tab, 1, 0)
    total, rest = even + odd, even - odd
    return side_by_side(cols_of(total, 0), cols_of(rest, 0)), side_by_side(cols_of(total, 1), cols_of(rest, 1))


def drain(ref, sem):
    pltpu.make_async_copy(ref, ref, sem).wait()


def shares(rows, ring):
    owners = min(ring, rows // 8)
    return owners, rows // owners


def kernel(sizes, cor_hbm, cnt_hbm, obj_hbm, prb_hbm, pat_hbm, tab_hbm, obj_out, prb_out,
           corners, counts, ext, body, prb, prb2, pat, patp, tab, nb, stage, cor_smem,
           gmid, gsend, grecv, relay, turned, rim, yrecv, gp, p1r, p3r, gpr, p2, p2x,
           loc, farsem, yh, corsem, patsem, gsem, rsem, ysem, csem, asem, agsem, xsem, casem, gprsem, outsem):
    G, PN, S, TR, M = sizes
    grp, pos = lax.axis_index("grp"), lax.axis_index("pos")
    core, chip, chips = lax.rem(pos, 2), pos // 2, PN // 2
    side, lines = lax.rem(chip, 2), chips // 2
    ring = G * lines
    owners, h3 = shares(M, ring)
    me = grp * lines + chip // 2
    late = side != core
    blocks = TR // HALO + 2
    split_ring = ring == owners and G == 2

    def at(g, p):
        return {"device_id": (g, lax.rem(p + PN, PN)), "device_id_type": MESH}

    col_peer = [at(grp, pos - 1), at(grp, pos + 1)]
    row_peer = [at(lax.rem(grp + G - 1, G), pos), at(lax.rem(grp + 1, G), pos)]
    col_send, col_recv = [pos > 0, pos < PN - 1], [pos < PN - 1, pos > 0]
    row_send, row_recv = [grp > 0, grp < G - 1], [grp < G - 1, grp > 0]
    partner = at(grp, pos + 1 - 2 * core)
    across = at(grp, pos + 2 * core - 1)
    has_outer = ((core == 0) & (pos > 0)) | ((core == 1) & (pos < PN - 1))
    has_relay = late & (((core == 1) & (pos + 3 < PN)) | ((core == 0) & (pos >= 3)))
    relay_peer, feeder = at(grp, pos + 6 * core - 3), at(grp, pos + 2 - 4 * core)
    forward_peer = at(grp, pos + 4 * core - 2)

    def ring_at(k):
        return lax.rem(me + k, ring)

    def ring_peer(k):
        q = ring_at(k)
        return at(q // lines, (lax.rem(q, lines) * 2 + side) * 2 + core)

    locals_ = [
        pltpu.make_async_copy(cor_hbm, corners, loc.at[0]),
        pltpu.make_async_copy(obj_hbm, body, loc.at[1]),
        pltpu.make_async_copy(obj_hbm, ext.at[:, pl.ds(HALO, TR), :], loc.at[2]),
        pltpu.make_async_copy(cnt_hbm, counts, loc.at[3]),
        pltpu.make_async_copy(prb_hbm, prb, loc.at[4]),
        pltpu.make_async_copy(tab_hbm, tab, loc.at[5]),
    ]
    for w in range(2):
        columns = pl.ds(w * HALO, HALO)
        locals_.append(pltpu.make_async_copy(pat_hbm.at[:, :, columns], pat.at[w], loc.at[6]))
        for turn in range(2):
            locals_.append(pltpu.make_async_copy(
                prb_hbm.at[:, :, columns], prb2.at[:, w, pl.ds(turn * M, M), :], loc.at[7]))

    locals_[0].start()
    near_ring = [
        (late & row_send[0], row_peer[0]), (late & row_send[1], row_peer[1]),
        (late & (pos >= 4), at(grp, pos - 4)), (late & (pos + 4 < PN), at(grp, pos + 4)),
    ]
    barrier = pltpu.get_barrier_semaphore()

    def greet(condition, peers):
        @pl.when(condition)
        def _():
            for peer in peers:
                pl.semaphore_signal(barrier, inc=1, **peer)
        return condition.astype(jnp.int32) * len(peers)

    expected = greet(col_send[0], [col_peer[0]]) + greet(col_send[1], [col_peer[1]])
    expected += greet(row_send[0], [row_peer[0]]) + greet(row_send[1], [row_peer[1]])
    expected += greet(near_ring[2][0], [near_ring[2][1]]) + greet(near_ring[3][0], [near_ring[3][1]])
    expected += greet(~late & has_outer, [relay_peer, feeder]) + greet(has_relay, [relay_peer, forward_peer])

    for c in locals_[1:3]:
        c.start()
    lane = lax.broadcasted_iota(jnp.int32, (M, HALO), 1)
    gp[...] = jnp.zeros(gp.shape, jnp.float32)

    locals_[0].wait()
    pl.semaphore_wait(barrier, expected)

    def cor_copy(d):
        return pltpu.make_async_remote_copy(corners, cor_smem.at[d], corsem.at[0, d], corsem.at[1, d], **col_peer[d])

    def row_at(d, s):
        return jnp.clip(cor_smem[d, 0, s] - grp * TR + HALO, 0, TR + 2 * HALO - M)

    def halo_copy(d):
        src, dst = ((HALO, HALO + TR), (TR, 0))[d]
        return pltpu.make_async_remote_copy(
            ext.at[:, pl.ds(src, HALO), :], ext.at[:, pl.ds(dst, HALO), :], yh.at[0, d], yh.at[1, d], **row_peer[d])

    for d in range(2):
        @pl.when(col_send[d])
        def _():
            cor_copy(d).start()
    for c in locals_[1:3]:
        c.wait()
    for c in locals_[3:]:
        c.start()
    for d in range(2):
        @pl.when(row_send[d])
        def _():
            halo_copy(d).start()
    for d in range(2):
        @pl.when(col_recv[d])
        def _():
            cor_copy(d).wait_recv()
    first_half = (grp < G - 1).astype(jnp.int32)
    halves = [first_half, 1 - first_half]

    def patch_copy(d, s, h):
        return pltpu.make_async_remote_copy(
            stage.at[d, s, h], nb.at[d, s, h], outsem.at[d], patsem.at[d, s], **col_peer[d])

    def wrapped(source, inset, c, r, h):
        after = r + HALO * (1 - h)
        base = after - lax.rem(after, 2 * HALO) + HALO * h
        last = source.shape[1] - HALO
        low, high = [
            source[c, pl.ds(jnp.clip(at_row - inset * HALO, 0, last), HALO), :]
            for at_row in (base, base + 2 * HALO)
        ]
        rows = lax.broadcasted_iota(jnp.int32, (HALO, HALO), 0) + base
        return jnp.where(rows >= r, low, high)

    def send_patch(s, which):
        h = halves[which]
        for d in range(2):
            @pl.when(col_send[d])
            def _():
                r = row_at(1 - d, s)
                for c in range(2):
                    stage[d, s, h, c] = wrapped((ext, body)[which], which, c, r, h)
                patch_copy(d, s, h).start()

    for s in range(min(2, S)):
        send_patch(s, 1)
    for d in range(2):
        @pl.when(row_recv[d])
        def _():
            halo_copy(d).wait_recv()
    for s in range(S):
        if s >= 2:
            send_patch(s, 1)
        send_patch(s, 0)

    for step in range(lines + G - 3):
        for there, peer in near_ring:
            @pl.when(there)
            def _():
                pl.semaphore_signal(farsem.at[step], inc=1, **peer)
        known = sum(there.astype(jnp.int32) for there, _ in near_ring)

        @pl.when(late)
        def _():
            pl.semaphore_wait(farsem.at[step], known)

    def chip_grad(s, h):
        d = 1 - core
        return pltpu.make_async_remote_copy(
            gsend.at[d, h, s], grecv.at[d, h, s], outsem.at[2 + d], gsem.at[d, 0], **partner)

    def outer_grad(s, h):
        return pltpu.make_async_remote_copy(
            gsend.at[core, h, s], grecv.at[core, h, s], outsem.at[2 + core], gsem.at[core, h], **across)

    def relay_grad(s, h):
        return pltpu.make_async_remote_copy(
            gsend.at[core, h, s], relay.at[h, s], outsem.at[2 + core], rsem.at[h], **relay_peer)

    def forward_grad(s, h):
        return pltpu.make_async_remote_copy(
            relay.at[h, s], grecv.at[1 - core, h, s], outsem.at[4], gsem.at[1 - core, h], **forward_peer)

    for c in locals_[3:6]:
        c.wait()
    drain(pat, loc.at[6])
    drain(prb2, loc.at[7])
    own_count = counts[grp * PN + pos]

    column = lax.broadcasted_iota(jnp.int32, (M, M), 1)
    wanted = jnp.where(column < M // 2, 2 * column, 2 * column - (M - 1))
    pick = (lax.broadcasted_iota(jnp.int32, (M, M), 0) == wanted).astype(jnp.float32).astype(jnp.bfloat16)

    def reorder(s, carry):
        rows = side_by_side(*[
            stack(*[pat[w, s, pl.ds(odd, M // 2, stride=2), :] for odd in range(2)]) for w in range(2)
        ])
        high, low = split(rows)
        last = (rows - high.astype(jnp.float32) - low.astype(jnp.float32)).astype(jnp.bfloat16)
        patp[s] = dot(high, pick) + (dot(low, pick) + dot(last, pick))
        return carry

    lax.fori_loop(0, S, reorder, 0)

    def row_of(s):
        return jnp.clip(corners[0, s] - grp * TR + HALO, 0, TR + 2 * HALO - M)

    def slot(s, carry):
        r = row_of(s)
        shift = jnp.clip(corners[1, s] - pos * HALO + HALO, 0, HALO)
        for d in range(2):
            @pl.when(col_recv[d])
            def _():
                drain(nb.at[d, s], patsem.at[d, s])
        back = lax.rem(HALO - shift, HALO)
        forth = lax.rem(shift, HALO)
        first = lane < HALO - shift
        patch = []
        for c in range(2):
            mid, before, after = [
                pltpu.roll(stack(*pair), back, 1)
                for pair in (
                    [wrapped(ext, 0, c, r, h) for h in range(2)],
                    [nb[1, s, h, c] for h in range(2)],
                    [nb[0, s, h, c] for h in range(2)],
                )
            ]
            patch.append(side_by_side(jnp.where(first, before, mid), jnp.where(first, mid, after)))
        turn = lax.rem(r, M)
        pr, pi = [side_by_side(*[prb2[c, w, pl.ds(M - turn, M), :] for w in range(2)]) for c in range(2)]
        fr, fi = forward(tab, pr * patch[0] - pi * patch[1], pr * patch[1] + pi * patch[0])
        excess = fr * fr + fi * fi - patp[s]
        excess = jnp.where(jnp.full((M, M), s, jnp.int32) < own_count, excess, 0.0)
        cr, ci = backward(tab, excess * fr, excess * fi)
        parts = (pr * cr + pi * ci, pr * ci - pi * cr)
        for c, part in enumerate((patch[0] * cr + patch[1] * ci, patch[0] * ci - patch[1] * cr)):
            for w in range(2):
                turned[c, w, :M] = cols_of(part, w)
                turned[c, w, M:] = cols_of(part, w)
                gp[c, :, w * HALO : (w + 1) * HALO] += turned[c, w, pl.ds(turn, M), :]
        tail = lane >= shift
        for c in range(2):
            g0, g1 = [pltpu.roll(cols_of(parts[c], w), forth, 1) for w in range(2)]
            left, middle, right = jnp.where(tail, g0, 0.0), jnp.where(tail, g1, g0), jnp.where(tail, 0.0, g1)
            for h in range(2):
                gsend[0, h, s, c] = rows_of(left, h)
                gmid[s, h, c] = rows_of(middle, h)
                gsend[1, h, s, c] = rows_of(right, h)
        for h in range(2):
            chip_grad(s, h).start()

        @pl.when(has_outer & late)
        def _():
            outer_grad(s, halves[0]).start()

        @pl.when(has_outer & ~late)
        def _():
            relay_grad(s, halves[0]).start()
        return carry

    lax.fori_loop(0, S, slot, 0)

    core_copy = pltpu.make_async_remote_copy(gp, p1r, csem.at[0], csem.at[1], **partner)

    def share_rows(q):
        return pl.ds(pl.multiple_of(lax.rem(q, owners) * h3, 8), h3)

    pieces = M // HALO

    def chunk(q, owner):
        return q // pieces, share_rows(owner), pl.ds(q % pieces * HALO, HALO)

    def share_copy(q, k):
        return pltpu.make_async_remote_copy(
            gp.at[chunk(q, ring_at(k))], p3r.at[q, k - 1], outsem.at[5], asem.at[q], **ring_peer(k))

    group_rows = pl.ds(pl.multiple_of(grp * lines * h3, 8), lines * h3)

    def group_share():
        other = group_at(1)
        rows = pl.ds(pl.multiple_of(other * lines * h3, 8), lines * h3)
        return pltpu.make_async_remote_copy(gp.at[1, rows, :], gpr, outsem.at[10], gprsem.at[0], **at(other, pos))

    def line_share(q, k):
        return pltpu.make_async_remote_copy(
            gp.at[chunk(q, grp * lines + line_at(k))], p3r.at[q, k - 1], outsem.at[11], asem.at[q], **line_peer(k))

    def pass_share(q, owner, send_sem, recv_sem, peer):
        where = chunk(q, owner)
        return pltpu.make_async_remote_copy(prb_out.at[where], prb_out.at[where], send_sem, recv_sem, **peer)

    line = chip // 2

    def line_at(k):
        return lax.rem(line + k + lines, lines)

    def line_peer(k):
        return at(grp, (line_at(k) * 2 + side) * 2 + core)

    def group_at(j):
        return lax.rem(grp + j + G, G)

    def line_spread(q, k):
        return pass_share(q, me, outsem.at[6], agsem.at[q, 0], line_peer(k))

    def group_spread(q, owner):
        return pass_share(q, owner, outsem.at[7], agsem.at[q, 1], at(group_at(1), pos))

    def spread_copy(q, k, owner):
        return pass_share(q, owner, outsem.at[6], agsem.at[q, 0], ring_peer(k))

    def hand_copy(q, owner):
        return pass_share(q, owner, outsem.at[8], casem.at[0], partner)

    def across_copy(q):
        return pltpu.make_async_remote_copy(p2.at[q], p2x.at[q], outsem.at[9], xsem.at[q], **across)

    chunks = range(2 * pieces)
    direct = chunks[:pieces] if split_ring else chunks

    def source(k):
        return lax.rem(me + ring - k, ring)

    def pass_on(h):
        @pl.when(has_relay)
        def _():
            drain(relay.at[h], rsem.at[h])
            for s in range(S):
                forward_grad(s, h).start()

    def covers(block, r):
        rows = lax.broadcasted_iota(jnp.int32, (HALO, HALO), 0) + (block * HALO - r)
        return (rows >= 0) & (rows < M)

    def own(totals, block, h):
        for s in range(S):
            inside = covers(block, row_of(s))
            totals = [t + jnp.where(inside, gmid[s, h, c], 0.0) for c, t in enumerate(totals)]
        return totals

    def others(totals, block, h, d):
        for s in range(S):
            inside = covers(block, row_at(d, s))
            totals = [t + jnp.where(inside, grecv[d, h, s, c], 0.0) for c, t in enumerate(totals)]
        return totals

    zeros = [jnp.zeros((HALO, HALO), jnp.float32)] * 2

    def near(block, carry):
        h = lax.rem(block, 2)
        totals = others(own(zeros, block, h), block, h, core)
        rows = pl.ds(pl.multiple_of(block * HALO, HALO), HALO)
        for c in range(2):
            obj_out[c, pl.ds(pl.multiple_of(block * HALO - HALO, HALO), HALO), :] = (
                ext[c, rows, :] - STEP_OBJECT * totals[c])
        return carry

    def near_all():
        drain(grecv.at[core], gsem.at[core, 0])
        lax.fori_loop(1, blocks - 1, near, 0)

    def second(first, last):
        @pl.when(has_outer)
        def _():
            for s in range(first, last):
                outer_grad(s, halves[1]).start()

    @pl.when(~late)
    def _():
        core_copy.start()

        @pl.when(has_outer)
        def _():
            for s in range(S):
                relay_grad(s, halves[1]).start()
        near_all()

    @pl.when(late)
    def _():
        core_copy.wait_recv()
        gp[...] += p1r[...]
        if split_ring:
            group_share().start()
        for q in direct:
            for k in range(1, ring):
                @pl.when(ring_at(k) < owners)
                def _():
                    share_copy(q, k).start()
        pass_on(halves[0])
        near_all()
        if split_ring:
            drain(gpr, gprsem.at[0])
            gp[1, group_rows, :] += gpr[...]
            for q in chunks[pieces:]:
                for k in range(1, lines):
                    line_share(q, k).start()
        for q in chunks:
            @pl.when(me < owners)
            def _():
                total = gp[chunk(q, me)]
                terms = (ring if q in direct else lines) - 1
                drain(p3r.at[q, pl.ds(0, terms)], asem.at[q])
                for k in range(terms):
                    total = total + p3r[q, k]
                p2[q] = total
                across_copy(q).start()

            if q == pieces - 1:
                second(0, 1)
        second(1, S)

        pass_on(halves[1])
        live = counts[0]
        for i in range(1, G * PN):
            live = live + counts[i]

        @pl.when(me < owners)
        def _():
            for q in chunks:
                across_copy(q).wait_recv()
                total = p2[q] + p2x[q]
                divisor = jnp.full(total.shape, live, jnp.int32).astype(jnp.float32)
                prb_out[chunk(q, me)] = prb[chunk(q, me)] - STEP_PROBE * total / divisor
                if split_ring:
                    for k in range(1, lines):
                        line_spread(q, k).start()
                    group_spread(q, me).start()
                else:
                    for k in range(1, ring):
                        spread_copy(q, k, me).start()
                hand_copy(q, me).start()

    def rim_copy(d):
        return pltpu.make_async_remote_copy(rim.at[d], yrecv.at[d], ysem.at[0, d], ysem.at[1, d], **row_peer[d])

    def finish(h):
        @pl.when(has_outer)
        def _():
            drain(grecv.at[1 - core, h], gsem.at[1 - core, h])
        for d in range(2):
            block = d * (blocks - 1)

            @pl.when(row_send[d] & (h == d))
            def _():
                totals = others(own(zeros, block, d), block, d, core)
                for c in range(2):
                    rim[d, c] = totals[c]

                @pl.when(has_outer)
                def _():
                    more = others([rim[d, c] for c in range(2)], block, d, 1 - core)
                    for c in range(2):
                        rim[d, c] = more[c]
                rim_copy(d).start()

        @pl.when(has_outer)
        def _():
            def far(i, carry):
                block = 2 * i + 2 - h
                totals = others(zeros, block, h, 1 - core)
                rows = pl.ds(pl.multiple_of(block * HALO - HALO, HALO), HALO)
                for c in range(2):
                    obj_out[c, rows, :] = obj_out[c, rows, :] - STEP_OBJECT * totals[c]
                return carry

            lax.fori_loop(0, blocks // 2 - 1, far, 0)

    finish(halves[0])

    @pl.when(late)
    def _():
        if split_ring:
            for q in chunks:
                drain(prb_out.at[0, pl.ds(0, (lines - 1) * h3), pl.ds(0, HALO)], agsem.at[q, 0])
                for k in range(1, lines):
                    owner = grp * lines + line_at(-k)
                    group_spread(q, owner).start()
                    hand_copy(q, owner).start()
        else:
            for q in chunks:
                for k in range(1, ring):
                    @pl.when(source(k) < owners)
                    def _():
                        spread_copy(q, k, source(k)).wait_recv()
                        hand_copy(q, source(k)).start()

    if split_ring:
        @pl.when(late)
        def _():
            for q in chunks:
                drain(prb_out.at[0, pl.ds(0, lines * h3), pl.ds(0, HALO)], agsem.at[q, 1])
                for k in range(lines):
                    hand_copy(q, group_at(1) * lines + line_at(-k)).start()

    finish(halves[1])

    for d in range(2):
        @pl.when(row_recv[d])
        def _():
            rim_copy(d).wait_recv()
            rows = pl.ds((TR - HALO, 0)[d], HALO)
            obj_out[:, rows, :] = obj_out[:, rows, :] - STEP_OBJECT * yrecv[d]

    @pl.when(~late)
    def _():
        drain(prb_out, casem.at[0])

    for d in range(2):
        @pl.when(col_send[d])
        def _():
            cor_copy(d).wait_send()
            drain(stage.at[d], outsem.at[d])

        @pl.when(row_send[d])
        def _():
            halo_copy(d).wait_send()
            rim_copy(d).wait_send()
    drain(gsend.at[1 - core], outsem.at[3 - core])

    @pl.when(has_outer)
    def _():
        drain(gsend.at[core], outsem.at[2 + core])

    @pl.when(has_relay)
    def _():
        drain(relay, outsem.at[4])

    @pl.when(~late)
    def _():
        core_copy.wait_send()

    @pl.when(late)
    def _():
        if split_ring:
            drain(p3r.at[pl.ds(0, pieces)], outsem.at[5])
            drain(gpr, outsem.at[10])
            drain(p3r.at[pl.ds(pieces, pieces), pl.ds(0, lines - 1)], outsem.at[11])
            drain(prb_out.at[:, pl.ds(0, (lines - 1) * h3), :], outsem.at[6])
            drain(prb_out.at[:, pl.ds(0, lines * h3), :], outsem.at[7])
        else:
            for q in chunks:
                for k in range(1, ring):
                    @pl.when(ring_at(k) < owners)
                    def _():
                        share_copy(q, k).wait_send()

                @pl.when(me < owners)
                def _():
                    for k in range(1, ring):
                        spread_copy(q, k, me).wait_send()

        @pl.when(me < owners)
        def _():
            drain(p2, outsem.at[9])
        drain(prb_out, outsem.at[8])


def store(obj, prb, obj_out, prb_out, sems):
    pairs = []
    for whole, out in ((obj, obj_out), (prb, prb_out)):
        rows = whole.shape[1] // PIECES
        pairs += [(whole.at[:, pl.ds(i * rows, rows), :], out.at[:, pl.ds(i * rows, rows), :]) for i in range(PIECES)]
    copies = [pltpu.make_async_copy(*pair, sems.at[i]) for i, pair in enumerate(pairs)]
    for c in copies:
        c.start()
    for c in copies:
        c.wait()


def on_device(grp_size, pos_size, tables, object_field, probe_field, patterns, corners, counts):
    TR, S, M = object_field.shape[1], patterns.shape[0], probe_field.shape[1]
    ring = grp_size * (pos_size // 4)
    owners, h3 = shares(M, ring)
    f32 = jnp.float32
    V, D = pltpu.VMEM, pltpu.SemaphoreType.DMA
    hbm = pl.BlockSpec(memory_space=pl.ANY)
    vmem = pl.BlockSpec(memory_space=pltpu.VMEM)
    half, chunks = (2, HALO, HALO), 2 * (M // HALO)
    object_new, probe_new = pl.pallas_call(
        functools.partial(kernel, (grp_size, pos_size, S, TR, M)),
        out_shape=(
            pltpu.VMEM(object_field.shape, f32),
            pltpu.VMEM(probe_field.shape, f32),
        ),
        in_specs=[hbm] * 6,
        out_specs=(vmem, vmem),
        scratch_shapes=[
            pltpu.SMEM(corners.shape, jnp.int32),
            pltpu.SMEM(counts.shape, jnp.int32),
            V((2, TR + 2 * HALO, HALO), f32),
            V((2, TR, HALO), f32),
            V((2, M, M), f32),
            V((2, 2, 2 * M, HALO), f32),
            V((2, S, M, HALO), f32),
            V((S, M, M), f32),
            V(tables.shape, jnp.bfloat16),
            V((2, S, 2, *half), f32),
            V((2, S, 2, *half), f32),
            pltpu.SMEM((2, *corners.shape), jnp.int32),
            V((S, 2, *half), f32),
            V((2, 2, S, *half), f32),
            V((2, 2, S, *half), f32),
            V((2, S, *half), f32),
            V((2, 2, 2 * M, HALO), f32),
            V((2, *half), f32),
            V((2, *half), f32),
            V((2, M, M), f32),
            V((2, M, M), f32),
            V((chunks, ring - 1, h3, HALO), f32),
            V((M // grp_size, M), f32),
            V((chunks, h3, HALO), f32),
            V((chunks, h3, HALO), f32),
            D((8,)), pltpu.SemaphoreType.REGULAR((max(1, grp_size + pos_size // 4 - 3),)), D((2, 2)), D((2, 2)), D((2, S)),
            D((2, 2)), D((2,)), D((2, 2)), D((2,)), D((chunks,)), D((chunks, 2)), D((chunks,)), D((1,)), D((1,)), D((12,)),
        ],
        compiler_params=pltpu.CompilerParams(
            collective_id=0, has_side_effects=True, vmem_limit_bytes=56 * 1024 * 1024
        ),
    )(corners, counts, object_field, probe_field, patterns, jnp.asarray(tables))
    object_new = pltpu.with_memory_space_constraint(object_new, pltpu.VMEM)
    probe_new = pltpu.with_memory_space_constraint(probe_new, pltpu.VMEM)
    return pl.pallas_call(
        store,
        out_shape=(
            jax.ShapeDtypeStruct(object_field.shape, f32),
            jax.ShapeDtypeStruct(probe_field.shape, f32),
        ),
        in_specs=[hbm, hbm],
        out_specs=(hbm, hbm),
        scratch_shapes=[D((2 * PIECES,))],
        compiler_params=pltpu.CompilerParams(vmem_limit_bytes=1024 * 1024),
    )(object_new, probe_new)

def solution(mesh):
    def body(object_field, probe_field, patterns, corners, counts):
        tables = dft_tables(probe_field.shape[1])
        return on_device(
            mesh.shape["grp"], mesh.shape["pos"], tables, object_field, probe_field, patterns, corners, counts
        )

    return jax.shard_map(
        body,
        mesh=mesh,
        in_specs=(
            P(None, "grp", "pos"),
            P(),
            P(("grp", "pos"), None, None),
            P(None, ("grp", "pos")),
            P(),
        ),
        out_specs=(P(None, "grp", "pos"), P()),
        check_vma=False,
    )
```

```python
import functools

import jax
import jax.numpy as jnp
import numpy as np
from jax import lax
from jax.experimental import pallas as pl
from jax.experimental.pallas import tpu as pltpu
from jax.sharding import PartitionSpec as P

HALO = 128
STEP_OBJECT = 0.25
STEP_PROBE = 4.0
PIECES = 1
MESH = pl.DeviceIdType.MESH


def dft_tables(order):
    half = order // 2
    columns = np.arange(half, dtype=np.int64)
    tables = []
    for odd in range(2):
        rows = 2 * np.arange(half, dtype=np.int64) + odd
        angles = (rows[:, None] * columns[None, :] % order) * (2.0 * np.pi / order)
        re, im = np.cos(angles) / np.sqrt(order), -np.sin(angles) / np.sqrt(order)
        block = np.block([[re, -im], [im, re]])
        tables.append(np.stack([block, block.T]))
    both = np.stack(tables).astype(np.float32)
    high = both.astype(jnp.bfloat16)
    low = (both - high.astype(np.float32)).astype(jnp.bfloat16)
    return np.stack([high, low], axis=2)


def split(x):
    high = x.astype(jnp.bfloat16)
    low = (x - high.astype(jnp.float32)).astype(jnp.bfloat16)
    return high, low


def dot(a, b):
    return jnp.dot(a, b, preferred_element_type=jnp.float32)


def table_left(tab, odd, turn, data):
    high, low = split(data)
    th, tl = tab[odd, turn, 0], tab[odd, turn, 1]
    return dot(th, high) + (dot(th, low) + dot(tl, high))


def table_right(data, tab, odd, turn):
    high, low = split(data)
    th, tl = tab[odd, turn, 0], tab[odd, turn, 1]
    return dot(high, th) + (dot(low, th) + dot(high, tl))


def rows_of(x, h):
    n = x.shape[0] // 2
    return x[h * n : (h + 1) * n]


def cols_of(x, h):
    n = x.shape[1] // 2
    return x[:, h * n : (h + 1) * n]


def stack(a, b):
    return jnp.concatenate([a, b], axis=0)


def side_by_side(a, b):
    return jnp.concatenate([a, b], axis=1)


def forward(tab, re, im):
    r0, r1, i0, i1 = rows_of(re, 0), rows_of(re, 1), rows_of(im, 0), rows_of(im, 1)
    even = table_left(tab, 0, 0, stack(r0 + r1, i0 + i1))
    odd = table_left(tab, 1, 0, stack(r0 - r1, i0 - i1))
    re, im = stack(rows_of(even, 0), rows_of(odd, 0)), stack(rows_of(even, 1), rows_of(odd, 1))
    r0, r1, i0, i1 = cols_of(re, 0), cols_of(re, 1), cols_of(im, 0), cols_of(im, 1)
    even = table_right(side_by_side(r0 + r1, i0 + i1), tab, 0, 1)
    odd = table_right(side_by_side(r0 - r1, i0 - i1), tab, 1, 1)
    return side_by_side(cols_of(even, 0), cols_of(odd, 0)), side_by_side(cols_of(even, 1), cols_of(odd, 1))


def backward(tab, re, im):
    even = table_left(tab, 0, 1, stack(rows_of(re, 0), rows_of(im, 0)))
    odd = table_left(tab, 1, 1, stack(rows_of(re, 1), rows_of(im, 1)))
    total, rest = even + odd, even - odd
    re, im = stack(rows_of(total, 0), rows_of(rest, 0)), stack(rows_of(total, 1), rows_of(rest, 1))
    even = table_right(side_by_side(cols_of(re, 0), cols_of(im, 0)), tab, 0, 0)
    odd = table_right(side_by_side(cols_of(re, 1), cols_of(im, 1)), tab, 1, 0)
    total, rest = even + odd, even - odd
    return side_by_side(cols_of(total, 0), cols_of(rest, 0)), side_by_side(cols_of(total, 1), cols_of(rest, 1))


def drain(ref, sem):
    pltpu.make_async_copy(ref, ref, sem).wait()


def shares(rows, ring):
    owners = min(ring, rows // 8)
    return owners, rows // owners


def kernel(sizes, cor_hbm, cnt_hbm, obj_hbm, prb_hbm, pat_hbm, tab_hbm, obj_out, prb_out,
           corners, counts, ext, body, prb, prb2, pat, patp, tab, nb, stage, cor_smem,
           gmid, gsend, grecv, relay, turned, rim, yrecv, gp, p1r, p3r, gpr, p2, p2x,
           loc, farsem, yh, corsem, patsem, gsem, rsem, ysem, csem, asem, agsem, xsem, casem, gprsem, outsem):
    G, PN, S, TR, M = sizes
    grp, pos = lax.axis_index("grp"), lax.axis_index("pos")
    core, chip, chips = lax.rem(pos, 2), pos // 2, PN // 2
    side, lines = lax.rem(chip, 2), chips // 2
    ring = G * lines
    owners, h3 = shares(M, ring)
    me = grp * lines + chip // 2
    late = side != core
    blocks = TR // HALO + 2
    split_ring = ring == owners and G == 2

    def at(g, p):
        return {"device_id": (g, lax.rem(p + PN, PN)), "device_id_type": MESH}

    col_peer = [at(grp, pos - 1), at(grp, pos + 1)]
    row_peer = [at(lax.rem(grp + G - 1, G), pos), at(lax.rem(grp + 1, G), pos)]
    col_send, col_recv = [pos > 0, pos < PN - 1], [pos < PN - 1, pos > 0]
    row_send, row_recv = [grp > 0, grp < G - 1], [grp < G - 1, grp > 0]
    partner = at(grp, pos + 1 - 2 * core)
    across = at(grp, pos + 2 * core - 1)
    has_outer = ((core == 0) & (pos > 0)) | ((core == 1) & (pos < PN - 1))
    has_relay = late & (((core == 1) & (pos + 3 < PN)) | ((core == 0) & (pos >= 3)))
    relay_peer, feeder = at(grp, pos + 6 * core - 3), at(grp, pos + 2 - 4 * core)
    forward_peer = at(grp, pos + 4 * core - 2)

    def ring_at(k):
        return lax.rem(me + k, ring)

    def ring_peer(k):
        q = ring_at(k)
        return at(q // lines, (lax.rem(q, lines) * 2 + side) * 2 + core)

    locals_ = [
        pltpu.make_async_copy(cor_hbm, corners, loc.at[0]),
        pltpu.make_async_copy(obj_hbm, body, loc.at[1]),
        pltpu.make_async_copy(obj_hbm, ext.at[:, pl.ds(HALO, TR), :], loc.at[2]),
        pltpu.make_async_copy(cnt_hbm, counts, loc.at[3]),
        pltpu.make_async_copy(prb_hbm, prb, loc.at[4]),
        pltpu.make_async_copy(tab_hbm, tab, loc.at[5]),
    ]
    for w in range(2):
        columns = pl.ds(w * HALO, HALO)
        locals_.append(pltpu.make_async_copy(pat_hbm.at[:, :, columns], pat.at[w], loc.at[6]))
        for turn in range(2):
            locals_.append(pltpu.make_async_copy(
                prb_hbm.at[:, :, columns], prb2.at[:, w, pl.ds(turn * M, M), :], loc.at[7]))

    locals_[0].start()
    near_ring = [
        (late & row_send[0], row_peer[0]), (late & row_send[1], row_peer[1]),
        (late & (pos >= 4), at(grp, pos - 4)), (late & (pos + 4 < PN), at(grp, pos + 4)),
    ]
    barrier = pltpu.get_barrier_semaphore()

    def greet(condition, peers):
        @pl.when(condition)
        def _():
            for peer in peers:
                pl.semaphore_signal(barrier, inc=1, **peer)
        return condition.astype(jnp.int32) * len(peers)

    expected = greet(col_send[0], [col_peer[0]]) + greet(col_send[1], [col_peer[1]])
    expected += greet(row_send[0], [row_peer[0]]) + greet(row_send[1], [row_peer[1]])
    expected += greet(near_ring[2][0], [near_ring[2][1]]) + greet(near_ring[3][0], [near_ring[3][1]])
    expected += greet(~late & has_outer, [relay_peer, feeder]) + greet(has_relay, [relay_peer, forward_peer])

    for c in locals_[1:3]:
        c.start()
    lane = lax.broadcasted_iota(jnp.int32, (M, HALO), 1)
    gp[...] = jnp.zeros(gp.shape, jnp.float32)

    locals_[0].wait()
    pl.semaphore_wait(barrier, expected)

    def cor_copy(d):
        return pltpu.make_async_remote_copy(corners, cor_smem.at[d], corsem.at[0, d], corsem.at[1, d], **col_peer[d])

    def row_at(d, s):
        return jnp.clip(cor_smem[d, 0, s] - grp * TR + HALO, 0, TR + 2 * HALO - M)

    def halo_copy(d):
        src, dst = ((HALO, HALO + TR), (TR, 0))[d]
        return pltpu.make_async_remote_copy(
            ext.at[:, pl.ds(src, HALO), :], ext.at[:, pl.ds(dst, HALO), :], yh.at[0, d], yh.at[1, d], **row_peer[d])

    for d in range(2):
        @pl.when(col_send[d])
        def _():
            cor_copy(d).start()
    for c in locals_[1:3]:
        c.wait()
    for c in locals_[3:]:
        c.start()
    for d in range(2):
        @pl.when(row_send[d])
        def _():
            halo_copy(d).start()
    for d in range(2):
        @pl.when(col_recv[d])
        def _():
            cor_copy(d).wait_recv()
    first_half = (grp < G - 1).astype(jnp.int32)
    halves = [first_half, 1 - first_half]

    def patch_copy(d, s, h):
        return pltpu.make_async_remote_copy(
            stage.at[d, s, h], nb.at[d, s, h], outsem.at[d], patsem.at[d, s], **col_peer[d])

    def wrapped(source, inset, c, r, h):
        after = r + HALO * (1 - h)
        base = after - lax.rem(after, 2 * HALO) + HALO * h
        last = source.shape[1] - HALO
        low, high = [
            source[c, pl.ds(jnp.clip(at_row - inset * HALO, 0, last), HALO), :]
            for at_row in (base, base + 2 * HALO)
        ]
        rows = lax.broadcasted_iota(jnp.int32, (HALO, HALO), 0) + base
        return jnp.where(rows >= r, low, high)

    def send_patch(s, which):
        h = halves[which]
        for d in range(2):
            @pl.when(col_send[d])
            def _():
                r = row_at(1 - d, s)
                for c in range(2):
                    stage[d, s, h, c] = wrapped((ext, body)[which], which, c, r, h)
                patch_copy(d, s, h).start()

    for s in range(min(2, S)):
        send_patch(s, 1)
    for d in range(2):
        @pl.when(row_recv[d])
        def _():
            halo_copy(d).wait_recv()
    for s in range(S):
        if s >= 2:
            send_patch(s, 1)
        send_patch(s, 0)

    for step in range(lines + G - 3):
        for there, peer in near_ring:
            @pl.when(there)
            def _():
                pl.semaphore_signal(farsem.at[step], inc=1, **peer)
        known = sum(there.astype(jnp.int32) for there, _ in near_ring)

        @pl.when(late)
        def _():
            pl.semaphore_wait(farsem.at[step], known)

    def chip_grad(s, h):
        d = 1 - core
        return pltpu.make_async_remote_copy(
            gsend.at[d, h, s], grecv.at[d, h, s], outsem.at[2 + d], gsem.at[d, 0], **partner)

    def outer_grad(s, h):
        return pltpu.make_async_remote_copy(
            gsend.at[core, h, s], grecv.at[core, h, s], outsem.at[2 + core], gsem.at[core, h], **across)

    def relay_grad(s, h):
        return pltpu.make_async_remote_copy(
            gsend.at[core, h, s], relay.at[h, s], outsem.at[2 + core], rsem.at[h], **relay_peer)

    def forward_grad(s, h):
        return pltpu.make_async_remote_copy(
            relay.at[h, s], grecv.at[1 - core, h, s], outsem.at[4], gsem.at[1 - core, h], **forward_peer)

    for c in locals_[3:6]:
        c.wait()
    drain(pat, loc.at[6])
    drain(prb2, loc.at[7])
    own_count = counts[grp * PN + pos]

    column = lax.broadcasted_iota(jnp.int32, (M, M), 1)
    wanted = jnp.where(column < M // 2, 2 * column, 2 * column - (M - 1))
    pick = (lax.broadcasted_iota(jnp.int32, (M, M), 0) == wanted).astype(jnp.float32).astype(jnp.bfloat16)

    def reorder(s, carry):
        rows = side_by_side(*[
            stack(*[pat[w, s, pl.ds(odd, M // 2, stride=2), :] for odd in range(2)]) for w in range(2)
        ])
        high, low = split(rows)
        last = (rows - high.astype(jnp.float32) - low.astype(jnp.float32)).astype(jnp.bfloat16)
        patp[s] = dot(high, pick) + (dot(low, pick) + dot(last, pick))
        return carry

    lax.fori_loop(0, S, reorder, 0)

    def row_of(s):
        return jnp.clip(corners[0, s] - grp * TR + HALO, 0, TR + 2 * HALO - M)

    def slot(s, carry):
        r = row_of(s)
        shift = jnp.clip(corners[1, s] - pos * HALO + HALO, 0, HALO)
        for d in range(2):
            @pl.when(col_recv[d])
            def _():
                drain(nb.at[d, s], patsem.at[d, s])
        back = lax.rem(HALO - shift, HALO)
        forth = lax.rem(shift, HALO)
        first = lane < HALO - shift
        patch = []
        for c in range(2):
            mid, before, after = [
                pltpu.roll(stack(*pair), back, 1)
                for pair in (
                    [wrapped(ext, 0, c, r, h) for h in range(2)],
                    [nb[1, s, h, c] for h in range(2)],
                    [nb[0, s, h, c] for h in range(2)],
                )
            ]
            patch.append(side_by_side(jnp.where(first, before, mid), jnp.where(first, mid, after)))
        turn = lax.rem(r, M)
        pr, pi = [side_by_side(*[prb2[c, w, pl.ds(M - turn, M), :] for w in range(2)]) for c in range(2)]
        fr, fi = forward(tab, pr * patch[0] - pi * patch[1], pr * patch[1] + pi * patch[0])
        excess = fr * fr + fi * fi - patp[s]
        excess = jnp.where(jnp.full((M, M), s, jnp.int32) < own_count, excess, 0.0)
        cr, ci = backward(tab, excess * fr, excess * fi)
        parts = (pr * cr + pi * ci, pr * ci - pi * cr)
        for c, part in enumerate((patch[0] * cr + patch[1] * ci, patch[0] * ci - patch[1] * cr)):
            for w in range(2):
                turned[c, w, :M] = cols_of(part, w)
                turned[c, w, M:] = cols_of(part, w)
                gp[c, :, w * HALO : (w + 1) * HALO] += turned[c, w, pl.ds(turn, M), :]
        tail = lane >= shift
        for c in range(2):
            g0, g1 = [pltpu.roll(cols_of(parts[c], w), forth, 1) for w in range(2)]
            left, middle, right = jnp.where(tail, g0, 0.0), jnp.where(tail, g1, g0), jnp.where(tail, 0.0, g1)
            for h in range(2):
                gsend[0, h, s, c] = rows_of(left, h)
                gmid[s, h, c] = rows_of(middle, h)
                gsend[1, h, s, c] = rows_of(right, h)
        for h in range(2):
            chip_grad(s, h).start()

        @pl.when(has_outer & late)
        def _():
            outer_grad(s, halves[0]).start()

        @pl.when(has_outer & ~late)
        def _():
            relay_grad(s, halves[0]).start()
        return carry

    lax.fori_loop(0, S, slot, 0)

    core_copy = pltpu.make_async_remote_copy(gp, p1r, csem.at[0], csem.at[1], **partner)

    def share_rows(q):
        return pl.ds(pl.multiple_of(lax.rem(q, owners) * h3, 8), h3)

    pieces = M // HALO

    def chunk(q, owner):
        return q // pieces, share_rows(owner), pl.ds(q % pieces * HALO, HALO)

    def share_copy(q, k):
        return pltpu.make_async_remote_copy(
            gp.at[chunk(q, ring_at(k))], p3r.at[q, k - 1], outsem.at[5], asem.at[q], **ring_peer(k))

    group_rows = pl.ds(pl.multiple_of(grp * lines * h3, 8), lines * h3)

    def group_share():
        other = group_at(1)
        rows = pl.ds(pl.multiple_of(other * lines * h3, 8), lines * h3)
        return pltpu.make_async_remote_copy(gp.at[1, rows, :], gpr, outsem.at[10], gprsem.at[0], **at(other, pos))

    def line_share(q, k):
        return pltpu.make_async_remote_copy(
            gp.at[chunk(q, grp * lines + line_at(k))], p3r.at[q, k - 1], outsem.at[11], asem.at[q], **line_peer(k))

    def pass_share(q, owner, send_sem, recv_sem, peer):
        where = chunk(q, owner)
        return pltpu.make_async_remote_copy(prb_out.at[where], prb_out.at[where], send_sem, recv_sem, **peer)

    line = chip // 2

    def line_at(k):
        return lax.rem(line + k + lines, lines)

    def line_peer(k):
        return at(grp, (line_at(k) * 2 + side) * 2 + core)

    def group_at(j):
        return lax.rem(grp + j + G, G)

    def line_spread(q, k):
        return pass_share(q, me, outsem.at[6], agsem.at[q, 0], line_peer(k))

    def group_spread(q, owner):
        return pass_share(q, owner, outsem.at[7], agsem.at[q, 1], at(group_at(1), pos))

    def spread_copy(q, k, owner):
        return pass_share(q, owner, outsem.at[6], agsem.at[q, 0], ring_peer(k))

    def hand_copy(q, owner):
        return pass_share(q, owner, outsem.at[8], casem.at[0], partner)

    def across_copy(q):
        return pltpu.make_async_remote_copy(p2.at[q], p2x.at[q], outsem.at[9], xsem.at[q], **across)

    chunks = range(2 * pieces)
    direct = chunks[:pieces] if split_ring else chunks

    def source(k):
        return lax.rem(me + ring - k, ring)

    def pass_on(h):
        @pl.when(has_relay)
        def _():
            drain(relay.at[h], rsem.at[h])
            for s in range(S):
                forward_grad(s, h).start()

    def covers(block, r):
        rows = lax.broadcasted_iota(jnp.int32, (HALO, HALO), 0) + (block * HALO - r)
        return (rows >= 0) & (rows < M)

    def own(totals, block, h):
        for s in range(S):
            inside = covers(block, row_of(s))
            totals = [t + jnp.where(inside, gmid[s, h, c], 0.0) for c, t in enumerate(totals)]
        return totals

    def others(totals, block, h, d):
        for s in range(S):
            inside = covers(block, row_at(d, s))
            totals = [t + jnp.where(inside, grecv[d, h, s, c], 0.0) for c, t in enumerate(totals)]
        return totals

    zeros = [jnp.zeros((HALO, HALO), jnp.float32)] * 2

    def near(block, carry):
        h = lax.rem(block, 2)
        totals = others(own(zeros, block, h), block, h, core)
        rows = pl.ds(pl.multiple_of(block * HALO, HALO), HALO)
        for c in range(2):
            obj_out[c, pl.ds(pl.multiple_of(block * HALO - HALO, HALO), HALO), :] = (
                ext[c, rows, :] - STEP_OBJECT * totals[c])
        return carry

    def near_all():
        drain(grecv.at[core], gsem.at[core, 0])
        lax.fori_loop(1, blocks - 1, near, 0)

    def second(first, last):
        @pl.when(has_outer)
        def _():
            for s in range(first, last):
                outer_grad(s, halves[1]).start()

    @pl.when(~late)
    def _():
        core_copy.start()

        @pl.when(has_outer)
        def _():
            for s in range(S):
                relay_grad(s, halves[1]).start()
        near_all()

    @pl.when(late)
    def _():
        core_copy.wait_recv()
        gp[1] += p1r[1]
        if split_ring:
            group_share().start()
        gp[0] += p1r[0]
        for q in direct:
            for k in range(1, ring):
                @pl.when(ring_at(k) < owners)
                def _():
                    share_copy(q, k).start()
        pass_on(halves[0])
        near_all()
        if split_ring:
            drain(gpr, gprsem.at[0])
            gp[1, group_rows, :] += gpr[...]
            for q in chunks[pieces:]:
                for k in range(1, lines):
                    line_share(q, k).start()
        for q in chunks:
            @pl.when(me < owners)
            def _():
                total = gp[chunk(q, me)]
                terms = (ring if q in direct else lines) - 1
                drain(p3r.at[q, pl.ds(0, terms)], asem.at[q])
                for k in range(terms):
                    total = total + p3r[q, k]
                p2[q] = total
                across_copy(q).start()

            if q == pieces - 1:
                second(0, 1)
        second(1, S)

        pass_on(halves[1])
        live = counts[0]
        for i in range(1, G * PN):
            live = live + counts[i]

        @pl.when(me < owners)
        def _():
            for q in chunks:
                across_copy(q).wait_recv()
                total = p2[q] + p2x[q]
                divisor = jnp.full(total.shape, live, jnp.int32).astype(jnp.float32)
                prb_out[chunk(q, me)] = prb[chunk(q, me)] - STEP_PROBE * total / divisor
                if split_ring:
                    for k in range(1, lines):
                        line_spread(q, k).start()
                    group_spread(q, me).start()
                else:
                    for k in range(1, ring):
                        spread_copy(q, k, me).start()
                hand_copy(q, me).start()

    def rim_copy(d):
        return pltpu.make_async_remote_copy(rim.at[d], yrecv.at[d], ysem.at[0, d], ysem.at[1, d], **row_peer[d])

    def finish(h):
        @pl.when(has_outer)
        def _():
            drain(grecv.at[1 - core, h], gsem.at[1 - core, h])
        for d in range(2):
            block = d * (blocks - 1)

            @pl.when(row_send[d] & (h == d))
            def _():
                totals = others(own(zeros, block, d), block, d, core)
                for c in range(2):
                    rim[d, c] = totals[c]

                @pl.when(has_outer)
                def _():
                    more = others([rim[d, c] for c in range(2)], block, d, 1 - core)
                    for c in range(2):
                        rim[d, c] = more[c]
                rim_copy(d).start()

        @pl.when(has_outer)
        def _():
            def far(i, carry):
                block = 2 * i + 2 - h
                totals = others(zeros, block, h, 1 - core)
                rows = pl.ds(pl.multiple_of(block * HALO - HALO, HALO), HALO)
                for c in range(2):
                    obj_out[c, rows, :] = obj_out[c, rows, :] - STEP_OBJECT * totals[c]
                return carry

            lax.fori_loop(0, blocks // 2 - 1, far, 0)

    finish(halves[0])

    @pl.when(late)
    def _():
        if split_ring:
            for q in chunks:
                drain(prb_out.at[0, pl.ds(0, (lines - 1) * h3), pl.ds(0, HALO)], agsem.at[q, 0])
                for k in range(1, lines):
                    owner = grp * lines + line_at(-k)
                    group_spread(q, owner).start()
                    hand_copy(q, owner).start()
        else:
            for q in chunks:
                for k in range(1, ring):
                    @pl.when(source(k) < owners)
                    def _():
                        spread_copy(q, k, source(k)).wait_recv()
                        hand_copy(q, source(k)).start()

    if split_ring:
        @pl.when(late)
        def _():
            for q in chunks:
                drain(prb_out.at[0, pl.ds(0, lines * h3), pl.ds(0, HALO)], agsem.at[q, 1])
                for k in range(lines):
                    hand_copy(q, group_at(1) * lines + line_at(-k)).start()

    finish(halves[1])

    for d in range(2):
        @pl.when(row_recv[d])
        def _():
            rim_copy(d).wait_recv()
            rows = pl.ds((TR - HALO, 0)[d], HALO)
            obj_out[:, rows, :] = obj_out[:, rows, :] - STEP_OBJECT * yrecv[d]

    @pl.when(~late)
    def _():
        drain(prb_out, casem.at[0])

    for d in range(2):
        @pl.when(col_send[d])
        def _():
            cor_copy(d).wait_send()
            drain(stage.at[d], outsem.at[d])

        @pl.when(row_send[d])
        def _():
            halo_copy(d).wait_send()
            rim_copy(d).wait_send()
    drain(gsend.at[1 - core], outsem.at[3 - core])

    @pl.when(has_outer)
    def _():
        drain(gsend.at[core], outsem.at[2 + core])

    @pl.when(has_relay)
    def _():
        drain(relay, outsem.at[4])

    @pl.when(~late)
    def _():
        core_copy.wait_send()

    @pl.when(late)
    def _():
        if split_ring:
            drain(p3r.at[pl.ds(0, pieces)], outsem.at[5])
            drain(gpr, outsem.at[10])
            drain(p3r.at[pl.ds(pieces, pieces), pl.ds(0, lines - 1)], outsem.at[11])
            drain(prb_out.at[:, pl.ds(0, (lines - 1) * h3), :], outsem.at[6])
            drain(prb_out.at[:, pl.ds(0, lines * h3), :], outsem.at[7])
        else:
            for q in chunks:
                for k in range(1, ring):
                    @pl.when(ring_at(k) < owners)
                    def _():
                        share_copy(q, k).wait_send()

                @pl.when(me < owners)
                def _():
                    for k in range(1, ring):
                        spread_copy(q, k, me).wait_send()

        @pl.when(me < owners)
        def _():
            drain(p2, outsem.at[9])
        drain(prb_out, outsem.at[8])


def store(obj, prb, obj_out, prb_out, sems):
    pairs = []
    for whole, out in ((obj, obj_out), (prb, prb_out)):
        rows = whole.shape[1] // PIECES
        pairs += [(whole.at[:, pl.ds(i * rows, rows), :], out.at[:, pl.ds(i * rows, rows), :]) for i in range(PIECES)]
    copies = [pltpu.make_async_copy(*pair, sems.at[i]) for i, pair in enumerate(pairs)]
    for c in copies:
        c.start()
    for c in copies:
        c.wait()


def on_device(grp_size, pos_size, tables, object_field, probe_field, patterns, corners, counts):
    TR, S, M = object_field.shape[1], patterns.shape[0], probe_field.shape[1]
    ring = grp_size * (pos_size // 4)
    owners, h3 = shares(M, ring)
    f32 = jnp.float32
    V, D = pltpu.VMEM, pltpu.SemaphoreType.DMA
    hbm = pl.BlockSpec(memory_space=pl.ANY)
    vmem = pl.BlockSpec(memory_space=pltpu.VMEM)
    half, chunks = (2, HALO, HALO), 2 * (M // HALO)
    object_new, probe_new = pl.pallas_call(
        functools.partial(kernel, (grp_size, pos_size, S, TR, M)),
        out_shape=(
            pltpu.VMEM(object_field.shape, f32),
            pltpu.VMEM(probe_field.shape, f32),
        ),
        in_specs=[hbm] * 6,
        out_specs=(vmem, vmem),
        scratch_shapes=[
            pltpu.SMEM(corners.shape, jnp.int32),
            pltpu.SMEM(counts.shape, jnp.int32),
            V((2, TR + 2 * HALO, HALO), f32),
            V((2, TR, HALO), f32),
            V((2, M, M), f32),
            V((2, 2, 2 * M, HALO), f32),
            V((2, S, M, HALO), f32),
            V((S, M, M), f32),
            V(tables.shape, jnp.bfloat16),
            V((2, S, 2, *half), f32),
            V((2, S, 2, *half), f32),
            pltpu.SMEM((2, *corners.shape), jnp.int32),
            V((S, 2, *half), f32),
            V((2, 2, S, *half), f32),
            V((2, 2, S, *half), f32),
            V((2, S, *half), f32),
            V((2, 2, 2 * M, HALO), f32),
            V((2, *half), f32),
            V((2, *half), f32),
            V((2, M, M), f32),
            V((2, M, M), f32),
            V((chunks, ring - 1, h3, HALO), f32),
            V((M // grp_size, M), f32),
            V((chunks, h3, HALO), f32),
            V((chunks, h3, HALO), f32),
            D((8,)), pltpu.SemaphoreType.REGULAR((max(1, grp_size + pos_size // 4 - 3),)), D((2, 2)), D((2, 2)), D((2, S)),
            D((2, 2)), D((2,)), D((2, 2)), D((2,)), D((chunks,)), D((chunks, 2)), D((chunks,)), D((1,)), D((1,)), D((12,)),
        ],
        compiler_params=pltpu.CompilerParams(
            collective_id=0, has_side_effects=True, vmem_limit_bytes=56 * 1024 * 1024
        ),
    )(corners, counts, object_field, probe_field, patterns, jnp.asarray(tables))
    object_new = pltpu.with_memory_space_constraint(object_new, pltpu.VMEM)
    probe_new = pltpu.with_memory_space_constraint(probe_new, pltpu.VMEM)
    return pl.pallas_call(
        store,
        out_shape=(
            jax.ShapeDtypeStruct(object_field.shape, f32),
            jax.ShapeDtypeStruct(probe_field.shape, f32),
        ),
        in_specs=[hbm, hbm],
        out_specs=(hbm, hbm),
        scratch_shapes=[D((2 * PIECES,))],
        compiler_params=pltpu.CompilerParams(vmem_limit_bytes=1024 * 1024),
    )(object_new, probe_new)

def solution(mesh):
    def body(object_field, probe_field, patterns, corners, counts):
        tables = dft_tables(probe_field.shape[1])
        return on_device(
            mesh.shape["grp"], mesh.shape["pos"], tables, object_field, probe_field, patterns, corners, counts
        )

    return jax.shard_map(
        body,
        mesh=mesh,
        in_specs=(
            P(None, "grp", "pos"),
            P(),
            P(("grp", "pos"), None, None),
            P(None, ("grp", "pos")),
            P(),
        ),
        out_specs=(P(None, "grp", "pos"), P()),
        check_vma=False,
    )
```
